128 devices in a mesh: visit: 4 (over x), patch: 32 (over z, y, core).
Axes of the slice: x: 4, y: 4, z: 4, core: 2. Of those that a mesh axis runs over, the one named last changes fastest.
Arguments:
- image: float32 [4096, 128, 128], P(('visit', 'patch')), may hold values from -6 to 6
- variance: float32 [4096, 128, 128], P(('visit', 'patch')), may hold values from 0.25 to 4
- intersections: int32 [4096, 2], P(('visit', 'patch')), may hold values from 0 to 31, all different within a row; in each aligned block of 32 rows (0 to 31, 32 to 63, ...) at most 3 rows name the same one
- boxes: int32 [4096, 2, 2], P(('visit', 'patch')), may hold values from -64 to 191
- shifts: float32 [4096, 2, 2], P(('visit', 'patch')), may hold values from 0 to 1
- basis_ids: int32 [4096, 3], P(('visit', 'patch')), may hold values from 0 to 7
- coefs: float32 [4096, 3], P(('visit', 'patch')), may hold values from 0.3 to 1.5
- taps: float32 [8, 2, 41], replicated, may hold values from -1 to 1
Outputs:
- coadd: float32 [8192, 256], P('patch')
- coadd_var: float32 [8192, 256], P('patch')
The draws below stay inside these ranges and needn't reach their ends.
Inputs may be any that keep to these rules, and one draw needn't show every extreme that they name: `intersections`: the rows of one device name every patch at most 3 times; each tile names two different patches.
All inputs are finite; a program needn't handle non-finite values.
Results may differ from the reference program's by a relative error of at most 0.0003.
Values sent between devices are 32-bit elements; how exact they have to be, the bound alone decides.
No kernel may reach another device: no remote copies, remote signals or barrier semaphores. Data moves between devices by JAX's collectives and lax.ppermute only.
A program may use at most 128 MiB of HBM per device.

```python
import math
import jax
import jax.numpy as jnp
import numpy as np
from jax import lax

TS = 128
PATCH = 256
TAPS = 41
NB = 3
NBASIS = 8
TILES_DEV = 32
CAP = 3
PATCHES = 32
TILES = 4096


def touch_ends(drawn, own_key, least, largest):
    spot = [jax.random.randint(jax.random.fold_in(own_key, axis), (), 0, length) for axis, length in enumerate(drawn.shape)]
    widest = drawn.shape.index(max(drawn.shape))
    neighbour = spot[:widest] + [(spot[widest] + 1) % drawn.shape[widest]] + spot[widest + 1:]
    return drawn.at[tuple(spot)].set(least).at[tuple(neighbour)].set(largest)


def block_levels(stream_key, dims, pieces, least, largest):
    gain = 1.0
    for position, shards_of in pieces:
        draws = jax.random.uniform(jax.random.fold_in(jax.random.fold_in(stream_key, 6), position), (shards_of,), jnp.float32, least / len(pieces), largest / len(pieces))
        gain = gain * jnp.repeat(jnp.exp(draws), dims[position] // shards_of).reshape((-1,) + (1,) * (len(dims) - 1 - position))
    return gain


def deal_out(key, own, number, rows, amount, top, most, lean):
    order = jax.random.permutation(key, amount)
    heavy_load, usual = shares(amount, rows * top, most, lean, True), shares(amount, rows * top, most, lean, False)
    places = jnp.arange(amount)

    def named(sizes, rotation):
        used = int((sizes > 0).sum())
        fixed = max(1, used // 4)
        passed = fixed + (places - fixed + rotation * (used - fixed)) % max(1, amount - fixed)
        return jnp.zeros((amount,), jnp.int32).at[order[jnp.where(places < fixed, places, passed)]].set(jnp.asarray(sizes, jnp.int32))

    sizes = jnp.where(number % 4 == 0, named(heavy_load, number // 4), named(usual, number - number // 4 - 1))
    mixed = jax.random.permutation(jax.random.fold_in(own, 3), amount)
    donor, taker = mixed[0:amount // 2 * 2:2], mixed[1:amount // 2 * 2:2]
    slack = jnp.minimum(sizes[donor] - 1, most - sizes[taker]) // 2
    slack = jnp.where((donor == order[0]) | (taker == order[0]) | (sizes[taker] == 0), 0, jnp.maximum(slack, 0))
    passed = jax.random.randint(jax.random.fold_in(own, 4), (amount // 2,), 0, 1 << 20) % (slack + 1)
    sizes = sizes.at[donor].add(-passed).at[taker].add(passed)
    labels = jnp.searchsorted(jnp.cumsum(sizes), jnp.arange(rows * top), side="right").astype(jnp.int32)
    table = labels.reshape(top, rows).T
    table = table[jax.random.permutation(jax.random.fold_in(own, 1), rows)]
    rotation = jax.random.randint(jax.random.fold_in(own, 2), (rows, 1), 0, top)
    return jnp.take_along_axis(table, (jnp.arange(top)[None, :] + rotation) % top, axis=1)


def shares(count, total, most, slope, full):
    portions = [(1 << 20) // math.isqrt(standing ** slope) + 1 for standing in range(1, count + 1)]
    largest = most if full else min(most, max(-(-total // count), total * portions[0] // sum(portions)))
    least = 1 if total - largest >= count - 1 else 0
    counts, surplus = [largest] + [least] * (count - 1), total - largest - least * (count - 1)
    while surplus > 0:
        movable = [i for i in range(1, count) if counts[i] < largest] or [i for i in range(1, count) if counts[i] < most]
        whole, remaining = sum([portions[i] for i in movable]), surplus
        for i in movable:
            extra = min(most - counts[i], max(1, remaining * portions[i] // whole), surplus)
            counts[i] = counts[i] + extra
            surplus = surplus - extra
    return np.array(counts)


def gaussian(stream_key, extent, scale, reach, cuts=(), kind=jnp.bfloat16):
    array = jax.random.normal(stream_key, extent, jnp.float32) * scale
    if len(cuts) > 0:
        array = block_levels(stream_key, extent, cuts, -0.22, 0.18) * array
    return jnp.clip(array, min=-reach, max=reach).astype(kind)


def setup_inputs(seed: int = 0) -> dict:
    seeds = jax.random.split(jax.random.key(seed), 9)
    image = gaussian(seeds[0], (TILES, TS, TS), 1.0, 6.0, ((0, 128),), jnp.float32)
    variance = jnp.clip(jnp.exp(math.log(4.0) - 2.7725887 * jax.random.uniform(seeds[1], (TILES, TS, TS), jnp.float32) ** block_levels(seeds[1], (TILES, TS, TS), ((0, 128),), -0.2, 0.2)), 0.25, 4.0)
    intersections_keys = jax.random.split(jax.random.fold_in(seeds[2], 1), TILES // TILES_DEV)
    intersections_turns = jax.random.permutation(jax.random.fold_in(seeds[2], 3), TILES // TILES_DEV)
    intersections = jax.vmap(lambda own, number: deal_out(jax.random.fold_in(seeds[2], 2), own, number, TILES_DEV, PATCHES, 2, CAP, 2))(intersections_keys, intersections_turns).reshape((TILES, 2))
    boxes = touch_ends(jax.random.randint(seeds[3], (TILES, 2, 2), 0 - TS // 2, PATCH - TS // 2), jax.random.fold_in(seeds[3], 1), 0 - TS // 2, (PATCH - TS // 2) - 1).astype(jnp.int32)
    shifts = jnp.clip(1.0 * jax.random.uniform(seeds[4], (TILES, 2, 2), jnp.float32) ** block_levels(seeds[4], (TILES, 2, 2), ((0, 128),), -0.2, 0.2), 0.0, 1.0)
    basis_ids = touch_ends(jax.random.randint(seeds[5], (TILES, NB), 0, NBASIS), jax.random.fold_in(seeds[5], 1), 0, NBASIS - 1).astype(jnp.int32)
    coefs = jnp.clip(0.3 + 1.2 * jax.random.uniform(seeds[6], (TILES, NB), jnp.float32) ** block_levels(seeds[6], (TILES, NB), ((0, 128),), -0.2, 0.2), 0.3, 1.5)
    taps = gaussian(seeds[7], (NBASIS, 2, TAPS), TAPS ** -0.5, 1.0, (), jnp.float32)
    return {"image": image, "variance": variance, "intersections": intersections, "boxes": boxes, "shifts": shifts, "basis_ids": basis_ids, "coefs": coefs, "taps": taps}


HI = lax.Precision.HIGHEST


def band_table(side, ntaps):
    offs = jnp.arange(side)[:, None] - jnp.arange(side)[None, :] + (ntaps - 1) // 2
    return (offs[:, :, None] == jnp.arange(ntaps)[None, None, :]).astype(jnp.float32)


def convolve(images, row_taps, col_taps, weights_b):
    band = band_table(images.shape[-1], row_taps.shape[-1])
    row_mats = jnp.einsum('ikt,gbt->gbik', band, row_taps, precision=HI)
    col_mats = jnp.einsum('jlt,gbt->gbjl', band, col_taps, precision=HI)
    partial_rows = jnp.einsum('gbik,gkl->gbil', row_mats, images, precision=HI)
    scaled = partial_rows * weights_b[:, :, None, None]
    return jnp.einsum('gbil,gbjl->gij', scaled, col_mats, precision=HI)


def interpolation(offset, shift, count, side):
    place = (jnp.arange(count).astype(jnp.float32)[None, :, None] - offset[:, None, None]
             - shift[:, None, None] - jnp.arange(side).astype(jnp.float32)[None, None, :])
    return jnp.maximum(0.0, 1.0 - jnp.abs(place))


def warp_group(planes, meta, patch_side):
    side = planes.shape[-1]
    rows_w = interpolation(meta[:, 1], meta[:, 3], patch_side, side)
    cols_w = interpolation(meta[:, 2], meta[:, 4], patch_side, side)
    left = jnp.einsum('gpi,gcij->gcpj', rows_w, planes, precision=HI)
    both = jnp.einsum('gcpj,gqj->gcpq', left, cols_w, precision=HI)
    weight = meta[:, 0]
    num = jnp.sum(weight[:, None, None] * both[:, 0], 0)
    vsum = jnp.sum((weight * weight)[:, None, None] * both[:, 1], 0)
    cover = jnp.sum(rows_w, 2)[:, :, None] * jnp.sum(cols_w, 2)[:, None, :]
    den = jnp.sum(weight[:, None, None] * cover, 0)
    return jnp.stack([num, den, vsum], 0)


def finish(num, den, vsum):
    safe = jnp.maximum(den, 1.0)
    return num / safe, vsum / (safe * safe)


def reference(image, variance, intersections, boxes, shifts, basis_ids, coefs, taps):
    maps = jnp.zeros((PATCHES, 3, PATCH, PATCH), jnp.float32)
    nbasis = taps.shape[0]

    def step(maps, parts):
        img, var, dest, box, shift, ids, coef = parts
        select = (ids[:, None] == jnp.arange(nbasis)[None, :]).astype(jnp.float32)
        row_t = jnp.dot(select, taps[:, 0], precision=HI)
        col_t = jnp.dot(select, taps[:, 1], precision=HI)
        conv = convolve(img[None], row_t[None], col_t[None], coef[None])[0]
        weight = 1.0 / jnp.mean(var)
        planes = jnp.stack([conv, var], 0)[None]
        boxf = box.astype(jnp.float32)
        for route in range(2):
            meta = jnp.stack([weight, boxf[route, 0], boxf[route, 1], shift[route, 0], shift[route, 1]])[None]
            contrib = warp_group(planes, meta, PATCH)
            maps = maps.at[dest[route]].add(contrib)
        return maps, None

    maps = lax.scan(step, maps, (image, variance, intersections, boxes, shifts, basis_ids, coefs))[0]
    coadd, coadd_var = finish(maps[:, 0], maps[:, 1], maps[:, 2])
    return coadd.reshape(PATCHES * PATCH, PATCH), coadd_var.reshape(PATCHES * PATCH, PATCH)
```

```python
import functools

import jax
import jax.numpy as jnp
from jax import lax
from jax.experimental import pallas as pl
from jax.experimental.pallas import tpu as pltpu
from jax.sharding import PartitionSpec as P

TS = 128
PATCH = 256
NB = 3
NBASIS = 8
HALF = 20
TILES = 32
ROUTES = 2 * TILES
CAP = 3
META = 24
PAD = 64
SLOTS = 256
F32 = jnp.float32
BF16 = jnp.bfloat16

BOX, SHIFT, IDS, COEF = ROUTES, 3 * ROUTES, 5 * ROUTES, 5 * ROUTES + NB * TILES


def split(x):
    high = x.astype(BF16)
    return high, (x - high.astype(F32)).astype(BF16)


def match_kernel(table, rows, cols, image, variance, out, row_mats, col_mats):
    i = lax.broadcasted_iota(jnp.int32, (TS, TS), 0)
    k = lax.broadcasted_iota(jnp.int32, (TS, TS), 1)
    near = jnp.abs(i - k) <= HALF
    for b in range(NBASIS):
        for source, target, axis in ((rows, row_mats, 0), (cols, col_mats, 1)):
            line = jnp.broadcast_to(source[b : b + 1, :], (TS, TS))
            band = jnp.where(near, pltpu.roll(line, 0, 1, stride=1, stride_axis=0), 0.0)
            target[b] = jnp.concatenate(split(band), axis)

    @pl.loop(0, TILES)
    def _(t):
        weight = float(TS * TS) / jnp.sum(variance[t], axis=(0, 1), keepdims=True)
        pixels = jnp.concatenate(split(image[t]), 1)
        total = None
        for j in range(NB):
            basis = table[IDS + NB * t + j].astype(jnp.int32)
            p = jnp.dot(row_mats[basis], pixels, preferred_element_type=F32)
            part = p[:TS, :TS] + (p[TS:, :TS] + p[:TS, TS:])
            part = jnp.concatenate(split(part * table[COEF + NB * t + j]), 0)
            p = jnp.dot(part, col_mats[basis], preferred_element_type=F32)
            p = p[:TS, :TS] + (p[TS:, :TS] + p[:TS, TS:])
            total = p if total is None else total + p
        out[t] = total * weight


def match(table, rows, cols, image, variance):
    vmem = pl.BlockSpec(memory_space=pltpu.VMEM)
    return pl.pallas_call(
        match_kernel,
        out_shape=jax.ShapeDtypeStruct((TILES, TS, TS), F32),
        in_specs=[pl.BlockSpec(memory_space=pltpu.SMEM)] + [vmem] * 4,
        out_specs=vmem,
        scratch_shapes=[pltpu.VMEM((NBASIS, 2 * TS, TS), BF16), pltpu.VMEM((NBASIS, TS, 2 * TS), BF16)],
        compiler_params=pltpu.CompilerParams(vmem_limit_bytes=40 << 20),
        cost_estimate=pl.CostEstimate(flops=8_000_000_000, bytes_accessed=6 << 20, transcendentals=0),
        name="match",
    )(table, rows, cols, image, variance)


def place(tile, row, col, frac_row, frac_col, scale, stage, acc):
    lane = lax.broadcasted_iota(jnp.int32, (1, TS), 1)
    turn = (col + TS) & (TS - 1)
    first = (col + TS) >> 7
    near, far = (1.0 - frac_col) * scale, frac_col * scale
    here = jnp.where(lane >= turn, near, 0.0)
    here_next = jnp.where(lane >= turn + 1, far, 0.0)
    over, over_next = near - here, far - here_next
    r0 = pltpu.roll(tile, turn, 1)
    r1 = pltpu.roll(r0, 1, 1)
    stage[0, 8 : 8 + TS, :] = r0 * here + r1 * here_next
    stage[1, 8 : 8 + TS, :] = r0 * over + r1 * over_next
    down = (row + PAD) & 7
    base = pl.multiple_of(((row + PAD) >> 3) * 8, 8)
    for side in range(2):
        upper = stage[side, pl.ds(8 - down, TS + 8), :]
        lower = stage[side, pl.ds(7 - down, TS + 8), :]
        acc[first + side, pl.ds(base, TS + 8), :] += upper * (1.0 - frac_row) + lower * frac_row


def geometry(table, item):
    return (
        table[BOX + 2 * item].astype(jnp.int32),
        table[BOX + 2 * item + 1].astype(jnp.int32),
        table[SHIFT + 2 * item],
        table[SHIFT + 2 * item + 1],
    )


def warp_kernel(with_meta, *refs):
    if with_meta:
        where_ref, own, other, own_tiles, other_tiles = refs[:5]
        left_keep, left_send, right_keep, right_send, slots = refs[5:10]
        stage, acc, weights, counts = refs[10:]
    else:
        slots, own, other, own_tiles, other_tiles = refs[:5]
        left_keep, left_send, right_keep, right_send = refs[5:9]
        stage, acc = refs[9:]
    lane = lax.broadcasted_iota(jnp.int32, (1, TS), 1)
    stage[:, 0:8, :] = jnp.zeros((2, 8, TS), F32)
    stage[:, 8 + TS :, :] = jnp.zeros((2, 8, TS), F32)

    if with_meta:
        mine, core, chip = where_ref[0], where_ref[1], where_ref[2]
        for side, table in ((0, own), (1, other)):
            for k in range(17):
                counts[k] = 0

            @pl.loop(0, ROUTES)
            def _(item, side=side, table=table):
                dest = table[item].astype(jnp.int32)
                z, y = dest >> 3, (dest >> 1) & 3
                z, y = z ^ (z >> 1), y ^ (y >> 1)
                code = ((z & 1) << 3) | ((z >> 1) << 2) | ((y & 1) << 1) | (y >> 1)
                k = jnp.where((dest & 1) == core, code ^ mine, 16)
                seen = counts[k]
                slots[SLOTS // 2 * side + 16 + k * CAP + seen] = item
                counts[k] = seen + 1

            for k in range(16):
                slots[SLOTS // 2 * side + k] = counts[k]

        for side, tiles in ((0, own_tiles), (1, other_tiles)):

            @pl.loop(0, TILES, step=8)
            def _(t, side=side, tiles=tiles):
                sums = jnp.concatenate([jnp.sum(tiles[t + u], axis=0, keepdims=True) for u in range(8)], 0)
                sums = jnp.sum(sums, axis=1, keepdims=True)
                at = pl.multiple_of(side * TILES + t, 8)
                weights[pl.ds(at, 8), :] = jnp.broadcast_to(float(TS * TS) / sums, (8, TS))

    @pl.loop(0, 16)
    def _(k):
        for side in (1, 2):
            acc[side, PAD : PAD + PATCH, :] = jnp.zeros((PATCH, TS), F32)
        if with_meta:
            acc[0, 384 : 384 + META, :] = jnp.zeros((META, TS), F32)
        for side, table, tiles in ((0, own, own_tiles), (1, other, other_tiles)):

            @pl.loop(0, slots[SLOTS // 2 * side + k])
            def _(n, side=side, table=table, tiles=tiles):
                item = slots[SLOTS // 2 * side + 16 + k * CAP + n]
                row, col, frac_row, frac_col = geometry(table, item)
                t = item >> 1
                if with_meta:
                    weight = weights[pl.ds(side * TILES + t, 1), :]
                    scale = weight * weight
                    field = lax.broadcasted_iota(jnp.int32, (8, TS), 0)
                    value = jnp.where(field == 1, row.astype(F32), weight)
                    value = jnp.where(field == 2, col.astype(F32), value)
                    value = jnp.where(field == 3, frac_row, value)
                    value = jnp.where(field == 4, frac_col, value)
                    value = jnp.where((field < 5) & (lane == 2 * chip + side), value, 0.0)
                    acc[0, pl.ds(pl.multiple_of(384 + 8 * n, 8), 8), :] += value
                else:
                    scale = 1.0
                place(tiles[t], row, col, frac_row, frac_col, scale, stage, acc)

        z_first, z_second, y_first, y_second = k >> 3, (k >> 2) & 1, (k >> 1) & 1, k & 1
        if not with_meta:
            z_first, z_second, y_first, y_second = z_second, z_first, y_second, y_first
        left = z_second * 4 + y_first * 2 + y_second
        right = y_second * 4 + z_first * 2 + z_second

        for gate, keep, send, index, side in (
            (z_first, left_keep, left_send, left, 1),
            (y_first, right_keep, right_send, right, 2),
        ):
            for value, target in ((0, keep), (1, send)):

                @pl.when(gate == value)
                def _(target=target, index=index, side=side):
                    target[index, 0:PATCH, :] = acc[side, PAD : PAD + PATCH, :]
                    if with_meta and side == 1:
                        target[index, PATCH : PATCH + META, :] = acc[0, 384 : 384 + META, :]


def warp(with_meta, first, own, other, own_tiles, other_tiles):
    smem, vmem = pl.BlockSpec(memory_space=pltpu.SMEM), pl.BlockSpec(memory_space=pltpu.VMEM)
    rows = PATCH + META if with_meta else PATCH
    left = jax.ShapeDtypeStruct((8, rows, TS), F32)
    right = jax.ShapeDtypeStruct((8, PATCH, TS), F32)
    outs, specs = [left, left, right, right], [vmem] * 4
    scratch = [pltpu.VMEM((2, TS + 16, TS), F32), pltpu.VMEM((4, 384 + META, TS), F32)]
    if with_meta:
        outs, specs = outs + [jax.ShapeDtypeStruct((SLOTS,), jnp.int32)], specs + [smem]
        scratch += [pltpu.VMEM((2 * TILES, TS), F32), pltpu.SMEM((17,), jnp.int32)]
    return pl.pallas_call(
        functools.partial(warp_kernel, with_meta),
        out_shape=outs,
        in_specs=[smem] * 3 + [vmem] * 2,
        out_specs=specs,
        scratch_shapes=scratch,
        compiler_params=pltpu.CompilerParams(vmem_limit_bytes=40 << 20),
        cost_estimate=pl.CostEstimate(flops=8_000_000_000, bytes_accessed=8 << 20, transcendentals=0),
        name="warp_meta" if with_meta else "warp",
    )(first, own, other, own_tiles, other_tiles)


def finish_kernel(num_left, num_right, var_left, var_right, coadd, coadd_var):
    place_of = lax.broadcasted_iota(jnp.int32, (PATCH, TS), 0).astype(F32)

    def cover(offset, shift):
        u = place_of - offset
        lower = jnp.where((u >= 0.0) & (u <= TS - 1.0), 1.0 - shift, 0.0)
        return lower + jnp.where((u >= 1.0) & (u <= float(TS)), shift, 0.0)

    den = jnp.zeros((PATCH, PATCH), F32)
    for slot in range(CAP):
        at = PATCH + 8 * slot
        weight, row, col, frac_row, frac_col = (var_left[at + f : at + f + 1, :] for f in range(5))
        down, across = cover(row, frac_row) * weight, cover(col, frac_col)
        den += lax.dot_general(
            down, across, (((1,), (1,)), ((), ())), precision=lax.Precision.HIGHEST, preferred_element_type=F32
        )
    safe = jnp.maximum(den, 1.0)
    for num, var, lo in ((num_left, var_left, 0), (num_right, var_right, TS)):
        part = safe[:, lo : lo + TS]
        coadd[:, lo : lo + TS] = num[0:PATCH, :] / part
        coadd_var[:, lo : lo + TS] = var[0:PATCH, :] / (part * part)


def finish(num_left, num_right, var_left, var_right):
    vmem = pl.BlockSpec(memory_space=pltpu.VMEM)
    return pl.pallas_call(
        finish_kernel,
        out_shape=[jax.ShapeDtypeStruct((PATCH, PATCH), F32)] * 2,
        in_specs=[vmem] * 4,
        out_specs=[vmem] * 2,
        name="finish",
    )(num_left, num_right, var_left, var_right)


EDGES = (((0, 1), (1, 0), (2, 3), (3, 2)), ((1, 2), (2, 1), (3, 0), (0, 3)))


def over_patch(axis, edge):
    pairs = []
    for a, b in EDGES[edge]:
        for other in range(4):
            for core in range(2):
                src, dst = ((a, other), (b, other)) if axis == "z" else ((other, a), (other, b))
                pairs.append((src[0] * 8 + src[1] * 2 + core, dst[0] * 8 + dst[1] * 2 + core))
    return pairs


def halve(keep, send, order):
    for step, (axis, edge) in enumerate(order):
        got = lax.ppermute(send, "patch", over_patch(axis, edge))
        n = keep.shape[0] // 2
        if step == len(order) - 1:
            return keep[0] + got[0]
        send, keep = keep[n:] + got[n:], keep[:n] + got[:n]


def double(x, first):
    for edge in (first, 1 - first):
        x = x + lax.ppermute(x, "visit", EDGES[edge])
    return x


def shards(image, variance, intersections, boxes, shifts, basis_ids, coefs, taps):
    swap = [(i, i ^ 1) for i in range(32)]
    other_variance = lax.ppermute(variance, "patch", swap)
    table = jnp.concatenate(
        [
            intersections.reshape(-1).astype(F32),
            boxes.reshape(-1).astype(F32),
            shifts.reshape(-1),
            basis_ids.reshape(-1).astype(F32),
            coefs.reshape(-1),
        ]
    )
    other_table = lax.ppermute(table, "patch", swap)
    flat = taps[:, :, ::-1]
    gap = jnp.zeros((NBASIS, TS - 2 * HALF - 1), F32)
    rows = jnp.concatenate([flat[:, 0, HALF:], gap, flat[:, 0, :HALF]], 1)
    cols = jnp.concatenate([taps[:, 1, HALF:], gap, taps[:, 1, :HALF]], 1)
    matched = match(table, rows, cols, image, variance)
    other_matched = lax.ppermute(matched, "patch", swap)

    patch = lax.axis_index("patch")
    z, y = patch >> 3, (patch >> 1) & 3
    chip = lax.axis_index("visit") * 16 + z * 4 + y
    z, y = z ^ (z >> 1), y ^ (y >> 1)
    mine = ((z & 1) << 3) | ((z >> 1) << 2) | ((y & 1) << 1) | (y >> 1)
    where = jnp.stack([mine, patch & 1, chip])

    var_left_keep, var_left_send, var_right_keep, var_right_send, slots = warp(
        True, where, table, other_table, variance, other_variance
    )
    num_left_keep, num_left_send, num_right_keep, num_right_send = warp(
        False, slots, table, other_table, matched, other_matched
    )
    z1, z2, y1, y2 = ("z", 0), ("z", 1), ("y", 0), ("y", 1)
    var_left = double(halve(var_left_keep, var_left_send, (z1, z2, y1, y2)), 0)
    var_right = double(halve(var_right_keep, var_right_send, (y1, y2, z1, z2)), 1)
    num_left = double(halve(num_left_keep, num_left_send, (z2, z1, y2, y1)), 0)
    num_right = double(halve(num_right_keep, num_right_send, (y2, y1, z2, z1)), 1)
    return tuple(finish(num_left, num_right, var_left, var_right))


def solution(mesh):
    split_spec = ("visit", "patch")
    in_specs = (
        P(split_spec, None, None),
        P(split_spec, None, None),
        P(split_spec, None),
        P(split_spec, None, None),
        P(split_spec, None, None),
        P(split_spec, None),
        P(split_spec, None),
        P(),
    )
    out_specs = (P("patch", None), P("patch", None))
    return jax.shard_map(shards, mesh=mesh, in_specs=in_specs, out_specs=out_specs, check_vma=False)
```

```python
import functools

import jax
import jax.numpy as jnp
from jax import lax
from jax.experimental import pallas as pl
from jax.experimental.pallas import tpu as pltpu
from jax.sharding import PartitionSpec as P

TS = 128
PATCH = 256
NB = 3
NBASIS = 8
HALF = 20
TILES = 32
ROUTES = 2 * TILES
CAP = 3
META = 24
PAD = 64
SLOTS = 256
F32 = jnp.float32
BF16 = jnp.bfloat16

IDS, COEF = 10, 13
EMPTY = 1 << 24
UNROLL = 4
MATCH_UNROLL = 4
MATCH_COST = WARP_COST = 10_000_000_000


def split(x):
    high = x.astype(BF16)
    return high, (x - high.astype(F32)).astype(BF16)


def pack_kernel(mine, intersections, boxes, shifts, basis_ids, coefs, out):
    out[...] = jnp.zeros_like(out)
    z, y, core = intersections[...] >> 3, (intersections[...] >> 1) & 3, intersections[...] & 1
    z, y = z ^ (z >> 1), y ^ (y >> 1)
    code = ((z & 1) << 3) | ((z >> 1) << 2) | ((y & 1) << 1) | (y >> 1)
    out[0:2, 0:TILES] = ((code ^ mine[0]) + 16 * core).astype(F32)
    for route in range(2):
        out[2 + 2 * route : 4 + 2 * route, 0:TILES] = boxes[route].astype(F32)
        out[6 + 2 * route : 8 + 2 * route, 0:TILES] = shifts[route]
    out[IDS : IDS + NB, 0:TILES] = basis_ids[...].astype(F32)
    out[COEF : COEF + NB, 0:TILES] = coefs[...]


def pack(mine, intersections, boxes, shifts, basis_ids, coefs):
    vmem = pl.BlockSpec(memory_space=pltpu.VMEM)
    return pl.pallas_call(
        pack_kernel,
        out_shape=jax.ShapeDtypeStruct((16, TS), F32),
        in_specs=[pl.BlockSpec(memory_space=pltpu.SMEM)] + [vmem] * 5,
        out_specs=vmem,
        name="pack",
    )(mine, intersections.T, boxes.transpose(1, 2, 0), shifts.transpose(1, 2, 0), basis_ids.T, coefs.T)


def match_kernel(table, taps, image, variance, out, line, row_mats, col_mats):
    i = lax.broadcasted_iota(jnp.int32, (TS, TS), 0)
    k = lax.broadcasted_iota(jnp.int32, (TS, TS), 1)
    near = jnp.abs(i - k) <= HALF
    line[...] = jnp.zeros_like(line)
    for b in range(NBASIS):
        line[2 * b : 2 * b + 2, 0 : 2 * HALF + 1] = taps[b]
    line[...] = pltpu.roll(line[...], TS - HALF, 1)
    for b in range(NBASIS):
        for side, target, axis in ((0, row_mats, 0), (1, col_mats, 1)):
            band = jnp.broadcast_to(line[2 * b + side : 2 * b + side + 1, :], (TS, TS))
            band = pltpu.roll(band, 0, 1, stride=1, stride_axis=0)
            band = jnp.where(near, band, 0.0)
            target[b] = jnp.concatenate(split(band.T if side == 0 else band), axis)

    def total(p):
        return p[:TS, :TS] + (p[TS:, :TS] + p[:TS, TS:])

    @pl.loop(0, TILES, step=MATCH_UNROLL)
    def _(first):
        for t in [first + u for u in range(MATCH_UNROLL)]:
            weight = float(TS * TS) / jnp.sum(variance[t], axis=(0, 1), keepdims=True)
            pixels = jnp.concatenate(split(image[t]), 1)
            parts, bands = [], []
            for j in range(NB):
                basis = table[IDS + j, t].astype(jnp.int32)
                p = total(jnp.dot(row_mats[basis], pixels, preferred_element_type=F32))
                parts.append(jnp.concatenate(split(p * table[COEF + j, t]), 0))
                bands.append(col_mats[basis])
            p = jnp.dot(jnp.concatenate(parts[:2], 1), jnp.concatenate(bands[:2], 0), preferred_element_type=F32)
            p = p + jnp.dot(parts[2], bands[2], preferred_element_type=F32)
            out[t] = total(p) * weight


def match(table, taps, image, variance):
    vmem = pl.BlockSpec(memory_space=pltpu.VMEM)
    return pl.pallas_call(
        match_kernel,
        out_shape=jax.ShapeDtypeStruct((TILES, TS, TS), F32),
        in_specs=[pl.BlockSpec(memory_space=pltpu.SMEM)] + [vmem] * 3,
        out_specs=vmem,
        scratch_shapes=[
            pltpu.VMEM((2 * NBASIS, TS), F32),
            pltpu.VMEM((NBASIS, 2 * TS, TS), BF16),
            pltpu.VMEM((NBASIS, TS, 2 * TS), BF16),
        ],
        compiler_params=pltpu.CompilerParams(vmem_limit_bytes=40 << 20),
        cost_estimate=pl.CostEstimate(flops=MATCH_COST, bytes_accessed=6 << 20, transcendentals=0),
        name="match",
    )(table, taps, image, variance)


def warp_kernel(with_meta, *refs):
    first, own, other, own_tiles, other_tiles = refs[:5]
    outs = refs[5:9]
    if with_meta:
        slots = refs[9]
        stage, acc, tiles, sems, both, meta, weights, counts = refs[10:]
    else:
        slots = first
        stage, acc, tiles, sems = refs[9:]
    copies = [
        pltpu.make_async_copy(source, tiles.at[pl.ds(TILES * i, TILES)], sems.at[i])
        for i, source in enumerate((own_tiles, other_tiles))
    ]
    for copy in copies:
        copy.start()
    lane = lax.broadcasted_iota(jnp.int32, (8, TS), 1)
    stage[:, :, 0:8, :] = jnp.zeros((UNROLL, 2, 8, TS), F32)
    stage[:, :, 8 + TS :, :] = jnp.zeros((UNROLL, 2, 8, TS), F32)
    for k in range(16):
        for side in (1, 2):
            acc[4 * k + side, PAD : PAD + PATCH, :] = jnp.zeros((PATCH, TS), F32)

    if with_meta:
        core, chip = first[1], first[2]
        meta[...] = jnp.zeros_like(meta)
        for side in range(2):
            for k in range(17):
                counts[side, k] = 0

        for route in range(2):

            @pl.loop(0, TILES)
            def _(t, route=route):
                for side, table in ((0, own), (1, other)):
                    k = table[route, t].astype(jnp.int32) - 16 * core
                    k = jnp.where((k >= 0) & (k < 16), k, 16)
                    seen = counts[side, k]
                    both[side, k * CAP + seen] = 2 * t + route
                    counts[side, k] = seen + 1

        n = jnp.int32(0)
        for k in range(16):
            for side in range(2):

                def add(m, n, side=side, k=k):
                    slots[1 + n] = both[side, k * CAP + m] + ((k << 16) + (side << 8)) + (m << 12)
                    return n + 1

                n = lax.fori_loop(0, counts[side, k], add, n)
        slots[0] = n
        for u in range(UNROLL):
            slots[1 + n + u] = EMPTY

    for copy in copies:
        copy.wait()

    if with_meta:

        @pl.loop(0, 2 * TILES, step=8)
        def _(t):
            sums = jnp.concatenate([jnp.sum(tiles[t + u], axis=0, keepdims=True) for u in range(8)], 0)
            sums = jnp.sum(sums, axis=1, keepdims=True)
            weights[pl.ds(pl.multiple_of(t, 8), 8), :] = jnp.broadcast_to(float(TS * TS) / sums, (8, TS))

    def place(entry, u):
        item, side, slot, k = entry & 255, (entry >> 8) & 1, (entry >> 12) & 3, (entry >> 16) & 15
        t, route = item >> 1, item & 1

        def scalar(row):
            return jnp.where(side == 0, own[row + 2 * route, t], other[row + 2 * route, t])

        row, col = scalar(2).astype(jnp.int32), scalar(3).astype(jnp.int32)
        frac_row, frac_col = scalar(6), scalar(7)
        real = jnp.where(entry >= EMPTY, 0.0, 1.0)
        at = side * TILES + t
        near, far = jnp.full((8, TS), (1.0 - frac_col) * real), jnp.full((8, TS), frac_col * real)
        if with_meta:
            weight = jnp.broadcast_to(weights[pl.ds(at, 1), :], (8, TS))
            field = lax.broadcasted_iota(jnp.int32, (8, TS), 0)
            value = jnp.where(field == 1, row.astype(F32), weight)
            value = jnp.where(field == 2, col.astype(F32), value)
            value = jnp.where(field == 3, frac_row, value)
            value = jnp.where(field == 4, frac_col, value)
            value = jnp.where((field < 5) & (lane == 2 * chip + side), value * real, 0.0)
            meta[k * CAP + slot] += value
            near, far = near * (weight * weight), far * (weight * weight)
        turn = (col + TS) & (TS - 1)
        here = jnp.where(lane >= turn, near, 0.0)
        here_next = jnp.where(lane >= turn + 1, far, 0.0)
        over, over_next = near - here, far - here_next
        tile = tiles[at]
        r0 = pltpu.roll(tile, turn, 1).reshape(TS // 8, 8, TS)
        r1 = pltpu.roll(tile, (turn + 1) & (TS - 1), 1).reshape(TS // 8, 8, TS)
        stage[u, 0, 8 : 8 + TS, :] = (r0 * here + r1 * here_next).reshape(TS, TS)
        stage[u, 1, 8 : 8 + TS, :] = (r0 * over + r1 * over_next).reshape(TS, TS)
        return 4 * k + ((col + TS) >> 7), row + PAD, frac_row

    def add_rows(u, first, row, frac_row):
        down = row & 7
        base = pl.multiple_of((row >> 3) * 8, 8)
        for side in range(2):
            upper = stage[u, side, pl.ds(8 - down, TS + 8), :]
            lower = stage[u, side, pl.ds(7 - down, TS + 8), :]
            acc[first + side, pl.ds(base, TS + 8), :] += upper * (1.0 - frac_row) + lower * frac_row

    @pl.loop(0, (slots[0] + UNROLL - 1) // UNROLL)
    def _(m):
        placed = [place(slots[1 + m * UNROLL + u], u) for u in range(UNROLL)]
        for u in range(UNROLL):
            add_rows(u, *placed[u])

    for k in range(16):
        z_first, z_second, y_first, y_second = k >> 3, (k >> 2) & 1, (k >> 1) & 1, k & 1
        if not with_meta:
            z_first, z_second, y_first, y_second = z_second, z_first, y_second, y_first
        left, right = outs[z_first], outs[2 + y_first]
        at = z_second * 4 + y_first * 2 + y_second
        left[at, 0:PATCH, :] = acc[4 * k + 1, PAD : PAD + PATCH, :]
        if with_meta:
            for slot in range(CAP):
                left[at, PATCH + 8 * slot : PATCH + 8 * slot + 8, :] = meta[k * CAP + slot]
        right[y_second * 4 + z_first * 2 + z_second, :, :] = acc[4 * k + 2, PAD : PAD + PATCH, :]


def warp(with_meta, first, own, other, own_tiles, other_tiles):
    smem, vmem = pl.BlockSpec(memory_space=pltpu.SMEM), pl.BlockSpec(memory_space=pltpu.VMEM)
    anywhere = pl.BlockSpec(memory_space=pl.ANY)
    rows = PATCH + META if with_meta else PATCH
    left = jax.ShapeDtypeStruct((8, rows, TS), F32)
    right = jax.ShapeDtypeStruct((8, PATCH, TS), F32)
    outs, specs = [left, left, right, right], [vmem] * 4
    scratch = [
        pltpu.VMEM((UNROLL, 2, TS + 16, TS), F32),
        pltpu.VMEM((64, 384, TS), F32),
        pltpu.VMEM((2 * TILES, TS, TS), F32),
        pltpu.SemaphoreType.DMA((2,)),
    ]
    if with_meta:
        outs, specs = outs + [jax.ShapeDtypeStruct((SLOTS,), jnp.int32)], specs + [smem]
        scratch += [
            pltpu.SMEM((2, 16 * CAP + ROUTES + 1), jnp.int32),
            pltpu.VMEM((16 * CAP, 8, TS), F32),
            pltpu.VMEM((2 * TILES, TS), F32),
            pltpu.SMEM((2, 17), jnp.int32),
        ]
    return pl.pallas_call(
        functools.partial(warp_kernel, with_meta),
        out_shape=outs,
        in_specs=[smem] * 3 + [anywhere] * 2,
        out_specs=specs,
        scratch_shapes=scratch,
        compiler_params=pltpu.CompilerParams(vmem_limit_bytes=40 << 20),
        cost_estimate=pl.CostEstimate(flops=WARP_COST, bytes_accessed=8 << 20, transcendentals=0),
        name="warp_meta" if with_meta else "warp",
    )(first, own, other, own_tiles, other_tiles)


def finish_kernel(num_left, num_right, var_left, var_right, coadd, coadd_var):
    place_of = lax.broadcasted_iota(jnp.int32, (PATCH, TS), 0).astype(F32)

    def cover(offset, shift):
        u = place_of - offset
        lower = jnp.where((u >= 0.0) & (u <= TS - 1.0), 1.0 - shift, 0.0)
        return lower + jnp.where((u >= 1.0) & (u <= float(TS)), shift, 0.0)

    den = jnp.zeros((PATCH, PATCH), F32)
    for slot in range(CAP):
        at = PATCH + 8 * slot
        weight, row, col, frac_row, frac_col = (var_left[at + f : at + f + 1, :] for f in range(5))
        down, across = cover(row, frac_row) * weight, cover(col, frac_col)
        den += lax.dot_general(
            down, across, (((1,), (1,)), ((), ())), precision=lax.Precision.HIGHEST, preferred_element_type=F32
        )
    safe = jnp.maximum(den, 1.0)
    for num, var, lo in ((num_left, var_left, 0), (num_right, var_right, TS)):
        part = safe[:, lo : lo + TS]
        coadd[:, lo : lo + TS] = num[0:PATCH, :] / part
        coadd_var[:, lo : lo + TS] = var[0:PATCH, :] / (part * part)


def finish(num_left, num_right, var_left, var_right):
    vmem = pl.BlockSpec(memory_space=pltpu.VMEM)
    return pl.pallas_call(
        finish_kernel,
        out_shape=[jax.ShapeDtypeStruct((PATCH, PATCH), F32)] * 2,
        in_specs=[vmem] * 4,
        out_specs=[vmem] * 2,
        name="finish",
    )(num_left, num_right, var_left, var_right)


EDGES = (((0, 1), (1, 0), (2, 3), (3, 2)), ((1, 2), (2, 1), (3, 0), (0, 3)))


def over_patch(axis, edge):
    pairs = []
    for a, b in EDGES[edge]:
        for other in range(4):
            for core in range(2):
                src, dst = ((a, other), (b, other)) if axis == "z" else ((other, a), (other, b))
                pairs.append((src[0] * 8 + src[1] * 2 + core, dst[0] * 8 + dst[1] * 2 + core))
    return pairs


def halve(keep, send, order):
    for step, (axis, edge) in enumerate(order):
        got = lax.ppermute(send, "patch", over_patch(axis, edge))
        n = keep.shape[0] // 2
        if step == len(order) - 1:
            return keep[0] + got[0]
        send, keep = keep[n:] + got[n:], keep[:n] + got[:n]


def double(x, first):
    for edge in (first, 1 - first):
        x = x + lax.ppermute(x, "visit", EDGES[edge])
    return x


def shards(image, variance, intersections, boxes, shifts, basis_ids, coefs, taps):
    swap = [(i, i ^ 1) for i in range(32)]
    patch = lax.axis_index("patch")
    z, y = patch >> 3, (patch >> 1) & 3
    chip = lax.axis_index("visit") * 16 + z * 4 + y
    z, y = z ^ (z >> 1), y ^ (y >> 1)
    mine = ((z & 1) << 3) | ((z >> 1) << 2) | ((y & 1) << 1) | (y >> 1)
    where = jnp.stack([mine, patch & 1, chip])

    other_variance = lax.ppermute(variance, "patch", swap)
    table = pack(where, intersections, boxes, shifts, basis_ids, coefs)
    other_table = lax.ppermute(table, "patch", swap)
    matched = match(table, taps, image, variance)
    other_matched = lax.ppermute(matched, "patch", swap)
    var_left_keep, var_left_send, var_right_keep, var_right_send, slots = warp(
        True, where, table, other_table, variance, other_variance
    )
    num_left_keep, num_left_send, num_right_keep, num_right_send = warp(
        False, slots, table, other_table, matched, other_matched
    )
    z1, z2, y1, y2 = ("z", 0), ("z", 1), ("y", 0), ("y", 1)
    var_left = double(halve(var_left_keep, var_left_send, (z1, z2, y1, y2)), 0)
    var_right = double(halve(var_right_keep, var_right_send, (y1, y2, z1, z2)), 1)
    num_left = double(halve(num_left_keep, num_left_send, (z2, z1, y2, y1)), 0)
    num_right = double(halve(num_right_keep, num_right_send, (y2, y1, z2, z1)), 1)
    return tuple(finish(num_left, num_right, var_left, var_right))


def solution(mesh):
    split_spec = ("visit", "patch")
    in_specs = (
        P(split_spec, None, None),
        P(split_spec, None, None),
        P(split_spec, None),
        P(split_spec, None, None),
        P(split_spec, None, None),
        P(split_spec, None),
        P(split_spec, None),
        P(),
    )
    out_specs = (P("patch", None), P("patch", None))
    return jax.shard_map(shards, mesh=mesh, in_specs=in_specs, out_specs=out_specs, check_vma=False)
```

```python
import functools

import jax
import jax.numpy as jnp
from jax import lax
from jax.experimental import pallas as pl
from jax.experimental.pallas import tpu as pltpu
from jax.sharding import PartitionSpec as P

TS = 128
PATCH = 256
NB = 3
NBASIS = 8
HALF = 20
TILES = 32
ROUTES = 2 * TILES
CAP = 3
META = 24
PAD = 64
F32 = jnp.float32
BF16 = jnp.bfloat16

EMPTY = 1 << 24
UNROLL = 2
MATCH_UNROLL = 8
CHUNKS = 2
MATCH_COST = 100_000_000_000
WARP_COST = 10_000_000_000


def split(x):
    high = x.astype(BF16)
    return high, (x - high.astype(F32)).astype(BF16)


def pack_kernel(mine, intersections, boxes, shifts, out):
    out[...] = jnp.zeros_like(out)
    z, y, core = intersections[...] >> 3, (intersections[...] >> 1) & 3, intersections[...] & 1
    z, y = z ^ (z >> 1), y ^ (y >> 1)
    code = ((z & 1) << 3) | ((z >> 1) << 2) | ((y & 1) << 1) | (y >> 1)
    out[0:2, 0:TILES] = ((code ^ mine[0]) + 16 * core).astype(F32)
    for route in range(2):
        out[2 + 2 * route : 4 + 2 * route, 0:TILES] = boxes[route].astype(F32)
        out[6 + 2 * route : 8 + 2 * route, 0:TILES] = shifts[route]


def pack(mine, intersections, boxes, shifts):
    vmem = pl.BlockSpec(memory_space=pltpu.VMEM)
    return pl.pallas_call(
        pack_kernel,
        out_shape=jax.ShapeDtypeStruct((16, TS), F32),
        in_specs=[pl.BlockSpec(memory_space=pltpu.SMEM)] + [vmem] * 3,
        out_specs=vmem,
        name="pack",
    )(mine, intersections.T, boxes.transpose(1, 2, 0), shifts.transpose(1, 2, 0))


def match_kernel(
    basis_ids, coefs, taps_hbm, image_hbm, variance_hbm, out, taps, line, row_mats, col_mats, image, variance, sems, taps_sem
):
    size = TILES // CHUNKS
    copies = [
        [
            pltpu.make_async_copy(source.at[pl.ds(c * size, size)], target.at[pl.ds(c * size, size)], sems.at[i, c])
            for i, (source, target) in enumerate(((image_hbm, image), (variance_hbm, variance)))
        ]
        for c in range(CHUNKS)
    ]
    fetch = pltpu.make_async_copy(taps_hbm, taps, taps_sem)
    fetch.start()
    for pair in copies:
        for copy in pair:
            copy.start()
    i = lax.broadcasted_iota(jnp.int32, (TS, TS), 0)
    k = lax.broadcasted_iota(jnp.int32, (TS, TS), 1)
    near = jnp.abs(i - k) <= HALF
    none = jnp.zeros((TS, TS), BF16)
    line[...] = jnp.zeros_like(line)
    fetch.wait()
    for b in range(NBASIS):
        line[2 * b : 2 * b + 2, 0 : 2 * HALF + 1] = taps[b]
    line[...] = pltpu.roll(line[...], TS - HALF, 1)

    def square(high, low):
        return jnp.concatenate([jnp.concatenate([high, low], 1), jnp.concatenate([high, none], 1)], 0)

    for b in range(NBASIS):
        for side in range(2):
            band = jnp.broadcast_to(line[2 * b + side : 2 * b + side + 1, :], (TS, TS))
            band = jnp.where(near, pltpu.roll(band, 0, 1, stride=1, stride_axis=0), 0.0)
            if side == 0:
                row_mats[b] = jnp.concatenate(split(band.T), 1)
            else:
                col_mats[b] = square(*split(band))

    for c in range(CHUNKS):
        for copy in copies[c]:
            copy.wait()

        @pl.loop(c * size, (c + 1) * size, step=MATCH_UNROLL)
        def _(first):
            for t in [first + u for u in range(MATCH_UNROLL)]:
                weight = float(TS * TS) / jnp.sum(variance[t], axis=(0, 1), keepdims=True)
                pixels = square(*split(image[t]))
                total = None
                for j in range(NB):
                    basis = basis_ids[j, t]
                    p = jnp.dot(row_mats[basis], pixels, preferred_element_type=F32)
                    part = (p[:, :TS] + p[:, TS:]) * coefs[j, t]
                    p = jnp.dot(jnp.concatenate(split(part), 1), col_mats[basis], preferred_element_type=F32)
                    total = p if total is None else total + p
                out[t] = (total[:, :TS] + total[:, TS:]) * weight


def match(basis_ids, coefs, taps, image, variance):
    vmem, hbm = pl.BlockSpec(memory_space=pltpu.VMEM), pl.BlockSpec(memory_space=pltpu.HBM)
    return pl.pallas_call(
        match_kernel,
        out_shape=jax.ShapeDtypeStruct((TILES, TS, TS), F32),
        in_specs=[pl.BlockSpec(memory_space=pltpu.SMEM)] * 2 + [hbm] * 3,
        out_specs=vmem,
        scratch_shapes=[
            pltpu.VMEM((NBASIS, 2, 2 * HALF + 1), F32),
            pltpu.VMEM((2 * NBASIS, TS), F32),
            pltpu.VMEM((NBASIS, TS, 2 * TS), BF16),
            pltpu.VMEM((NBASIS, 2 * TS, 2 * TS), BF16),
            pltpu.VMEM((TILES, TS, TS), F32),
            pltpu.VMEM((TILES, TS, TS), F32),
            pltpu.SemaphoreType.DMA((2, CHUNKS)),
            pltpu.SemaphoreType.DMA,
        ],
        compiler_params=pltpu.CompilerParams(vmem_limit_bytes=40 << 20),
        cost_estimate=pl.CostEstimate(flops=MATCH_COST, bytes_accessed=6 << 20, transcendentals=0),
        name="match",
    )(*(pltpu.with_memory_space_constraint(x, pltpu.HBM) for x in (basis_ids.T, coefs.T, taps, image, variance)))


def warp_kernel(with_meta, *refs):
    first, own, other, own_tiles, other_tiles = refs[:5]
    outs = refs[5:9]
    if with_meta:
        slots = refs[9]
        stage, acc, meta, weights, counts, seen = refs[10:]
    else:
        slots = first
        stage, acc = refs[9:]
    lane = lax.broadcasted_iota(jnp.int32, (8, TS), 1)
    stage[:, :, 0:8, :] = jnp.zeros((2 * UNROLL, 2, 8, TS), F32)
    stage[:, :, 8 + TS :, :] = jnp.zeros((2 * UNROLL, 2, 8, TS), F32)
    for k in range(16):
        for side in (1, 2):
            acc[4 * k + side, PAD : PAD + PATCH, :] = jnp.zeros((PATCH, TS), F32)

    if with_meta:
        core, chip = first[1], first[2]
        meta[...] = jnp.zeros_like(meta)
        for side in range(2):
            counts[side] = 0
            for k in range(17):
                seen[side, k] = 0

        for route in range(2):

            @pl.loop(0, TILES)
            def _(t, route=route):
                for side, table in ((0, own), (1, other)):
                    k = table[route, t].astype(jnp.int32) - 16 * core
                    ours = (k >= 0) & (k < 16)
                    k = jnp.where(ours, k, 16)
                    slot, n = seen[side, k], counts[side]
                    slots[side, 1 + n] = (k << 16) + (slot << 8) + (2 * t + route)
                    seen[side, k] = slot + 1
                    counts[side] = n + ours.astype(jnp.int32)

        for side in range(2):
            n = counts[side]
            slots[side, 0] = n
            for u in range(3 * UNROLL):
                slots[side, 1 + n + u] = EMPTY

        for side, tiles in ((0, own_tiles), (1, other_tiles)):

            @pl.loop(0, TILES, step=8)
            def _(t, side=side, tiles=tiles):
                sums = jnp.concatenate([jnp.sum(tiles[t + u], axis=0, keepdims=True) for u in range(8)], 0)
                sums = jnp.sum(sums, axis=1, keepdims=True)
                at = pl.multiple_of(side * TILES + t, 8)
                weights[pl.ds(at, 8), :] = jnp.broadcast_to(float(TS * TS) / sums, (8, TS))

    def place(entry, u, side, table, tiles):
        item, slot, k = entry & 255, (entry >> 8) & 255, (entry >> 16) & 15
        t, route = item >> 1, item & 1
        row, col = table[2 + 2 * route, t].astype(jnp.int32), table[3 + 2 * route, t].astype(jnp.int32)
        frac_row, frac_col = table[6 + 2 * route, t], table[7 + 2 * route, t]
        real = jnp.where(entry >= EMPTY, 0.0, 1.0)
        near, far = jnp.full((8, TS), (1.0 - frac_col) * real), jnp.full((8, TS), frac_col * real)
        if with_meta:
            weight = jnp.broadcast_to(weights[pl.ds(side * TILES + t, 1), :], (8, TS))
            field = lax.broadcasted_iota(jnp.int32, (8, TS), 0)
            value = jnp.where(field == 1, row.astype(F32), weight)
            value = jnp.where(field == 2, col.astype(F32), value)
            value = jnp.where(field == 3, frac_row, value)
            value = jnp.where(field == 4, frac_col, value)
            value = jnp.where((field < 5) & (lane == 2 * chip + side), value * real, 0.0)
            meta[k * CAP + slot] += value
            near, far = near * (weight * weight), far * (weight * weight)
        turn = (col + TS) & (TS - 1)
        here = jnp.where(lane >= turn, near, 0.0)
        here_next = jnp.where(lane >= turn + 1, far, 0.0)
        over, over_next = near - here, far - here_next
        tile = tiles[t]
        r0 = pltpu.roll(tile, turn, 1).reshape(TS // 8, 8, TS)
        r1 = pltpu.roll(tile, (turn + 1) & (TS - 1), 1).reshape(TS // 8, 8, TS)
        stage[u, 0, 8 : 8 + TS, :] = (r0 * here + r1 * here_next).reshape(TS, TS)
        stage[u, 1, 8 : 8 + TS, :] = (r0 * over + r1 * over_next).reshape(TS, TS)
        return 4 * k + ((col + TS) >> 7), row + PAD, frac_row

    def add_rows(u, first, row, frac_row):
        down = row & 7
        base = pl.multiple_of((row >> 3) * 8, 8)
        for side in range(2):
            upper = stage[u, side, pl.ds(8 - down, TS + 8), :]
            lower = stage[u, side, pl.ds(7 - down, TS + 8), :]
            acc[first + side, pl.ds(base, TS + 8), :] += upper * (1.0 - frac_row) + lower * frac_row

    for side, table, tiles in ((0, own, own_tiles), (1, other, other_tiles)):
        start = [place(slots[side, 1 + u], u, side, table, tiles) for u in range(UNROLL)]

        def body(m, placed, side=side, table=table, tiles=tiles):
            for half in range(2):
                group = 2 * m + half + 1
                then = [
                    place(slots[side, 1 + group * UNROLL + u], UNROLL * (1 - half) + u, side, table, tiles)
                    for u in range(UNROLL)
                ]
                for u in range(UNROLL):
                    add_rows(UNROLL * half + u, *placed[u])
                placed = then
            return placed

        lax.fori_loop(0, (slots[side, 0] + 2 * UNROLL - 1) // (2 * UNROLL), body, start)

    for k in range(16):
        z_first, z_second, y_first, y_second = k >> 3, (k >> 2) & 1, (k >> 1) & 1, k & 1
        if not with_meta:
            z_first, z_second, y_first, y_second = z_second, z_first, y_second, y_first
        left, right = outs[z_first], outs[2 + y_first]
        at = z_second * 4 + y_first * 2 + y_second
        left[at, 0:PATCH, :] = acc[4 * k + 1, PAD : PAD + PATCH, :]
        if with_meta:
            for slot in range(CAP):
                left[at, PATCH + 8 * slot : PATCH + 8 * slot + 8, :] = meta[k * CAP + slot]
        right[y_second * 4 + z_first * 2 + z_second, :, :] = acc[4 * k + 2, PAD : PAD + PATCH, :]


def warp(with_meta, first, own, other, own_tiles, other_tiles):
    smem, vmem = pl.BlockSpec(memory_space=pltpu.SMEM), pl.BlockSpec(memory_space=pltpu.VMEM)
    rows = PATCH + META if with_meta else PATCH
    left = jax.ShapeDtypeStruct((8, rows, TS), F32)
    right = jax.ShapeDtypeStruct((8, PATCH, TS), F32)
    outs, specs = [left, left, right, right], [vmem] * 4
    scratch = [
        pltpu.VMEM((2 * UNROLL, 2, TS + 16, TS), F32),
        pltpu.VMEM((64, 384, TS), F32),
    ]
    if with_meta:
        outs, specs = outs + [jax.ShapeDtypeStruct((2, 128), jnp.int32)], specs + [smem]
        scratch += [
            pltpu.VMEM((16 * CAP, 8, TS), F32),
            pltpu.VMEM((2 * TILES, TS), F32),
            pltpu.SMEM((2,), jnp.int32),
            pltpu.SMEM((2, 17), jnp.int32),
        ]
    return pl.pallas_call(
        functools.partial(warp_kernel, with_meta),
        out_shape=outs,
        in_specs=[smem] * 3 + [vmem] * 2,
        out_specs=specs,
        scratch_shapes=scratch,
        compiler_params=pltpu.CompilerParams(vmem_limit_bytes=40 << 20),
        cost_estimate=pl.CostEstimate(flops=WARP_COST, bytes_accessed=8 << 20, transcendentals=0),
        name="warp_meta" if with_meta else "warp",
    )(first, own, other, own_tiles, other_tiles)


def cover_kernel(left, left_got, right, right_got, coadd_var, safe_ref):
    place_of = lax.broadcasted_iota(jnp.int32, (PATCH, TS), 0).astype(F32)

    def cover(offset, shift):
        u = place_of - offset
        lower = jnp.where((u >= 0.0) & (u <= TS - 1.0), 1.0 - shift, 0.0)
        return lower + jnp.where((u >= 1.0) & (u <= float(TS)), shift, 0.0)

    den = jnp.zeros((PATCH, PATCH), F32)
    for slot in range(CAP):
        at = PATCH + 8 * slot
        fields = left[at : at + 8, :] + left_got[at : at + 8, :]
        weight, row, col, frac_row, frac_col = (fields[f : f + 1, :] for f in range(5))
        down, across = cover(row, frac_row) * weight, cover(col, frac_col)
        den += lax.dot_general(
            down, across, (((1,), (1,)), ((), ())), precision=lax.Precision.HIGHEST, preferred_element_type=F32
        )
    safe = jnp.maximum(den, 1.0)
    safe_ref[...] = safe
    for var, got, lo in ((left, left_got, 0), (right, right_got, TS)):
        part = safe[:, lo : lo + TS]
        coadd_var[:, lo : lo + TS] = (var[0:PATCH, :] + got[0:PATCH, :]) / (part * part)


def divide_kernel(left, left_got, right, right_got, safe, coadd):
    coadd[:, 0:TS] = (left[...] + left_got[...]) / safe[:, 0:TS]
    coadd[:, TS:] = (right[...] + right_got[...]) / safe[:, TS:]


def finish(kernel, name, outs, *args):
    vmem = pl.BlockSpec(memory_space=pltpu.VMEM)
    return pl.pallas_call(
        kernel,
        out_shape=[jax.ShapeDtypeStruct((PATCH, PATCH), F32)] * outs,
        in_specs=[vmem] * len(args),
        out_specs=[vmem] * outs,
        compiler_params=pltpu.CompilerParams(vmem_limit_bytes=8 << 20),
        cost_estimate=pl.CostEstimate(flops=1_000_000_000, bytes_accessed=1 << 20, transcendentals=0),
        name=name,
    )(*args)


EDGES = (((0, 1), (1, 0), (2, 3), (3, 2)), ((1, 2), (2, 1), (3, 0), (0, 3)))


def over_patch(axis, edge):
    pairs = []
    for a, b in EDGES[edge]:
        for other in range(4):
            for core in range(2):
                src, dst = ((a, other), (b, other)) if axis == "z" else ((other, a), (other, b))
                pairs.append((src[0] * 8 + src[1] * 2 + core, dst[0] * 8 + dst[1] * 2 + core))
    return pairs


def halve(left, right, orders, ahead=()):
    parts, received = [left, right], []
    for step in range(4):
        got = [lax.ppermute(send, "patch", over_patch(*order[step])) for (_, send), order in zip(parts, orders)]
        if step < len(ahead):
            got = lax.optimization_barrier((*got, *ahead[step]))[:2]
        received.append(tuple(got))
        if step < 3:
            n = 8 >> (step + 1)
            parts = [(keep[:n] + g[:n], keep[n:] + g[n:]) for (keep, _), g in zip(parts, got)]
        else:
            parts = [keep[0] + g[0] for (keep, _), g in zip(parts, got)]
    return parts, received


def double(left, right):
    parts = [x + lax.ppermute(x, "visit", EDGES[first]) for x, first in ((left, 0), (right, 1))]
    return [y for x, first in zip(parts, (1, 0)) for y in (x, lax.ppermute(x, "visit", EDGES[first]))]


def shards(image, variance, intersections, boxes, shifts, basis_ids, coefs, taps):
    swap = [(i, i ^ 1) for i in range(32)]
    patch = lax.axis_index("patch")
    z, y = patch >> 3, (patch >> 1) & 3
    chip = lax.axis_index("visit") * 16 + z * 4 + y
    z, y = z ^ (z >> 1), y ^ (y >> 1)
    mine = ((z & 1) << 3) | ((z >> 1) << 2) | ((y & 1) << 1) | (y >> 1)
    where = jnp.stack([mine, patch & 1, chip])

    other_variance = lax.ppermute(variance, "patch", swap)
    table = pack(where, intersections, boxes, shifts)
    other_table = lax.ppermute(table, "patch", swap)
    matched = match(basis_ids, coefs, taps, image, variance)
    matched, other_table = lax.optimization_barrier((matched, other_table))
    other_matched = lax.ppermute(matched, "patch", swap)
    var_left_keep, var_left_send, var_right_keep, var_right_send, slots = warp(
        True, where, table, other_table, variance, other_variance
    )
    num_left_keep, num_left_send, num_right_keep, num_right_send = warp(
        False, slots, table, other_table, matched, other_matched
    )
    z1, z2, y1, y2 = ("z", 0), ("z", 1), ("y", 0), ("y", 1)
    var, ahead = halve((var_left_keep, var_left_send), (var_right_keep, var_right_send), ((z1, z2, y1, y2), (y1, y2, z1, z2)))
    num, _ = halve(
        (num_left_keep, num_left_send), (num_right_keep, num_right_send), ((z2, z1, y2, y1), (y2, y1, z2, z1)), ahead
    )
    var, num = double(*var), double(*num)
    coadd_var, safe = finish(cover_kernel, "cover", 2, *var)
    (coadd,) = finish(divide_kernel, "divide", 1, *num, safe)
    return coadd, coadd_var


def solution(mesh):
    split_spec = ("visit", "patch")
    in_specs = (
        P(split_spec, None, None),
        P(split_spec, None, None),
        P(split_spec, None),
        P(split_spec, None, None),
        P(split_spec, None, None),
        P(split_spec, None),
        P(split_spec, None),
        P(),
    )
    out_specs = (P("patch", None), P("patch", None))
    return jax.shard_map(shards, mesh=mesh, in_specs=in_specs, out_specs=out_specs, check_vma=False)
```

```python
import functools

import jax
import jax.numpy as jnp
from jax import lax
from jax.experimental import pallas as pl
from jax.experimental.pallas import tpu as pltpu
from jax.sharding import PartitionSpec as P

TS = 128
PATCH = 256
NB = 3
NBASIS = 8
HALF = 20
TILES = 32
ROUTES = 2 * TILES
CAP = 3
META = 24
PAD = 64
F32 = jnp.float32
BF16 = jnp.bfloat16

EMPTY = 1 << 24
UNROLL = 2
MATCH_UNROLL = 8
CHUNKS = 4
MATCH_COST = 100_000_000_000
WARP_COST = 10_000_000_000


def split(x):
    high = x.astype(BF16)
    return high, (x - high.astype(F32)).astype(BF16)


def here():
    patch = lax.axis_index("patch")
    z, y = patch >> 3, (patch >> 1) & 3
    chip = lax.axis_index("visit") * 16 + z * 4 + y
    return place_code(z, y), patch & 1, chip


def place_code(z, y):
    z, y = z ^ (z >> 1), y ^ (y >> 1)
    return ((z & 1) << 3) | ((z >> 1) << 2) | ((y & 1) << 1) | (y >> 1)


def pack_kernel(intersections, boxes, shifts, out):
    mine = here()[0]
    out[...] = jnp.zeros_like(out)
    earlier_item = lax.broadcasted_iota(jnp.int32, (TILES, TILES), 0)
    item = lax.broadcasted_iota(jnp.int32, (TILES, TILES), 1)
    dest = [intersections[route : route + 1, :] for route in range(2)]

    def earlier(rows):
        columns = [jnp.sum(jnp.where(earlier_item == item, row, 0), axis=1, keepdims=True) for row in rows]
        counts = []
        for route, row in enumerate(rows):
            same = jnp.where((columns[route] == row) & (earlier_item < item), 1, 0)
            if route == 1:
                same = same + jnp.where(columns[0] == row, 1, 0)
            counts.append(jnp.sum(same, axis=0, keepdims=True))
        return counts

    slots, places = earlier(dest), earlier([d & 1 for d in dest])
    for route in range(2):
        d = dest[route]
        code = place_code(d >> 3, (d >> 1) & 3) ^ mine
        out[route : route + 1, 0:TILES] = (code + (slots[route] << 4) + ((d & 1) << 8)).astype(F32)
        out[10 + route : 11 + route, 0:TILES] = places[route].astype(F32)
        out[2 + 2 * route : 4 + 2 * route, 0:TILES] = boxes[route].astype(F32)
        out[6 + 2 * route : 8 + 2 * route, 0:TILES] = shifts[route]
    second = jnp.sum(intersections[...] & 1).astype(F32)
    lane = lax.broadcasted_iota(jnp.int32, (1, TS), 1)
    out[12:13, :] = jnp.where(lane == 0, ROUTES - second, second)


def pack(intersections, boxes, shifts):
    vmem = pl.BlockSpec(memory_space=pltpu.VMEM)
    return pl.pallas_call(
        pack_kernel,
        out_shape=jax.ShapeDtypeStruct((16, TS), F32),
        in_specs=[vmem] * 3,
        out_specs=vmem,
        name="pack",
    )(intersections.T, boxes.transpose(1, 2, 0), shifts.transpose(1, 2, 0))


def match_kernel(
    basis_ids, coefs, taps_hbm, image_hbm, variance_hbm, out, taps, line, row_mats, col_mats, image, variance, sems, taps_sem
):
    size = TILES // CHUNKS
    copies = [
        [
            pltpu.make_async_copy(source.at[pl.ds(c * size, size)], target.at[pl.ds(c * size, size)], sems.at[i, c])
            for i, (source, target) in enumerate(((image_hbm, image), (variance_hbm, variance)))
        ]
        for c in range(CHUNKS)
    ]
    fetch = pltpu.make_async_copy(taps_hbm, taps, taps_sem)
    fetch.start()
    for pair in copies:
        for copy in pair:
            copy.start()
    i = lax.broadcasted_iota(jnp.int32, (TS, TS), 0)
    k = lax.broadcasted_iota(jnp.int32, (TS, TS), 1)
    near = jnp.abs(i - k) <= HALF
    none = jnp.zeros((TS, TS), BF16)
    line[...] = jnp.zeros_like(line)
    fetch.wait()
    for b in range(NBASIS):
        line[2 * b : 2 * b + 2, 0 : 2 * HALF + 1] = taps[b]
    line[...] = pltpu.roll(line[...], TS - HALF, 1)

    def square(high, low):
        return jnp.concatenate([jnp.concatenate([high, low], 1), jnp.concatenate([high, none], 1)], 0)

    for b in range(NBASIS):
        for side in range(2):
            band = jnp.broadcast_to(line[2 * b + side : 2 * b + side + 1, :], (TS, TS))
            band = jnp.where(near, pltpu.roll(band, 0, 1, stride=1, stride_axis=0), 0.0)
            if side == 0:
                row_mats[b] = jnp.concatenate(split(band.T), 1)
            else:
                col_mats[b] = square(*split(band))

    for c in range(CHUNKS):
        for copy in copies[c]:
            copy.wait()

        @pl.loop(c * size, (c + 1) * size, step=MATCH_UNROLL)
        def _(first):
            for t in [first + u for u in range(MATCH_UNROLL)]:
                weight = float(TS * TS) / jnp.sum(variance[t], axis=(0, 1), keepdims=True)
                pixels = square(*split(image[t]))
                total = None
                for j in range(NB):
                    basis = basis_ids[j, t]
                    p = jnp.dot(row_mats[basis], pixels, preferred_element_type=F32)
                    part = (p[:, :TS] + p[:, TS:]) * coefs[j, t]
                    p = jnp.dot(jnp.concatenate(split(part), 1), col_mats[basis], preferred_element_type=F32)
                    total = p if total is None else total + p
                out[t] = (total[:, :TS] + total[:, TS:]) * weight


def match(basis_ids, coefs, taps, image, variance):
    vmem, hbm = pl.BlockSpec(memory_space=pltpu.VMEM), pl.BlockSpec(memory_space=pltpu.HBM)
    return pl.pallas_call(
        match_kernel,
        out_shape=jax.ShapeDtypeStruct((TILES, TS, TS), F32),
        in_specs=[pl.BlockSpec(memory_space=pltpu.SMEM)] * 2 + [hbm] * 3,
        out_specs=vmem,
        scratch_shapes=[
            pltpu.VMEM((NBASIS, 2, 2 * HALF + 1), F32),
            pltpu.VMEM((2 * NBASIS, TS), F32),
            pltpu.VMEM((NBASIS, TS, 2 * TS), BF16),
            pltpu.VMEM((NBASIS, 2 * TS, 2 * TS), BF16),
            pltpu.VMEM((TILES, TS, TS), F32),
            pltpu.VMEM((TILES, TS, TS), F32),
            pltpu.SemaphoreType.DMA((2, CHUNKS)),
            pltpu.SemaphoreType.DMA,
        ],
        compiler_params=pltpu.CompilerParams(vmem_limit_bytes=40 << 20),
        cost_estimate=pl.CostEstimate(flops=MATCH_COST, bytes_accessed=6 << 20, transcendentals=0),
        name="match",
    )(*(pltpu.with_memory_space_constraint(x, pltpu.HBM) for x in (basis_ids.T, coefs.T, taps, image, variance)))


def warp_kernel(with_meta, *refs):
    if with_meta:
        own, other, own_tiles, other_tiles = refs[:4]
        outs, slots = refs[4:8], refs[8]
        stage, acc, meta, weights = refs[9:]
    else:
        slots, own, other, own_tiles, other_tiles = refs[:5]
        outs = refs[5:9]
        stage, acc = refs[9:]
    lane = lax.broadcasted_iota(jnp.int32, (8, TS), 1)
    stage[:, :, 0:8, :] = jnp.zeros((2 * UNROLL, 2, 8, TS), F32)
    stage[:, :, 8 + TS :, :] = jnp.zeros((2 * UNROLL, 2, 8, TS), F32)
    for k in range(16):
        for side in (1, 2):
            acc[4 * k + side, PAD : PAD + PATCH, :] = jnp.zeros((PATCH, TS), F32)

    if with_meta:
        _, core, chip = here()
        meta[...] = jnp.zeros_like(meta)

        @pl.loop(0, TILES, step=8)
        def _(first):
            for side, table, tiles in ((0, own, own_tiles), (1, other, other_tiles)):
                for route in range(2):
                    for t in [first + u for u in range(8)]:
                        what = table[route, t].astype(jnp.int32)
                        at = jnp.where((what >> 8) == core, table[10 + route, t].astype(jnp.int32) + 1, 127)
                        slots[side, at] = (what << 8) + (2 * t + route)
                sums = jnp.concatenate([jnp.sum(tiles[first + u], axis=0, keepdims=True) for u in range(8)], 0)
                sums = jnp.sum(sums, axis=1, keepdims=True)
                at = pl.multiple_of(side * TILES + first, 8)
                weights[pl.ds(at, 8), :] = jnp.broadcast_to(float(TS * TS) / sums, (8, TS))

        for side, table in ((0, own), (1, other)):
            n = table[12, core].astype(jnp.int32)
            slots[side, 0] = n
            for u in range(3 * UNROLL):
                slots[side, 1 + n + u] = EMPTY

    def place(entry, u, side, table, tiles):
        item, k, slot = entry & 255, (entry >> 8) & 15, (entry >> 12) & 3
        t, route = item >> 1, item & 1
        row, col = table[2 + 2 * route, t].astype(jnp.int32), table[3 + 2 * route, t].astype(jnp.int32)
        frac_row, frac_col = table[6 + 2 * route, t], table[7 + 2 * route, t]
        real = jnp.where(entry >= EMPTY, 0.0, 1.0)
        near, far = jnp.full((8, TS), (1.0 - frac_col) * real), jnp.full((8, TS), frac_col * real)
        if with_meta:
            weight = jnp.broadcast_to(weights[pl.ds(side * TILES + t, 1), :], (8, TS))
            field = lax.broadcasted_iota(jnp.int32, (8, TS), 0)
            value = jnp.where(field == 1, row.astype(F32), weight)
            value = jnp.where(field == 2, col.astype(F32), value)
            value = jnp.where(field == 3, frac_row, value)
            value = jnp.where(field == 4, frac_col, value)
            value = jnp.where((field < 5) & (lane == 2 * chip + side), value * real, 0.0)
            meta[k * CAP + slot] += value
            near, far = near * (weight * weight), far * (weight * weight)
        turn = (col + TS) & (TS - 1)
        here = jnp.where(lane >= turn, near, 0.0)
        here_next = jnp.where(lane >= turn + 1, far, 0.0)
        over, over_next = near - here, far - here_next
        tile = tiles[t]
        r0 = pltpu.roll(tile, turn, 1).reshape(TS // 8, 8, TS)
        r1 = pltpu.roll(tile, (turn + 1) & (TS - 1), 1).reshape(TS // 8, 8, TS)
        stage[u, 0, 8 : 8 + TS, :] = (r0 * here + r1 * here_next).reshape(TS, TS)
        stage[u, 1, 8 : 8 + TS, :] = (r0 * over + r1 * over_next).reshape(TS, TS)
        return 4 * k + ((col + TS) >> 7), row + PAD, frac_row

    def add_rows(u, first, row, frac_row):
        down = row & 7
        base = pl.multiple_of((row >> 3) * 8, 8)
        for side in range(2):
            upper = stage[u, side, pl.ds(8 - down, TS + 8), :]
            lower = stage[u, side, pl.ds(7 - down, TS + 8), :]
            acc[first + side, pl.ds(base, TS + 8), :] += upper * (1.0 - frac_row) + lower * frac_row

    for side, table, tiles in ((0, own, own_tiles), (1, other, other_tiles)):
        start = [place(slots[side, 1 + u], u, side, table, tiles) for u in range(UNROLL)]

        def body(m, placed, side=side, table=table, tiles=tiles):
            for half in range(2):
                group = 2 * m + half + 1
                then = [
                    place(slots[side, 1 + group * UNROLL + u], UNROLL * (1 - half) + u, side, table, tiles)
                    for u in range(UNROLL)
                ]
                for u in range(UNROLL):
                    add_rows(UNROLL * half + u, *placed[u])
                placed = then
            return placed

        lax.fori_loop(0, (slots[side, 0] + 2 * UNROLL - 1) // (2 * UNROLL), body, start)

    for k in range(16):
        z_first, z_second, y_first, y_second = k >> 3, (k >> 2) & 1, (k >> 1) & 1, k & 1
        if not with_meta:
            z_first, z_second, y_first, y_second = z_second, z_first, y_second, y_first
        left, right = outs[z_first], outs[2 + y_first]
        at = y_first * 4 + z_second * 2 + y_second
        left[at, 0:PATCH, :] = acc[4 * k + 1, PAD : PAD + PATCH, :]
        if with_meta:
            for slot in range(CAP):
                left[at, PATCH + 8 * slot : PATCH + 8 * slot + 8, :] = meta[k * CAP + slot]
        right[z_first * 4 + y_second * 2 + z_second, :, :] = acc[4 * k + 2, PAD : PAD + PATCH, :]


def warp(with_meta, *args):
    smem, vmem = pl.BlockSpec(memory_space=pltpu.SMEM), pl.BlockSpec(memory_space=pltpu.VMEM)
    rows = PATCH + META if with_meta else PATCH
    left = jax.ShapeDtypeStruct((8, rows, TS), F32)
    right = jax.ShapeDtypeStruct((8, PATCH, TS), F32)
    outs, specs = [left, left, right, right], [vmem] * 4
    scratch = [
        pltpu.VMEM((2 * UNROLL, 2, TS + 16, TS), F32),
        pltpu.VMEM((64, 384, TS), F32),
    ]
    if with_meta:
        outs, specs = outs + [jax.ShapeDtypeStruct((2, 128), jnp.int32)], specs + [smem]
        scratch += [
            pltpu.VMEM((16 * CAP, 8, TS), F32),
            pltpu.VMEM((2 * TILES, TS), F32),
        ]
    return pl.pallas_call(
        functools.partial(warp_kernel, with_meta),
        out_shape=outs,
        in_specs=[smem] * (len(args) - 2) + [vmem] * 2,
        out_specs=specs,
        scratch_shapes=scratch,
        compiler_params=pltpu.CompilerParams(vmem_limit_bytes=40 << 20),
        cost_estimate=pl.CostEstimate(flops=WARP_COST, bytes_accessed=8 << 20, transcendentals=0),
        name="warp_meta" if with_meta else "warp",
    )(*args)


def cover_kernel(left, left_got, right, right_got, coadd_var, safe_ref):
    place_of = lax.broadcasted_iota(jnp.int32, (PATCH, TS), 0).astype(F32)

    def cover(offset, shift):
        u = place_of - offset
        lower = jnp.where((u >= 0.0) & (u <= TS - 1.0), 1.0 - shift, 0.0)
        return lower + jnp.where((u >= 1.0) & (u <= float(TS)), shift, 0.0)

    den = jnp.zeros((PATCH, PATCH), F32)
    for slot in range(CAP):
        at = PATCH + 8 * slot
        fields = left[at : at + 8, :] + left_got[at : at + 8, :]
        weight, row, col, frac_row, frac_col = (fields[f : f + 1, :] for f in range(5))
        down, across = cover(row, frac_row) * weight, cover(col, frac_col)
        den += lax.dot_general(
            down, across, (((1,), (1,)), ((), ())), precision=lax.Precision.HIGHEST, preferred_element_type=F32
        )
    safe = jnp.maximum(den, 1.0)
    safe_ref[...] = safe
    for var, got, lo in ((left, left_got, 0), (right, right_got, TS)):
        part = safe[:, lo : lo + TS]
        coadd_var[:, lo : lo + TS] = (var[0:PATCH, :] + got[0:PATCH, :]) / (part * part)


def divide_kernel(left, left_got, right, right_got, safe, coadd):
    coadd[:, 0:TS] = (left[...] + left_got[...]) / safe[:, 0:TS]
    coadd[:, TS:] = (right[...] + right_got[...]) / safe[:, TS:]


def finish(kernel, name, outs, *args):
    vmem = pl.BlockSpec(memory_space=pltpu.VMEM)
    return pl.pallas_call(
        kernel,
        out_shape=[jax.ShapeDtypeStruct((PATCH, PATCH), F32)] * outs,
        in_specs=[vmem] * len(args),
        out_specs=[vmem] * outs,
        compiler_params=pltpu.CompilerParams(vmem_limit_bytes=8 << 20),
        cost_estimate=pl.CostEstimate(flops=1_000_000_000, bytes_accessed=1 << 20, transcendentals=0),
        name=name,
    )(*args)


EDGES = (((0, 1), (1, 0), (2, 3), (3, 2)), ((1, 2), (2, 1), (3, 0), (0, 3)))


def over_patch(axis, edge):
    pairs = []
    for a, b in EDGES[edge]:
        for other in range(4):
            for core in range(2):
                src, dst = ((a, other), (b, other)) if axis == "z" else ((other, a), (other, b))
                pairs.append((src[0] * 8 + src[1] * 2 + core, dst[0] * 8 + dst[1] * 2 + core))
    return pairs


def halve(left, right, orders, ahead=()):
    parts, left_over = [left, right], []
    for step in range(4):
        got = [lax.ppermute(send, "patch", over_patch(*order[step])) for (_, send), order in zip(parts, orders)]
        if step < len(ahead):
            got = lax.optimization_barrier((*got, *ahead[step]))[:2]
        if step < 3:
            n = 8 >> (step + 1)
            parts = [(keep[:n] + g[:n], keep[n:] + g[n:]) for (keep, _), g in zip(parts, got)]
            left_over.append([send for _, send in parts])
        else:
            parts = [keep[0] + g[0] for (keep, _), g in zip(parts, got)]
            left_over.append(parts)
    return parts, left_over


def double(left, right):
    parts = [x + lax.ppermute(x, "visit", EDGES[first]) for x, first in ((left, 0), (right, 1))]
    return [y for x, first in zip(parts, (1, 0)) for y in (x, lax.ppermute(x, "visit", EDGES[first]))]


def shards(image, variance, intersections, boxes, shifts, basis_ids, coefs, taps):
    swap = [(i, i ^ 1) for i in range(32)]
    other_variance = lax.ppermute(variance, "patch", swap)
    table = pack(intersections, boxes, shifts)
    other_table = lax.ppermute(table, "patch", swap)
    matched = match(basis_ids, coefs, taps, image, variance)
    matched, other_table = lax.optimization_barrier((matched, other_table))
    other_matched = lax.ppermute(matched, "patch", swap)
    var_left_keep, var_left_send, var_right_keep, var_right_send, slots = warp(
        True, table, other_table, variance, other_variance
    )
    num_left_keep, num_left_send, num_right_keep, num_right_send = warp(
        False, slots, table, other_table, matched, other_matched
    )
    z1, z2, y1, y2 = ("z", 0), ("z", 1), ("y", 0), ("y", 1)
    var, ahead = halve((var_left_keep, var_left_send), (var_right_keep, var_right_send), ((z1, y1, z2, y2), (y1, z1, y2, z2)))
    num, _ = halve(
        (num_left_keep, num_left_send), (num_right_keep, num_right_send), ((z2, y2, z1, y1), (y2, z2, y1, z1)), ahead
    )
    var, num = double(*var), double(*num)
    coadd_var, safe = finish(cover_kernel, "cover", 2, *var)
    (coadd,) = finish(divide_kernel, "divide", 1, *num, safe)
    return coadd, coadd_var


def solution(mesh):
    split_spec = ("visit", "patch")
    in_specs = (
        P(split_spec, None, None),
        P(split_spec, None, None),
        P(split_spec, None),
        P(split_spec, None, None),
        P(split_spec, None, None),
        P(split_spec, None),
        P(split_spec, None),
        P(),
    )
    out_specs = (P("patch", None), P("patch", None))
    return jax.shard_map(shards, mesh=mesh, in_specs=in_specs, out_specs=out_specs, check_vma=False)
```

```python
import functools

import jax
import jax.numpy as jnp
from jax import lax
from jax.experimental import pallas as pl
from jax.experimental.pallas import tpu as pltpu
from jax.sharding import PartitionSpec as P

TS = 128
PATCH = 256
NB = 3
NBASIS = 8
HALF = 20
TILES = 32
ROUTES = 2 * TILES
CAP = 3
META = 24
PAD = 64
F32 = jnp.float32
BF16 = jnp.bfloat16

EMPTY = 1 << 24
UNROLL = 2
MATCH_UNROLL = 8
CHUNKS = 4
MATCH_COST = 100_000_000_000
WARP_COST = 10_000_000_000


def split(x):
    high = x.astype(BF16)
    return high, (x - high.astype(F32)).astype(BF16)


def here():
    patch = lax.axis_index("patch")
    z, y = patch >> 3, (patch >> 1) & 3
    return z, y, patch & 1, lax.axis_index("visit") * 16 + z * 4 + y


def place_code(z, y, core):
    first, second = jnp.where(core == 0, z, y), jnp.where(core == 0, y, z)
    first, second = first ^ (first >> 1), second ^ (second >> 1)
    return ((first & 1) << 3) | ((first >> 1) << 2) | ((second & 1) << 1) | (second >> 1)


def pack_kernel(intersections, boxes, shifts, out):
    z, y, _, _ = here()
    out[...] = jnp.zeros_like(out)
    earlier_item = lax.broadcasted_iota(jnp.int32, (TILES, TILES), 0)
    item = lax.broadcasted_iota(jnp.int32, (TILES, TILES), 1)
    dest = [intersections[route : route + 1, :] for route in range(2)]

    def earlier(rows):
        columns = [jnp.sum(jnp.where(earlier_item == item, row, 0), axis=1, keepdims=True) for row in rows]
        counts = []
        for route, row in enumerate(rows):
            same = jnp.where((columns[route] == row) & (earlier_item < item), 1, 0)
            if route == 1:
                same = same + jnp.where(columns[0] == row, 1, 0)
            counts.append(jnp.sum(same, axis=0, keepdims=True))
        return counts

    slots, places = earlier(dest), earlier([d & 1 for d in dest])
    for route in range(2):
        d = dest[route]
        code = place_code(d >> 3, (d >> 1) & 3, d & 1) ^ place_code(z, y, d & 1)
        out[route : route + 1, 0:TILES] = (code + (slots[route] << 4) + ((d & 1) << 8)).astype(F32)
        out[10 + route : 11 + route, 0:TILES] = places[route].astype(F32)
        out[2 + 2 * route : 4 + 2 * route, 0:TILES] = boxes[route].astype(F32)
        out[6 + 2 * route : 8 + 2 * route, 0:TILES] = shifts[route]
    second = jnp.sum(intersections[...] & 1).astype(F32)
    lane = lax.broadcasted_iota(jnp.int32, (1, TS), 1)
    out[12:13, :] = jnp.where(lane == 0, ROUTES - second, second)


def pack(intersections, boxes, shifts):
    vmem = pl.BlockSpec(memory_space=pltpu.VMEM)
    return pl.pallas_call(
        pack_kernel,
        out_shape=jax.ShapeDtypeStruct((16, TS), F32),
        in_specs=[vmem] * 3,
        out_specs=vmem,
        name="pack",
    )(intersections.T, boxes.transpose(1, 2, 0), shifts.transpose(1, 2, 0))


def match_kernel(
    basis_ids, coefs, taps_hbm, image_hbm, variance_hbm, out, taps, line, row_mats, col_mats, image, variance, sems, taps_sem
):
    size = TILES // CHUNKS
    copies = [
        [
            pltpu.make_async_copy(source.at[pl.ds(c * size, size)], target.at[pl.ds(c * size, size)], sems.at[i, c])
            for i, (source, target) in enumerate(((image_hbm, image), (variance_hbm, variance)))
        ]
        for c in range(CHUNKS)
    ]
    fetch = pltpu.make_async_copy(taps_hbm, taps, taps_sem)
    fetch.start()
    for pair in copies:
        for copy in pair:
            copy.start()
    i = lax.broadcasted_iota(jnp.int32, (TS, TS), 0)
    k = lax.broadcasted_iota(jnp.int32, (TS, TS), 1)
    near = jnp.abs(i - k) <= HALF
    none = jnp.zeros((TS, TS), BF16)
    line[...] = jnp.zeros_like(line)
    fetch.wait()
    for b in range(NBASIS):
        line[2 * b : 2 * b + 2, 0 : 2 * HALF + 1] = taps[b]
    line[...] = pltpu.roll(line[...], TS - HALF, 1)

    def square(high, low):
        return jnp.concatenate([jnp.concatenate([high, low], 1), jnp.concatenate([high, none], 1)], 0)

    for b in range(NBASIS):
        for side in range(2):
            band = jnp.broadcast_to(line[2 * b + side : 2 * b + side + 1, :], (TS, TS))
            band = jnp.where(near, pltpu.roll(band, 0, 1, stride=1, stride_axis=0), 0.0)
            if side == 0:
                row_mats[b] = jnp.concatenate(split(band.T), 1)
            else:
                col_mats[b] = square(*split(band))

    for c in range(CHUNKS):
        for copy in copies[c]:
            copy.wait()

        @pl.loop(c * size, (c + 1) * size, step=MATCH_UNROLL)
        def _(first):
            for t in [first + u for u in range(MATCH_UNROLL)]:
                weight = float(TS * TS) / jnp.sum(variance[t], axis=(0, 1), keepdims=True)
                pixels = square(*split(image[t]))
                total = None
                for j in range(NB):
                    basis = basis_ids[j, t]
                    p = jnp.dot(row_mats[basis], pixels, preferred_element_type=F32)
                    part = (p[:, :TS] + p[:, TS:]) * coefs[j, t]
                    p = jnp.dot(jnp.concatenate(split(part), 1), col_mats[basis], preferred_element_type=F32)
                    total = p if total is None else total + p
                out[t] = (total[:, :TS] + total[:, TS:]) * weight


def match(basis_ids, coefs, taps, image, variance):
    vmem, hbm = pl.BlockSpec(memory_space=pltpu.VMEM), pl.BlockSpec(memory_space=pltpu.HBM)
    return pl.pallas_call(
        match_kernel,
        out_shape=jax.ShapeDtypeStruct((TILES, TS, TS), F32),
        in_specs=[pl.BlockSpec(memory_space=pltpu.SMEM)] * 2 + [hbm] * 3,
        out_specs=vmem,
        scratch_shapes=[
            pltpu.VMEM((NBASIS, 2, 2 * HALF + 1), F32),
            pltpu.VMEM((2 * NBASIS, TS), F32),
            pltpu.VMEM((NBASIS, TS, 2 * TS), BF16),
            pltpu.VMEM((NBASIS, 2 * TS, 2 * TS), BF16),
            pltpu.VMEM((TILES, TS, TS), F32),
            pltpu.VMEM((TILES, TS, TS), F32),
            pltpu.SemaphoreType.DMA((2, CHUNKS)),
            pltpu.SemaphoreType.DMA,
        ],
        compiler_params=pltpu.CompilerParams(vmem_limit_bytes=40 << 20),
        cost_estimate=pl.CostEstimate(flops=MATCH_COST, bytes_accessed=6 << 20, transcendentals=0),
        name="match",
    )(*(pltpu.with_memory_space_constraint(x, pltpu.HBM) for x in (basis_ids.T, coefs.T, taps, image, variance)))


def warp_kernel(with_meta, *refs):
    if with_meta:
        own, other, own_tiles, other_tiles = refs[:4]
        outs, slots = refs[4:6], refs[6]
        stage, acc, meta, weights = refs[7:]
    else:
        slots, own, other, own_tiles, other_tiles = refs[:5]
        outs = refs[5:7]
        stage, acc = refs[7:]
    lane = lax.broadcasted_iota(jnp.int32, (8, TS), 1)
    stage[:, :, 0:8, :] = jnp.zeros((2 * UNROLL, 2, 8, TS), F32)
    stage[:, :, 8 + TS :, :] = jnp.zeros((2 * UNROLL, 2, 8, TS), F32)
    for k in range(16):
        for side in (1, 2):
            acc[4 * k + side, PAD : PAD + PATCH, :] = jnp.zeros((PATCH, TS), F32)

    if with_meta:
        _, _, core, chip = here()
        meta[...] = jnp.zeros_like(meta)

        @pl.loop(0, TILES, step=8)
        def _(first):
            for side, table, tiles in ((0, own, own_tiles), (1, other, other_tiles)):
                for route in range(2):
                    for t in [first + u for u in range(8)]:
                        what = table[route, t].astype(jnp.int32)
                        at = jnp.where((what >> 8) == core, table[10 + route, t].astype(jnp.int32) + 1, 127)
                        slots[side, at] = (what << 8) + (2 * t + route)
                sums = jnp.concatenate([jnp.sum(tiles[first + u], axis=0, keepdims=True) for u in range(8)], 0)
                sums = jnp.sum(sums, axis=1, keepdims=True)
                at = pl.multiple_of(side * TILES + first, 8)
                weights[pl.ds(at, 8), :] = jnp.broadcast_to(float(TS * TS) / sums, (8, TS))

        for side, table in ((0, own), (1, other)):
            n = table[12, core].astype(jnp.int32)
            slots[side, 0] = n
            for u in range(3 * UNROLL):
                slots[side, 1 + n + u] = EMPTY

    def place(entry, u, side, table, tiles):
        item, k, slot = entry & 255, (entry >> 8) & 15, (entry >> 12) & 3
        t, route = item >> 1, item & 1
        row, col = table[2 + 2 * route, t].astype(jnp.int32), table[3 + 2 * route, t].astype(jnp.int32)
        frac_row, frac_col = table[6 + 2 * route, t], table[7 + 2 * route, t]
        real = jnp.where(entry >= EMPTY, 0.0, 1.0)
        near, far = jnp.full((8, TS), (1.0 - frac_col) * real), jnp.full((8, TS), frac_col * real)
        if with_meta:
            weight = jnp.broadcast_to(weights[pl.ds(side * TILES + t, 1), :], (8, TS))
            field = lax.broadcasted_iota(jnp.int32, (8, TS), 0)
            value = jnp.where(field == 1, row.astype(F32), weight)
            value = jnp.where(field == 2, col.astype(F32), value)
            value = jnp.where(field == 3, frac_row, value)
            value = jnp.where(field == 4, frac_col, value)
            value = jnp.where((field < 5) & (lane == 2 * chip + side), value * real, 0.0)
            meta[k * CAP + slot] += value
            near, far = near * (weight * weight), far * (weight * weight)
        turn = (col + TS) & (TS - 1)
        here = jnp.where(lane >= turn, near, 0.0)
        here_next = jnp.where(lane >= turn + 1, far, 0.0)
        over, over_next = near - here, far - here_next
        tile = tiles[t]
        r0 = pltpu.roll(tile, turn, 1).reshape(TS // 8, 8, TS)
        r1 = pltpu.roll(tile, (turn + 1) & (TS - 1), 1).reshape(TS // 8, 8, TS)
        stage[u, 0, 8 : 8 + TS, :] = (r0 * here + r1 * here_next).reshape(TS, TS)
        stage[u, 1, 8 : 8 + TS, :] = (r0 * over + r1 * over_next).reshape(TS, TS)
        return 4 * k + ((col + TS) >> 7), row + PAD, frac_row

    def add_rows(u, first, row, frac_row):
        down = row & 7
        base = pl.multiple_of((row >> 3) * 8, 8)
        for side in range(2):
            upper = stage[u, side, pl.ds(8 - down, TS + 8), :]
            lower = stage[u, side, pl.ds(7 - down, TS + 8), :]
            acc[first + side, pl.ds(base, TS + 8), :] += upper * (1.0 - frac_row) + lower * frac_row

    for side, table, tiles in ((0, own, own_tiles), (1, other, other_tiles)):
        start = [place(slots[side, 1 + u], u, side, table, tiles) for u in range(UNROLL)]

        def body(m, placed, side=side, table=table, tiles=tiles):
            for half in range(2):
                group = 2 * m + half + 1
                then = [
                    place(slots[side, 1 + group * UNROLL + u], UNROLL * (1 - half) + u, side, table, tiles)
                    for u in range(UNROLL)
                ]
                for u in range(UNROLL):
                    add_rows(UNROLL * half + u, *placed[u])
                placed = then
            return placed

        lax.fori_loop(0, (slots[side, 0] + 2 * UNROLL - 1) // (2 * UNROLL), body, start)

    for k in range(16):
        a, b, c, d = k >> 3, (k >> 2) & 1, (k >> 1) & 1, k & 1
        if not with_meta:
            a, b, c, d = b, a, d, c
        out, at = outs[a], c * 4 + b * 2 + d
        out[at, 0:PATCH, :] = acc[4 * k + 1, PAD : PAD + PATCH, :]
        out[at, PATCH : 2 * PATCH, :] = acc[4 * k + 2, PAD : PAD + PATCH, :]
        if with_meta:
            for slot in range(CAP):
                out[at, 2 * PATCH + 8 * slot : 2 * PATCH + 8 * slot + 8, :] = meta[k * CAP + slot]


def warp(with_meta, *args):
    smem, vmem = pl.BlockSpec(memory_space=pltpu.SMEM), pl.BlockSpec(memory_space=pltpu.VMEM)
    rows = 2 * PATCH + META if with_meta else 2 * PATCH
    outs, specs = [jax.ShapeDtypeStruct((8, rows, TS), F32)] * 2, [vmem] * 2
    scratch = [
        pltpu.VMEM((2 * UNROLL, 2, TS + 16, TS), F32),
        pltpu.VMEM((64, 384, TS), F32),
    ]
    if with_meta:
        outs, specs = outs + [jax.ShapeDtypeStruct((2, 128), jnp.int32)], specs + [smem]
        scratch += [
            pltpu.VMEM((16 * CAP, 8, TS), F32),
            pltpu.VMEM((2 * TILES, TS), F32),
        ]
    return pl.pallas_call(
        functools.partial(warp_kernel, with_meta),
        out_shape=outs,
        in_specs=[smem] * (len(args) - 2) + [vmem] * 2,
        out_specs=specs,
        scratch_shapes=scratch,
        compiler_params=pltpu.CompilerParams(vmem_limit_bytes=40 << 20),
        cost_estimate=pl.CostEstimate(flops=WARP_COST, bytes_accessed=8 << 20, transcendentals=0),
        name="warp_meta" if with_meta else "warp",
    )(*args)


def cover_kernel(var, got, coadd_var, safe_ref):
    place_of = lax.broadcasted_iota(jnp.int32, (PATCH, TS), 0).astype(F32)

    def cover(offset, shift):
        u = place_of - offset
        lower = jnp.where((u >= 0.0) & (u <= TS - 1.0), 1.0 - shift, 0.0)
        return lower + jnp.where((u >= 1.0) & (u <= float(TS)), shift, 0.0)

    den = jnp.zeros((PATCH, PATCH), F32)
    for slot in range(CAP):
        at = 2 * PATCH + 8 * slot
        fields = var[at : at + 8, :] + got[at : at + 8, :]
        weight, row, col, frac_row, frac_col = (fields[f : f + 1, :] for f in range(5))
        down, across = cover(row, frac_row) * weight, cover(col, frac_col)
        den += lax.dot_general(
            down, across, (((1,), (1,)), ((), ())), precision=lax.Precision.HIGHEST, preferred_element_type=F32
        )
    safe = jnp.maximum(den, 1.0)
    safe_ref[...] = safe
    for half in range(2):
        rows, lanes = slice(half * PATCH, (half + 1) * PATCH), slice(half * TS, (half + 1) * TS)
        part = safe[:, lanes]
        coadd_var[:, lanes] = (var[rows, :] + got[rows, :]) / (part * part)


def divide_kernel(num, got, safe, coadd):
    for half in range(2):
        rows, lanes = slice(half * PATCH, (half + 1) * PATCH), slice(half * TS, (half + 1) * TS)
        coadd[:, lanes] = (num[rows, :] + got[rows, :]) / safe[:, lanes]


def finish(kernel, name, outs, *args):
    vmem = pl.BlockSpec(memory_space=pltpu.VMEM)
    return pl.pallas_call(
        kernel,
        out_shape=[jax.ShapeDtypeStruct((PATCH, PATCH), F32)] * outs,
        in_specs=[vmem] * len(args),
        out_specs=[vmem] * outs,
        compiler_params=pltpu.CompilerParams(vmem_limit_bytes=8 << 20),
        cost_estimate=pl.CostEstimate(flops=1_000_000_000, bytes_accessed=1 << 20, transcendentals=0),
        name=name,
    )(*args)


EDGES = (((0, 1), (1, 0), (2, 3), (3, 2)), ((1, 2), (2, 1), (3, 0), (0, 3)))


def over_patch(axis, edge):
    pairs = []
    for a, b in EDGES[edge]:
        for other in range(4):
            for core in range(2):
                src, dst = ((a, other), (b, other)) if axis == core else ((other, a), (other, b))
                pairs.append((src[0] * 8 + src[1] * 2 + core, dst[0] * 8 + dst[1] * 2 + core))
    return pairs


def over_visit(edge):
    return [
        (a * 32 + 2 * chip + core, b * 32 + 2 * chip + core)
        for core in range(2)
        for a, b in EDGES[edge ^ core]
        for chip in range(16)
    ]


def halve(keep, send, order, ahead=()):
    left_over = []
    for step, (axis, edge) in enumerate(order):
        got = lax.ppermute(send, "patch", over_patch(axis, edge))
        if step < len(ahead):
            got, _ = lax.optimization_barrier((got, ahead[step]))
        if step < 3:
            n = 8 >> (step + 1)
            keep, send = keep[:n] + got[:n], keep[n:] + got[n:]
            left_over.append(send)
        else:
            keep = keep[0] + got[0]
            left_over.append(keep)
    return keep, left_over


def double(x):
    x = x + lax.ppermute(x, ("visit", "patch"), over_visit(0))
    return x, lax.ppermute(x, ("visit", "patch"), over_visit(1))


def shards(image, variance, intersections, boxes, shifts, basis_ids, coefs, taps):
    swap = [(i, i ^ 1) for i in range(32)]
    other_variance = lax.ppermute(variance, "patch", swap)
    table = pack(intersections, boxes, shifts)
    other_table = lax.ppermute(table, "patch", swap)
    matched = match(basis_ids, coefs, taps, image, variance)
    matched, other_table = lax.optimization_barrier((matched, other_table))
    other_matched = lax.ppermute(matched, "patch", swap)
    var_keep, var_send, slots = warp(True, table, other_table, variance, other_variance)
    num_keep, num_send = warp(False, slots, table, other_table, matched, other_matched)
    var, ahead = halve(var_keep, var_send, ((0, 0), (1, 0), (0, 1), (1, 1)))
    num, _ = halve(num_keep, num_send, ((0, 1), (1, 1), (0, 0), (1, 0)), ahead)
    var, num = double(var), double(num)
    coadd_var, safe = finish(cover_kernel, "cover", 2, *var)
    (coadd,) = finish(divide_kernel, "divide", 1, *num, safe)
    return coadd, coadd_var


def solution(mesh):
    split_spec = ("visit", "patch")
    in_specs = (
        P(split_spec, None, None),
        P(split_spec, None, None),
        P(split_spec, None),
        P(split_spec, None, None),
        P(split_spec, None, None),
        P(split_spec, None),
        P(split_spec, None),
        P(),
    )
    out_specs = (P("patch", None), P("patch", None))
    return jax.shard_map(shards, mesh=mesh, in_specs=in_specs, out_specs=out_specs, check_vma=False)
```

```python
import functools

import jax
import jax.numpy as jnp
from jax import lax
from jax.experimental import pallas as pl
from jax.experimental.pallas import tpu as pltpu
from jax.sharding import PartitionSpec as P

TS = 128
PATCH = 256
NB = 3
NBASIS = 8
HALF = 20
TILES = 32
ROUTES = 2 * TILES
CAP = 3
META = 24
PAD = 64
F32 = jnp.float32
BF16 = jnp.bfloat16

EMPTY = 1 << 24
UNROLL = 2
MATCH_UNROLL = 8
CHUNKS = 4
MATCH_COST = 100_000_000_000
WARP_COST = 10_000_000_000


def split(x):
    high = x.astype(BF16)
    return high, (x - high.astype(F32)).astype(BF16)


def here():
    patch = lax.axis_index("patch")
    z, y = patch >> 3, (patch >> 1) & 3
    return z, y, patch & 1, lax.axis_index("visit") * 16 + z * 4 + y


def place_code(z, y, core):
    first, second = jnp.where(core == 0, z, y), jnp.where(core == 0, y, z)
    first, second = first ^ (first >> 1), second ^ (second >> 1)
    return ((first & 1) << 3) | ((first >> 1) << 2) | ((second & 1) << 1) | (second >> 1)


def pack_kernel(intersections, boxes, shifts, out):
    z, y, _, _ = here()
    out[...] = jnp.zeros_like(out)
    earlier_item = lax.broadcasted_iota(jnp.int32, (TILES, TILES), 0)
    item = lax.broadcasted_iota(jnp.int32, (TILES, TILES), 1)
    dest = [intersections[route : route + 1, :] for route in range(2)]

    def earlier(rows):
        columns = [jnp.sum(jnp.where(earlier_item == item, row, 0), axis=1, keepdims=True) for row in rows]
        counts = []
        for route, row in enumerate(rows):
            same = jnp.where((columns[route] == row) & (earlier_item < item), 1, 0)
            if route == 1:
                same = same + jnp.where(columns[0] == row, 1, 0)
            counts.append(jnp.sum(same, axis=0, keepdims=True))
        return counts

    slots, places = earlier(dest), earlier([d & 1 for d in dest])
    for route in range(2):
        d = dest[route]
        code = place_code(d >> 3, (d >> 1) & 3, d & 1) ^ place_code(z, y, d & 1)
        out[route : route + 1, 0:TILES] = (code + (slots[route] << 4) + ((d & 1) << 8)).astype(F32)
        out[10 + route : 11 + route, 0:TILES] = places[route].astype(F32)
        out[2 + 2 * route : 4 + 2 * route, 0:TILES] = boxes[route].astype(F32)
        out[6 + 2 * route : 8 + 2 * route, 0:TILES] = shifts[route]
    second = jnp.sum(intersections[...] & 1).astype(F32)
    lane = lax.broadcasted_iota(jnp.int32, (1, TS), 1)
    out[12:13, :] = jnp.where(lane == 0, ROUTES - second, second)


def pack(intersections, boxes, shifts):
    vmem = pl.BlockSpec(memory_space=pltpu.VMEM)
    return pl.pallas_call(
        pack_kernel,
        out_shape=jax.ShapeDtypeStruct((16, TS), F32),
        in_specs=[vmem] * 3,
        out_specs=vmem,
        name="pack",
    )(intersections.T, boxes.transpose(1, 2, 0), shifts.transpose(1, 2, 0))


def match_kernel(
    basis_ids, coefs, taps_hbm, image_hbm, variance_hbm, out, taps, line, row_mats, col_mats, image, variance, sems, taps_sem
):
    size = TILES // CHUNKS
    copies = [
        [
            pltpu.make_async_copy(source.at[pl.ds(c * size, size)], target.at[pl.ds(c * size, size)], sems.at[i, c])
            for i, (source, target) in enumerate(((image_hbm, image), (variance_hbm, variance)))
        ]
        for c in range(CHUNKS)
    ]
    fetch = pltpu.make_async_copy(taps_hbm, taps, taps_sem)
    fetch.start()
    for pair in copies:
        for copy in pair:
            copy.start()
    i = lax.broadcasted_iota(jnp.int32, (TS, TS), 0)
    k = lax.broadcasted_iota(jnp.int32, (TS, TS), 1)
    near = jnp.abs(i - k) <= HALF
    none = jnp.zeros((TS, TS), BF16)
    line[...] = jnp.zeros_like(line)
    fetch.wait()
    for b in range(NBASIS):
        line[2 * b : 2 * b + 2, 0 : 2 * HALF + 1] = taps[b]
    line[...] = pltpu.roll(line[...], TS - HALF, 1)

    def square(high, low):
        return jnp.concatenate([jnp.concatenate([high, low], 1), jnp.concatenate([high, none], 1)], 0)

    for b in range(NBASIS):
        for side in range(2):
            band = jnp.broadcast_to(line[2 * b + side : 2 * b + side + 1, :], (TS, TS))
            band = jnp.where(near, pltpu.roll(band, 0, 1, stride=1, stride_axis=0), 0.0)
            if side == 0:
                row_mats[b] = jnp.concatenate(split(band.T), 1)
            else:
                col_mats[b] = square(*split(band))

    for c in range(CHUNKS):
        for copy in copies[c]:
            copy.wait()

        @pl.loop(c * size, (c + 1) * size, step=MATCH_UNROLL)
        def _(first):
            for t in [first + u for u in range(MATCH_UNROLL)]:
                weight = float(TS * TS) / jnp.sum(variance[t], axis=(0, 1), keepdims=True)
                pixels = square(*split(image[t]))
                total = None
                for j in range(NB):
                    basis = basis_ids[j, t]
                    p = jnp.dot(row_mats[basis], pixels, preferred_element_type=F32)
                    part = (p[:, :TS] + p[:, TS:]) * coefs[j, t]
                    p = jnp.dot(jnp.concatenate(split(part), 1), col_mats[basis], preferred_element_type=F32)
                    total = p if total is None else total + p
                out[t] = (total[:, :TS] + total[:, TS:]) * weight


def match(basis_ids, coefs, taps, image, variance):
    vmem, hbm = pl.BlockSpec(memory_space=pltpu.VMEM), pl.BlockSpec(memory_space=pltpu.HBM)
    return pl.pallas_call(
        match_kernel,
        out_shape=jax.ShapeDtypeStruct((TILES, TS, TS), F32),
        in_specs=[pl.BlockSpec(memory_space=pltpu.SMEM)] * 2 + [hbm] * 3,
        out_specs=vmem,
        scratch_shapes=[
            pltpu.VMEM((NBASIS, 2, 2 * HALF + 1), F32),
            pltpu.VMEM((2 * NBASIS, TS), F32),
            pltpu.VMEM((NBASIS, TS, 2 * TS), BF16),
            pltpu.VMEM((NBASIS, 2 * TS, 2 * TS), BF16),
            pltpu.VMEM((TILES, TS, TS), F32),
            pltpu.VMEM((TILES, TS, TS), F32),
            pltpu.SemaphoreType.DMA((2, CHUNKS)),
            pltpu.SemaphoreType.DMA,
        ],
        compiler_params=pltpu.CompilerParams(vmem_limit_bytes=40 << 20),
        cost_estimate=pl.CostEstimate(flops=MATCH_COST, bytes_accessed=6 << 20, transcendentals=0),
        name="match",
    )(*(pltpu.with_memory_space_constraint(x, pltpu.HBM) for x in (basis_ids.T, coefs.T, taps, image, variance)))


def warp_kernel(with_meta, *refs):
    if with_meta:
        own, other, own_tiles, other_tiles = refs[:4]
        outs, slots = refs[4:8], refs[8]
        stage, acc, meta, weights = refs[9:]
    else:
        slots, own, other, own_tiles, other_tiles = refs[:5]
        outs = refs[5:9]
        stage, acc = refs[9:]
    lane = lax.broadcasted_iota(jnp.int32, (8, TS), 1)
    stage[:, :, 0:8, :] = jnp.zeros((2 * UNROLL, 2, 8, TS), F32)
    stage[:, :, 8 + TS :, :] = jnp.zeros((2 * UNROLL, 2, 8, TS), F32)
    for k in range(16):
        for side in (1, 2):
            acc[4 * k + side, PAD : PAD + PATCH, :] = jnp.zeros((PATCH, TS), F32)

    if with_meta:
        _, _, core, chip = here()
        meta[...] = jnp.zeros_like(meta)

        @pl.loop(0, TILES, step=8)
        def _(first):
            for side, table, tiles in ((0, own, own_tiles), (1, other, other_tiles)):
                for route in range(2):
                    for t in [first + u for u in range(8)]:
                        what = table[route, t].astype(jnp.int32)
                        at = jnp.where((what >> 8) == core, table[10 + route, t].astype(jnp.int32) + 1, 127)
                        slots[side, at] = (what << 8) + (2 * t + route)
                sums = jnp.concatenate([jnp.sum(tiles[first + u], axis=0, keepdims=True) for u in range(8)], 0)
                sums = jnp.sum(sums, axis=1, keepdims=True)
                at = pl.multiple_of(side * TILES + first, 8)
                weights[pl.ds(at, 8), :] = jnp.broadcast_to(float(TS * TS) / sums, (8, TS))

        for side, table in ((0, own), (1, other)):
            n = table[12, core].astype(jnp.int32)
            slots[side, 0] = n
            for u in range(3 * UNROLL):
                slots[side, 1 + n + u] = EMPTY

    def place(entry, u, side, table, tiles):
        item, k, slot = entry & 255, (entry >> 8) & 15, (entry >> 12) & 3
        t, route = item >> 1, item & 1
        row, col = table[2 + 2 * route, t].astype(jnp.int32), table[3 + 2 * route, t].astype(jnp.int32)
        frac_row, frac_col = table[6 + 2 * route, t], table[7 + 2 * route, t]
        real = jnp.where(entry >= EMPTY, 0.0, 1.0)
        near, far = jnp.full((8, TS), (1.0 - frac_col) * real), jnp.full((8, TS), frac_col * real)
        if with_meta:
            weight = jnp.broadcast_to(weights[pl.ds(side * TILES + t, 1), :], (8, TS))
            field = lax.broadcasted_iota(jnp.int32, (8, TS), 0)
            value = jnp.where(field == 1, row.astype(F32), weight)
            value = jnp.where(field == 2, col.astype(F32), value)
            value = jnp.where(field == 3, frac_row, value)
            value = jnp.where(field == 4, frac_col, value)
            value = jnp.where((field < 5) & (lane == 2 * chip + side), value * real, 0.0)
            meta[k * CAP + slot] += value
            near, far = near * (weight * weight), far * (weight * weight)
        turn = (col + TS) & (TS - 1)
        here = jnp.where(lane >= turn, near, 0.0)
        here_next = jnp.where(lane >= turn + 1, far, 0.0)
        over, over_next = near - here, far - here_next
        tile = tiles[t]
        r0 = pltpu.roll(tile, turn, 1).reshape(TS // 8, 8, TS)
        r1 = pltpu.roll(tile, (turn + 1) & (TS - 1), 1).reshape(TS // 8, 8, TS)
        stage[u, 0, 8 : 8 + TS, :] = (r0 * here + r1 * here_next).reshape(TS, TS)
        stage[u, 1, 8 : 8 + TS, :] = (r0 * over + r1 * over_next).reshape(TS, TS)
        return 4 * k + ((col + TS) >> 7), row + PAD, frac_row

    def add_rows(u, first, row, frac_row):
        down = row & 7
        base = pl.multiple_of((row >> 3) * 8, 8)
        for side in range(2):
            upper = stage[u, side, pl.ds(8 - down, TS + 8), :]
            lower = stage[u, side, pl.ds(7 - down, TS + 8), :]
            acc[first + side, pl.ds(base, TS + 8), :] += upper * (1.0 - frac_row) + lower * frac_row

    for side, table, tiles in ((0, own, own_tiles), (1, other, other_tiles)):
        start = [place(slots[side, 1 + u], u, side, table, tiles) for u in range(UNROLL)]

        def body(m, placed, side=side, table=table, tiles=tiles):
            for half in range(2):
                group = 2 * m + half + 1
                then = [
                    place(slots[side, 1 + group * UNROLL + u], UNROLL * (1 - half) + u, side, table, tiles)
                    for u in range(UNROLL)
                ]
                for u in range(UNROLL):
                    add_rows(UNROLL * half + u, *placed[u])
                placed = then
            return placed

        lax.fori_loop(0, (slots[side, 0] + 2 * UNROLL - 1) // (2 * UNROLL), body, start)

    for k in range(16):
        a, b, c, d = k >> 3, (k >> 2) & 1, (k >> 1) & 1, k & 1
        rest = 2 * c + d if with_meta else 2 * d + c
        left, right = outs[a], outs[2 + b]
        left[4 * b + rest, 0:PATCH, :] = acc[4 * k + 1, PAD : PAD + PATCH, :]
        right[4 * a + rest, :, :] = acc[4 * k + 2, PAD : PAD + PATCH, :]
        if with_meta:
            for slot in range(CAP):
                left[4 * b + rest, PATCH + 8 * slot : PATCH + 8 * slot + 8, :] = meta[k * CAP + slot]


def warp(with_meta, *args):
    smem, vmem = pl.BlockSpec(memory_space=pltpu.SMEM), pl.BlockSpec(memory_space=pltpu.VMEM)
    left = jax.ShapeDtypeStruct((8, PATCH + META if with_meta else PATCH, TS), F32)
    right = jax.ShapeDtypeStruct((8, PATCH, TS), F32)
    outs, specs = [left, left, right, right], [vmem] * 4
    scratch = [
        pltpu.VMEM((2 * UNROLL, 2, TS + 16, TS), F32),
        pltpu.VMEM((64, 384, TS), F32),
    ]
    if with_meta:
        outs, specs = outs + [jax.ShapeDtypeStruct((2, 128), jnp.int32)], specs + [smem]
        scratch += [
            pltpu.VMEM((16 * CAP, 8, TS), F32),
            pltpu.VMEM((2 * TILES, TS), F32),
        ]
    return pl.pallas_call(
        functools.partial(warp_kernel, with_meta),
        out_shape=outs,
        in_specs=[smem] * (len(args) - 2) + [vmem] * 2,
        out_specs=specs,
        scratch_shapes=scratch,
        compiler_params=pltpu.CompilerParams(vmem_limit_bytes=40 << 20),
        cost_estimate=pl.CostEstimate(flops=WARP_COST, bytes_accessed=8 << 20, transcendentals=0),
        name="warp_meta" if with_meta else "warp",
    )(*args)


def cover_kernel(var, got, coadd_var, safe_ref):
    place_of = lax.broadcasted_iota(jnp.int32, (PATCH, TS), 0).astype(F32)

    def cover(offset, shift):
        u = place_of - offset
        lower = jnp.where((u >= 0.0) & (u <= TS - 1.0), 1.0 - shift, 0.0)
        return lower + jnp.where((u >= 1.0) & (u <= float(TS)), shift, 0.0)

    den = jnp.zeros((PATCH, PATCH), F32)
    for slot in range(CAP):
        at = PATCH + 8 * slot
        fields = var[at : at + 8, :] + got[at : at + 8, :]
        weight, row, col, frac_row, frac_col = (fields[f : f + 1, :] for f in range(5))
        down, across = cover(row, frac_row) * weight, cover(col, frac_col)
        den += lax.dot_general(
            down, across, (((1,), (1,)), ((), ())), precision=lax.Precision.HIGHEST, preferred_element_type=F32
        )
    safe = jnp.maximum(den, 1.0)
    safe_ref[...] = safe
    for half in range(2):
        lo = half * (PATCH + META)
        rows, lanes = slice(lo, lo + PATCH), slice(half * TS, (half + 1) * TS)
        part = safe[:, lanes]
        coadd_var[:, lanes] = (var[rows, :] + got[rows, :]) / (part * part)


def divide_kernel(num, got, safe, coadd):
    for half in range(2):
        rows, lanes = slice(half * PATCH, (half + 1) * PATCH), slice(half * TS, (half + 1) * TS)
        coadd[:, lanes] = (num[rows, :] + got[rows, :]) / safe[:, lanes]


def finish(kernel, name, outs, *args):
    vmem = pl.BlockSpec(memory_space=pltpu.VMEM)
    return pl.pallas_call(
        kernel,
        out_shape=[jax.ShapeDtypeStruct((PATCH, PATCH), F32)] * outs,
        in_specs=[vmem] * len(args),
        out_specs=[vmem] * outs,
        compiler_params=pltpu.CompilerParams(vmem_limit_bytes=8 << 20),
        cost_estimate=pl.CostEstimate(flops=1_000_000_000, bytes_accessed=1 << 20, transcendentals=0),
        name=name,
    )(*args)


EDGES = (((0, 1), (1, 0), (2, 3), (3, 2)), ((1, 2), (2, 1), (3, 0), (0, 3)))


def over_patch(axis, edge):
    pairs = []
    for a, b in EDGES[edge]:
        for other in range(4):
            for core in range(2):
                src, dst = ((a, other), (b, other)) if axis == core else ((other, a), (other, b))
                pairs.append((src[0] * 8 + src[1] * 2 + core, dst[0] * 8 + dst[1] * 2 + core))
    return pairs


def over_visit(edge):
    return [
        (a * 32 + 2 * chip + core, b * 32 + 2 * chip + core)
        for core in range(2)
        for a, b in EDGES[edge ^ core]
        for chip in range(16)
    ]


def halve(left_keep, left_send, right_keep, right_send, last, ahead=()):
    def after(step, *got):
        return lax.optimization_barrier((*got, *ahead[step]))[: len(got)] if step < len(ahead) else got

    left, right = after(
        0, lax.ppermute(left_send, "patch", over_patch(0, 0)), lax.ppermute(right_send, "patch", over_patch(0, 1))
    )
    left_keep, left_send = left_keep[:4] + left[:4], left_keep[4:] + left[4:]
    right_keep, right_send = right_keep[:4] + right[:4], right_keep[4:] + right[4:]
    left_over = [(left_send, right_send)]
    left, right = after(
        1, lax.ppermute(left_send, "patch", over_patch(0, 1)), lax.ppermute(right_send, "patch", over_patch(0, 0))
    )
    keep, send = (
        jnp.concatenate([left_keep[part] + left[part], right_keep[part] + right[part]], 1)
        for part in (slice(0, 2), slice(2, 4))
    )
    left_over.append((send,))
    (got,) = after(2, lax.ppermute(send, "patch", over_patch(1, last)))
    keep, send = keep[:1] + got[:1], keep[1:] + got[1:]
    left_over.append((send,))
    (got,) = after(3, lax.ppermute(send, "patch", over_patch(1, 1 - last)))
    left_over.append((keep[0] + got[0],))
    return left_over[-1][0], left_over


def double(x):
    x = x + lax.ppermute(x, ("visit", "patch"), over_visit(0))
    return x, lax.ppermute(x, ("visit", "patch"), over_visit(1))


def shards(image, variance, intersections, boxes, shifts, basis_ids, coefs, taps):
    swap = [(i, i ^ 1) for i in range(32)]
    other_variance = lax.ppermute(variance, "patch", swap)
    table = pack(intersections, boxes, shifts)
    other_table = lax.ppermute(table, "patch", swap)
    matched = match(basis_ids, coefs, taps, image, variance)
    matched, other_table = lax.optimization_barrier((matched, other_table))
    other_matched = lax.ppermute(matched, "patch", swap)
    *var, slots = warp(True, table, other_table, variance, other_variance)
    num = warp(False, slots, table, other_table, matched, other_matched)
    var, ahead = halve(*var, 0)
    num, _ = halve(*num, 1, ahead)
    var, num = double(var), double(num)
    coadd_var, safe = finish(cover_kernel, "cover", 2, *var)
    (coadd,) = finish(divide_kernel, "divide", 1, *num, safe)
    return coadd, coadd_var


def solution(mesh):
    split_spec = ("visit", "patch")
    in_specs = (
        P(split_spec, None, None),
        P(split_spec, None, None),
        P(split_spec, None),
        P(split_spec, None, None),
        P(split_spec, None, None),
        P(split_spec, None),
        P(split_spec, None),
        P(),
    )
    out_specs = (P("patch", None), P("patch", None))
    return jax.shard_map(shards, mesh=mesh, in_specs=in_specs, out_specs=out_specs, check_vma=False)
```

```python
import functools

import jax
import jax.numpy as jnp
from jax import lax
from jax.experimental import pallas as pl
from jax.experimental.pallas import tpu as pltpu
from jax.sharding import PartitionSpec as P

TS = 128
PATCH = 256
NB = 3
NBASIS = 8
HALF = 20
TILES = 32
ROUTES = 2 * TILES
CAP = 3
META = 24
PITCH = TS + 8
PAD = 64
F32 = jnp.float32
BF16 = jnp.bfloat16

EMPTY = 1 << 24
UNROLL = 8
MATCH_UNROLL = 16
CHUNKS = 2
MATCH_COST = 100_000_000_000
WARP_COST = 10_000_000_000


def split(x):
    high = x.astype(BF16)
    return high, (x - high.astype(F32)).astype(BF16)


def here():
    patch = lax.axis_index("patch")
    z, y = patch >> 3, (patch >> 1) & 3
    return z, y, patch & 1, lax.axis_index("visit") * 16 + z * 4 + y


def place_code(z, y, core):
    first, second = jnp.where(core == 0, z, y), jnp.where(core == 0, y, z)
    first, second = first ^ (first >> 1), second ^ (second >> 1)
    return ((first & 1) << 3) | ((first >> 1) << 2) | ((second & 1) << 1) | (second >> 1)


def pack_kernel(intersections, boxes, shifts, out):
    z, y, _, _ = here()
    out[...] = jnp.zeros_like(out)
    earlier_item = lax.broadcasted_iota(jnp.int32, (TILES, TILES), 0)
    item = lax.broadcasted_iota(jnp.int32, (TILES, TILES), 1)
    dest = [intersections[route : route + 1, :] for route in range(2)]

    def earlier(rows):
        columns = [jnp.sum(jnp.where(earlier_item == item, row, 0), axis=1, keepdims=True) for row in rows]
        counts = []
        for route, row in enumerate(rows):
            same = jnp.where((columns[route] == row) & (earlier_item < item), 1, 0)
            if route == 1:
                same = same + jnp.where(columns[0] == row, 1, 0)
            counts.append(jnp.sum(same, axis=0, keepdims=True))
        return counts

    slots, places = earlier(dest), earlier([d & 1 for d in dest])
    for route in range(2):
        d = dest[route]
        code = place_code(d >> 3, (d >> 1) & 3, d & 1) ^ place_code(z, y, d & 1)
        out[route : route + 1, 0:TILES] = (code + (slots[route] << 4) + ((d & 1) << 8)).astype(F32)
        out[10 + route : 11 + route, 0:TILES] = places[route].astype(F32)
        out[2 + 2 * route : 4 + 2 * route, 0:TILES] = boxes[route].astype(F32)
        out[6 + 2 * route : 8 + 2 * route, 0:TILES] = shifts[route]
    second = jnp.sum(intersections[...] & 1).astype(F32)
    lane = lax.broadcasted_iota(jnp.int32, (1, TS), 1)
    out[12:13, :] = jnp.where(lane == 0, ROUTES - second, second)


def pack(intersections, boxes, shifts):
    vmem = pl.BlockSpec(memory_space=pltpu.VMEM)
    return pl.pallas_call(
        pack_kernel,
        out_shape=jax.ShapeDtypeStruct((16, TS), F32),
        in_specs=[vmem] * 3,
        out_specs=vmem,
        name="pack",
    )(intersections.T, boxes.transpose(1, 2, 0), shifts.transpose(1, 2, 0))


def match_kernel(
    basis_ids, coefs, taps_hbm, image_hbm, out, taps, line, row_mats, col_mats, image, sems, taps_sem
):
    size = TILES // CHUNKS
    copies = [
        pltpu.make_async_copy(image_hbm.at[pl.ds(c * size, size)], image.at[pl.ds(c * size, size)], sems.at[c])
        for c in range(CHUNKS)
    ]
    fetch = pltpu.make_async_copy(taps_hbm, taps, taps_sem)
    fetch.start()
    for copy in copies:
        copy.start()
    i = lax.broadcasted_iota(jnp.int32, (TS, TS), 0)
    k = lax.broadcasted_iota(jnp.int32, (TS, TS), 1)
    near = jnp.abs(i - k) <= HALF
    none = jnp.zeros((TS, TS), BF16)
    line[...] = jnp.zeros_like(line)
    fetch.wait()
    for b in range(NBASIS):
        line[2 * b : 2 * b + 2, 0 : 2 * HALF + 1] = taps[b]
    line[...] = pltpu.roll(line[...], TS - HALF, 1)

    def square(high, low):
        return jnp.concatenate([jnp.concatenate([high, low], 1), jnp.concatenate([high, none], 1)], 0)

    for b in range(NBASIS):
        for side in range(2):
            band = jnp.broadcast_to(line[2 * b + side : 2 * b + side + 1, :], (TS, TS))
            band = jnp.where(near, pltpu.roll(band, 0, 1, stride=1, stride_axis=0), 0.0)
            if side == 0:
                row_mats[b] = jnp.concatenate(split(band.T), 1)
            else:
                col_mats[b] = square(*split(band))

    out[TILES * PITCH :, :] = jnp.zeros((8, TS), F32)
    for c in range(CHUNKS):
        copies[c].wait()

        @pl.loop(c * size, (c + 1) * size, step=MATCH_UNROLL)
        def _(first):
            for t in [first + u for u in range(MATCH_UNROLL)]:
                pixels = square(*split(image[t]))
                total = None
                for j in range(NB):
                    basis = basis_ids[j, t]
                    p = jnp.dot(row_mats[basis], pixels, preferred_element_type=F32)
                    part = (p[:, :TS] + p[:, TS:]) * coefs[j, t]
                    p = jnp.dot(jnp.concatenate(split(part), 1), col_mats[basis], preferred_element_type=F32)
                    total = p if total is None else total + p
                at = pl.multiple_of(t * PITCH, 8)
                out[pl.ds(at, 8), :] = jnp.zeros((8, TS), F32)
                out[pl.ds(at + 8, TS), :] = total[:, :TS] + total[:, TS:]


def match(basis_ids, coefs, taps, image):
    vmem, hbm = pl.BlockSpec(memory_space=pltpu.VMEM), pl.BlockSpec(memory_space=pltpu.HBM)
    return pl.pallas_call(
        match_kernel,
        out_shape=jax.ShapeDtypeStruct((TILES * PITCH + 8, TS), F32),
        in_specs=[pl.BlockSpec(memory_space=pltpu.SMEM)] * 2 + [hbm] * 2,
        out_specs=vmem,
        scratch_shapes=[
            pltpu.VMEM((NBASIS, 2, 2 * HALF + 1), F32),
            pltpu.VMEM((2 * NBASIS, TS), F32),
            pltpu.VMEM((NBASIS, TS, 2 * TS), BF16),
            pltpu.VMEM((NBASIS, 2 * TS, 2 * TS), BF16),
            pltpu.VMEM((TILES, TS, TS), F32),
            pltpu.SemaphoreType.DMA((CHUNKS,)),
            pltpu.SemaphoreType.DMA,
        ],
        compiler_params=pltpu.CompilerParams(vmem_limit_bytes=40 << 20),
        cost_estimate=pl.CostEstimate(flops=MATCH_COST, bytes_accessed=6 << 20, transcendentals=0),
        name="match",
    )(*(pltpu.with_memory_space_constraint(x, pltpu.HBM) for x in (basis_ids.T, coefs.T, taps, image)))


def warp_kernel(with_meta, *refs):
    if with_meta:
        own, other, own_raw, other_raw = refs[:4]
        outs, slots, weights = refs[4:8], refs[8], refs[9]
        acc, meta, own_tiles, other_tiles = refs[10:]
    else:
        slots, own, other, weights, own_tiles, other_tiles = refs[:6]
        outs, acc = refs[6:10], refs[10]
    lane = lax.broadcasted_iota(jnp.int32, (8, TS), 1)
    for k in range(16):
        for side in (1, 2):
            acc[4 * k + side, PAD : PAD + PATCH, :] = jnp.zeros((PATCH, TS), F32)

    if with_meta:
        _, _, core, chip = here()
        meta[...] = jnp.zeros_like(meta)

        @pl.loop(0, TILES, step=8)
        def _(first):
            for side, table, raw, tiles in ((0, own, own_raw, own_tiles), (1, other, other_raw, other_tiles)):
                for route in range(2):
                    for t in [first + u for u in range(8)]:
                        what = table[route, t].astype(jnp.int32)
                        at = jnp.where((what >> 8) == core, table[10 + route, t].astype(jnp.int32) + 1, 127)
                        slots[side, at] = (what << 8) + (2 * t + route)
                sums = []
                for t in [first + u for u in range(8)]:
                    tile = raw[t]
                    at = pl.multiple_of(t * PITCH, 8)
                    tiles[pl.ds(at, 8), :] = jnp.zeros((8, TS), F32)
                    tiles[pl.ds(at + 8, TS), :] = tile
                    sums.append(jnp.sum(tile, axis=0, keepdims=True))
                sums = jnp.sum(jnp.concatenate(sums, 0), axis=1, keepdims=True)
                at = pl.multiple_of(side * TILES + first, 8)
                weights[pl.ds(at, 8), :] = jnp.broadcast_to(float(TS * TS) / sums, (8, TS))

        for side, table in ((0, own), (1, other)):
            n = table[12, core].astype(jnp.int32)
            slots[side, 0] = n
            for u in range(UNROLL):
                slots[side, 1 + n + u] = EMPTY
        for tiles in (own_tiles, other_tiles):
            tiles[TILES * PITCH :, :] = jnp.zeros((8, TS), F32)

    def place(entry, side, table, tiles):
        item, k, slot = entry & 255, (entry >> 8) & 15, (entry >> 12) & 3
        t, route = item >> 1, item & 1
        row, col = table[2 + 2 * route, t].astype(jnp.int32), table[3 + 2 * route, t].astype(jnp.int32)
        frac_row, frac_col = table[6 + 2 * route, t], table[7 + 2 * route, t]
        real = jnp.where(entry >= EMPTY, 0.0, 1.0)
        weight = jnp.broadcast_to(weights[pl.ds(side * TILES + t, 1), :], (8, TS))
        scale = weight * real
        if with_meta:
            field = lax.broadcasted_iota(jnp.int32, (8, TS), 0)
            value = jnp.where(field == 1, row.astype(F32), weight)
            value = jnp.where(field == 2, col.astype(F32), value)
            value = jnp.where(field == 3, frac_row, value)
            value = jnp.where(field == 4, frac_col, value)
            value = jnp.where((field < 5) & (lane == 2 * chip + side), value * real, 0.0)
            meta[k * CAP + slot] += value
            scale = scale * weight
        near, far = scale * (1.0 - frac_col), scale * frac_col
        turn, down = (col + TS) & (TS - 1), (row + PAD) & 7
        here = jnp.where(lane >= turn, near, 0.0)
        here_next = jnp.where(lane >= turn + 1, far, 0.0)
        over, over_next = near - here, far - here_next
        start = t * PITCH + 8 - down
        upper, lower = tiles[pl.ds(start, PITCH), :], tiles[pl.ds(start - 1, PITCH), :]
        rows = upper * (1.0 - frac_row) + lower * frac_row
        r0 = pltpu.roll(rows, turn, 1).reshape(PITCH // 8, 8, TS)
        r1 = pltpu.roll(rows, (turn + 1) & (TS - 1), 1).reshape(PITCH // 8, 8, TS)
        left = (r0 * here + r1 * here_next).reshape(PITCH, TS)
        right = (r0 * over + r1 * over_next).reshape(PITCH, TS)
        return left, right, 4 * k + ((col + TS) >> 7), pl.multiple_of(((row + PAD) >> 3) * 8, 8)

    for side, table, tiles in ((0, own, own_tiles), (1, other, other_tiles)):

        @pl.loop(0, (slots[side, 0] + UNROLL - 1) // UNROLL)
        def _(m, side=side, table=table, tiles=tiles):
            for u in range(UNROLL):
                left, right, first, base = place(slots[side, 1 + m * UNROLL + u], side, table, tiles)
                acc[first, pl.ds(base, PITCH), :] += left
                acc[first + 1, pl.ds(base, PITCH), :] += right

    for k in range(16):
        a, b, c, d = k >> 3, (k >> 2) & 1, (k >> 1) & 1, k & 1
        rest = 2 * c + d if with_meta else 2 * d + c
        left, right = outs[a], outs[2 + b]
        left[4 * b + rest, 0:PATCH, :] = acc[4 * k + 1, PAD : PAD + PATCH, :]
        right[4 * a + rest, :, :] = acc[4 * k + 2, PAD : PAD + PATCH, :]
        if with_meta:
            for slot in range(CAP):
                left[4 * b + rest, PATCH + 8 * slot : PATCH + 8 * slot + 8, :] = meta[k * CAP + slot]


def warp(with_meta, *args):
    smem, vmem = pl.BlockSpec(memory_space=pltpu.SMEM), pl.BlockSpec(memory_space=pltpu.VMEM)
    left = jax.ShapeDtypeStruct((8, PATCH + META if with_meta else PATCH, TS), F32)
    right = jax.ShapeDtypeStruct((8, PATCH, TS), F32)
    outs, specs = [left, left, right, right], [vmem] * 4
    scratch = [pltpu.VMEM((64, 384, TS), F32)]
    if with_meta:
        outs += [jax.ShapeDtypeStruct((2, 128), jnp.int32), jax.ShapeDtypeStruct((2 * TILES, TS), F32)]
        specs += [smem, vmem]
        scratch += [pltpu.VMEM((16 * CAP, 8, TS), F32)] + [pltpu.VMEM((TILES * PITCH + 8, TS), F32)] * 2
    scalars = 2 if with_meta else 3
    return pl.pallas_call(
        functools.partial(warp_kernel, with_meta),
        out_shape=outs,
        in_specs=[smem] * scalars + [vmem] * (len(args) - scalars),
        out_specs=specs,
        scratch_shapes=scratch,
        compiler_params=pltpu.CompilerParams(vmem_limit_bytes=40 << 20),
        cost_estimate=pl.CostEstimate(flops=WARP_COST, bytes_accessed=8 << 20, transcendentals=0),
        name="warp_meta" if with_meta else "warp",
    )(*args)


def cover_kernel(var, got, coadd_var, safe_ref):
    place_of = lax.broadcasted_iota(jnp.int32, (PATCH, TS), 0).astype(F32)

    def cover(offset, shift):
        u = place_of - offset
        lower = jnp.where((u >= 0.0) & (u <= TS - 1.0), 1.0 - shift, 0.0)
        return lower + jnp.where((u >= 1.0) & (u <= float(TS)), shift, 0.0)

    den = jnp.zeros((PATCH, PATCH), F32)
    for slot in range(CAP):
        at = PATCH + 8 * slot
        fields = var[at : at + 8, :] + got[at : at + 8, :]
        weight, row, col, frac_row, frac_col = (fields[f : f + 1, :] for f in range(5))
        down, across = cover(row, frac_row) * weight, cover(col, frac_col)
        den += lax.dot_general(
            down, across, (((1,), (1,)), ((), ())), precision=lax.Precision.HIGHEST, preferred_element_type=F32
        )
    safe = jnp.maximum(den, 1.0)
    safe_ref[...] = safe
    for half in range(2):
        lo = half * (PATCH + META)
        rows, lanes = slice(lo, lo + PATCH), slice(half * TS, (half + 1) * TS)
        part = safe[:, lanes]
        coadd_var[:, lanes] = (var[rows, :] + got[rows, :]) / (part * part)


def divide_kernel(num, got, safe, coadd):
    for half in range(2):
        rows, lanes = slice(half * PATCH, (half + 1) * PATCH), slice(half * TS, (half + 1) * TS)
        coadd[:, lanes] = (num[rows, :] + got[rows, :]) / safe[:, lanes]


def finish(kernel, name, outs, *args):
    vmem = pl.BlockSpec(memory_space=pltpu.VMEM)
    return pl.pallas_call(
        kernel,
        out_shape=[jax.ShapeDtypeStruct((PATCH, PATCH), F32)] * outs,
        in_specs=[vmem] * len(args),
        out_specs=[vmem] * outs,
        compiler_params=pltpu.CompilerParams(vmem_limit_bytes=8 << 20),
        cost_estimate=pl.CostEstimate(flops=1_000_000_000, bytes_accessed=1 << 20, transcendentals=0),
        name=name,
    )(*args)


EDGES = (((0, 1), (1, 0), (2, 3), (3, 2)), ((1, 2), (2, 1), (3, 0), (0, 3)))


def over_patch(axis, edge):
    pairs = []
    for a, b in EDGES[edge]:
        for other in range(4):
            for core in range(2):
                src, dst = ((a, other), (b, other)) if axis == core else ((other, a), (other, b))
                pairs.append((src[0] * 8 + src[1] * 2 + core, dst[0] * 8 + dst[1] * 2 + core))
    return pairs


def over_visit(edge):
    return [
        (a * 32 + 2 * chip + core, b * 32 + 2 * chip + core)
        for core in range(2)
        for a, b in EDGES[edge ^ core]
        for chip in range(16)
    ]


def halve(left_keep, left_send, right_keep, right_send, last, ahead=()):
    def after(step, *got):
        return lax.optimization_barrier((*got, *ahead[step]))[: len(got)] if step < len(ahead) else got

    left, right = after(
        0, lax.ppermute(left_send, "patch", over_patch(0, 0)), lax.ppermute(right_send, "patch", over_patch(0, 1))
    )
    left_keep, left_send = left_keep[:4] + left[:4], left_keep[4:] + left[4:]
    right_keep, right_send = right_keep[:4] + right[:4], right_keep[4:] + right[4:]
    left_over = [(left_send, right_send)]
    left, right = after(
        1, lax.ppermute(left_send, "patch", over_patch(0, 1)), lax.ppermute(right_send, "patch", over_patch(0, 0))
    )
    keep, send = (
        jnp.concatenate([left_keep[part] + left[part], right_keep[part] + right[part]], 1)
        for part in (slice(0, 2), slice(2, 4))
    )
    left_over.append((send,))
    (got,) = after(2, lax.ppermute(send, "patch", over_patch(1, last)))
    keep, send = keep[:1] + got[:1], keep[1:] + got[1:]
    left_over.append((send,))
    (got,) = after(3, lax.ppermute(send, "patch", over_patch(1, 1 - last)))
    left_over.append((keep[0] + got[0],))
    return left_over[-1][0], left_over


def double(x, first):
    x = x + lax.ppermute(x, ("visit", "patch"), over_visit(first))
    return x, lax.ppermute(x, ("visit", "patch"), over_visit(1 - first))


def shards(image, variance, intersections, boxes, shifts, basis_ids, coefs, taps):
    swap = [(i, i ^ 1) for i in range(32)]
    other_variance = lax.ppermute(variance, "patch", swap)
    table = pack(intersections, boxes, shifts)
    other_table = lax.ppermute(table, "patch", swap)
    matched = match(basis_ids, coefs, taps, image)
    matched, other_table = lax.optimization_barrier((matched, other_table))
    other_matched = lax.ppermute(matched, "patch", swap)
    *var, slots, weights = warp(True, table, other_table, variance, other_variance)
    num = warp(False, slots, table, other_table, weights, matched, other_matched)
    var, ahead = halve(*var, 0)
    num, _ = halve(*num, 1, ahead)
    var, num = double(var, 0), double(num, 1)
    coadd_var, safe = finish(cover_kernel, "cover", 2, *var)
    (coadd,) = finish(divide_kernel, "divide", 1, *num, safe)
    return coadd, coadd_var


def solution(mesh):
    split_spec = ("visit", "patch")
    in_specs = (
        P(split_spec, None, None),
        P(split_spec, None, None),
        P(split_spec, None),
        P(split_spec, None, None),
        P(split_spec, None, None),
        P(split_spec, None),
        P(split_spec, None),
        P(),
    )
    out_specs = (P("patch", None), P("patch", None))
    return jax.shard_map(shards, mesh=mesh, in_specs=in_specs, out_specs=out_specs, check_vma=False)
```

```python
import functools

import jax
import jax.numpy as jnp
from jax import lax
from jax.experimental import pallas as pl
from jax.experimental.pallas import tpu as pltpu
from jax.sharding import PartitionSpec as P

TS = 128
PATCH = 256
NB = 3
NBASIS = 8
HALF = 20
TILES = 32
ROUTES = 2 * TILES
CAP = 3
META = 24
PITCH = TS + 8
PAD = 64
F32 = jnp.float32
BF16 = jnp.bfloat16

EMPTY = 1 << 24
UNROLL = 8
MATCH_UNROLL = 16
CHUNKS = 2
MATCH_COST = 100_000_000_000
WARP_COST = 10_000_000_000


def split(x):
    high = x.astype(BF16)
    return high, (x - high.astype(F32)).astype(BF16)


def here():
    patch = lax.axis_index("patch")
    z, y = patch >> 3, (patch >> 1) & 3
    return z, y, patch & 1, lax.axis_index("visit") * 16 + z * 4 + y


def place_code(z, y, core):
    first, second = jnp.where(core == 0, z, y), jnp.where(core == 0, y, z)
    first, second = first ^ (first >> 1), second ^ (second >> 1)
    return ((first & 1) << 3) | ((first >> 1) << 2) | ((second & 1) << 1) | (second >> 1)


def pack_kernel(intersections, boxes, shifts, out):
    z, y, _, _ = here()
    out[...] = jnp.zeros_like(out)
    earlier_item = lax.broadcasted_iota(jnp.int32, (TILES, TILES), 0)
    item = lax.broadcasted_iota(jnp.int32, (TILES, TILES), 1)
    dest = [intersections[route : route + 1, :] for route in range(2)]

    def earlier(rows):
        columns = [jnp.sum(jnp.where(earlier_item == item, row, 0), axis=1, keepdims=True) for row in rows]
        counts = []
        for route, row in enumerate(rows):
            same = jnp.where((columns[route] == row) & (earlier_item < item), 1, 0)
            if route == 1:
                same = same + jnp.where(columns[0] == row, 1, 0)
            counts.append(jnp.sum(same, axis=0, keepdims=True))
        return counts

    slots, places = earlier(dest), earlier([d & 1 for d in dest])
    for route in range(2):
        d = dest[route]
        code = place_code(d >> 3, (d >> 1) & 3, d & 1) ^ place_code(z, y, d & 1)
        out[route : route + 1, 0:TILES] = (code + (slots[route] << 4) + ((d & 1) << 8)).astype(F32)
        out[10 + route : 11 + route, 0:TILES] = places[route].astype(F32)
        out[2 + 2 * route : 4 + 2 * route, 0:TILES] = boxes[route].astype(F32)
        out[6 + 2 * route : 8 + 2 * route, 0:TILES] = shifts[route]
    second = jnp.sum(intersections[...] & 1).astype(F32)
    lane = lax.broadcasted_iota(jnp.int32, (1, TS), 1)
    out[12:13, :] = jnp.where(lane == 0, ROUTES - second, second)


def pack(intersections, boxes, shifts):
    vmem = pl.BlockSpec(memory_space=pltpu.VMEM)
    return pl.pallas_call(
        pack_kernel,
        out_shape=jax.ShapeDtypeStruct((16, TS), F32),
        in_specs=[vmem] * 3,
        out_specs=vmem,
        name="pack",
    )(intersections.T, boxes.transpose(1, 2, 0), shifts.transpose(1, 2, 0))


def match_kernel(
    ids_hbm, coefs_hbm, taps_hbm, image_hbm, out, basis_ids, coefs, taps, line, row_mats, col_mats, image, sems, small_sems
):
    size = TILES // CHUNKS
    copies = [
        pltpu.make_async_copy(image_hbm.at[pl.ds(c * size, size)], image.at[pl.ds(c * size, size)], sems.at[c])
        for c in range(CHUNKS)
    ]
    small = [
        pltpu.make_async_copy(source, target, small_sems.at[i])
        for i, (source, target) in enumerate(((taps_hbm, taps), (ids_hbm, basis_ids), (coefs_hbm, coefs)))
    ]
    for copy in small + copies:
        copy.start()
    i = lax.broadcasted_iota(jnp.int32, (TS, TS), 0)
    k = lax.broadcasted_iota(jnp.int32, (TS, TS), 1)
    near = jnp.abs(i - k) <= HALF
    none = jnp.zeros((TS, TS), BF16)
    line[...] = jnp.zeros_like(line)
    for copy in small:
        copy.wait()
    for b in range(NBASIS):
        line[2 * b : 2 * b + 2, 0 : 2 * HALF + 1] = taps[b]
    line[...] = pltpu.roll(line[...], TS - HALF, 1)

    def square(high, low):
        return jnp.concatenate([jnp.concatenate([high, low], 1), jnp.concatenate([high, none], 1)], 0)

    for b in range(NBASIS):
        for side in range(2):
            band = jnp.broadcast_to(line[2 * b + side : 2 * b + side + 1, :], (TS, TS))
            band = jnp.where(near, pltpu.roll(band, 0, 1, stride=1, stride_axis=0), 0.0)
            if side == 0:
                row_mats[b] = jnp.concatenate(split(band.T), 1)
            else:
                col_mats[b] = square(*split(band))

    out[TILES * PITCH :, :] = jnp.zeros((8, TS), F32)
    for c in range(CHUNKS):
        copies[c].wait()

        @pl.loop(c * size, (c + 1) * size, step=MATCH_UNROLL)
        def _(first):
            for t in [first + u for u in range(MATCH_UNROLL)]:
                pixels = square(*split(image[t]))
                bases = [basis_ids[j, t] for j in range(NB)]
                bands = jnp.concatenate([row_mats[basis] for basis in bases], 0)
                p = jnp.dot(bands, pixels, preferred_element_type=F32)
                p = p[:, :TS] + p[:, TS:]
                parts = [jnp.concatenate(split(p[TS * j : TS * (j + 1)] * coefs[j, t]), 1) for j in range(NB)]
                bands = jnp.concatenate([col_mats[basis] for basis in bases], 0)
                total = jnp.dot(jnp.concatenate(parts, 1), bands, preferred_element_type=F32)
                at = pl.multiple_of(t * PITCH, 8)
                out[pl.ds(at, 8), :] = jnp.zeros((8, TS), F32)
                out[pl.ds(at + 8, TS), :] = total[:, :TS] + total[:, TS:]


def match(basis_ids, coefs, taps, image):
    vmem, hbm = pl.BlockSpec(memory_space=pltpu.VMEM), pl.BlockSpec(memory_space=pltpu.HBM)
    return pl.pallas_call(
        match_kernel,
        out_shape=jax.ShapeDtypeStruct((TILES * PITCH + 8, TS), F32),
        in_specs=[hbm] * 4,
        out_specs=vmem,
        scratch_shapes=[
            pltpu.SMEM((NB, TILES), jnp.int32),
            pltpu.SMEM((NB, TILES), F32),
            pltpu.VMEM((NBASIS, 2, 2 * HALF + 1), F32),
            pltpu.VMEM((2 * NBASIS, TS), F32),
            pltpu.VMEM((NBASIS, TS, 2 * TS), BF16),
            pltpu.VMEM((NBASIS, 2 * TS, 2 * TS), BF16),
            pltpu.VMEM((TILES, TS, TS), F32),
            pltpu.SemaphoreType.DMA((CHUNKS,)),
            pltpu.SemaphoreType.DMA((3,)),
        ],
        compiler_params=pltpu.CompilerParams(vmem_limit_bytes=40 << 20),
        cost_estimate=pl.CostEstimate(flops=MATCH_COST, bytes_accessed=6 << 20, transcendentals=0),
        name="match",
    )(*(pltpu.with_memory_space_constraint(x, pltpu.HBM) for x in (basis_ids.T, coefs.T, taps, image)))


def warp_kernel(with_meta, *refs):
    if with_meta:
        own, other, own_raw, other_raw = refs[:4]
        outs, slots, weights = refs[4:8], refs[8], refs[9]
        acc, meta, own_tiles, other_tiles = refs[10:]
    else:
        slots, own, other, weights, own_tiles, other_tiles = refs[:6]
        outs, acc = refs[6:10], refs[10]
    lane = lax.broadcasted_iota(jnp.int32, (8, TS), 1)
    for k in range(16):
        for side in (1, 2):
            acc[4 * k + side, PAD : PAD + PATCH, :] = jnp.zeros((PATCH, TS), F32)

    if with_meta:
        _, _, core, chip = here()
        meta[...] = jnp.zeros_like(meta)

        @pl.loop(0, TILES, step=8)
        def _(first):
            for side, table, raw, tiles in ((0, own, own_raw, own_tiles), (1, other, other_raw, other_tiles)):
                for route in range(2):
                    for t in [first + u for u in range(8)]:
                        what = table[route, t].astype(jnp.int32)
                        at = jnp.where((what >> 8) == core, table[10 + route, t].astype(jnp.int32) + 1, 127)
                        slots[side, at] = (what << 8) + (2 * t + route)
                sums = []
                for t in [first + u for u in range(8)]:
                    tile = raw[t]
                    at = pl.multiple_of(t * PITCH, 8)
                    tiles[pl.ds(at, 8), :] = jnp.zeros((8, TS), F32)
                    tiles[pl.ds(at + 8, TS), :] = tile
                    sums.append(jnp.sum(tile, axis=0, keepdims=True))
                sums = jnp.sum(jnp.concatenate(sums, 0), axis=1, keepdims=True)
                at = pl.multiple_of(side * TILES + first, 8)
                weights[pl.ds(at, 8), :] = jnp.broadcast_to(float(TS * TS) / sums, (8, TS))

        for side, table in ((0, own), (1, other)):
            n = table[12, core].astype(jnp.int32)
            slots[side, 0] = n
            for u in range(UNROLL):
                slots[side, 1 + n + u] = EMPTY
        for tiles in (own_tiles, other_tiles):
            tiles[TILES * PITCH :, :] = jnp.zeros((8, TS), F32)

    def place(entry, side, table, tiles):
        item, k, slot = entry & 255, (entry >> 8) & 15, (entry >> 12) & 3
        t, route = item >> 1, item & 1
        row, col = table[2 + 2 * route, t].astype(jnp.int32), table[3 + 2 * route, t].astype(jnp.int32)
        frac_row, frac_col = table[6 + 2 * route, t], table[7 + 2 * route, t]
        real = jnp.where(entry >= EMPTY, 0.0, 1.0)
        weight = jnp.broadcast_to(weights[pl.ds(side * TILES + t, 1), :], (8, TS))
        scale = weight * real
        if with_meta:
            field = lax.broadcasted_iota(jnp.int32, (8, TS), 0)
            value = jnp.where(field == 1, row.astype(F32), weight)
            value = jnp.where(field == 2, col.astype(F32), value)
            value = jnp.where(field == 3, frac_row, value)
            value = jnp.where(field == 4, frac_col, value)
            value = jnp.where((field < 5) & (lane == 2 * chip + side), value * real, 0.0)
            meta[k * CAP + slot] += value
            scale = scale * weight
        near, far = scale * (1.0 - frac_col), scale * frac_col
        turn, down = (col + TS) & (TS - 1), (row + PAD) & 7
        here = jnp.where(lane >= turn, near, 0.0)
        here_next = jnp.where(lane >= turn + 1, far, 0.0)
        over, over_next = near - here, far - here_next
        start = t * PITCH + 8 - down
        upper, lower = tiles[pl.ds(start, PITCH), :], tiles[pl.ds(start - 1, PITCH), :]
        rows = upper * (1.0 - frac_row) + lower * frac_row
        r0 = pltpu.roll(rows, turn, 1).reshape(PITCH // 8, 8, TS)
        r1 = pltpu.roll(rows, (turn + 1) & (TS - 1), 1).reshape(PITCH // 8, 8, TS)
        left = (r0 * here + r1 * here_next).reshape(PITCH, TS)
        right = (r0 * over + r1 * over_next).reshape(PITCH, TS)
        return left, right, 4 * k + ((col + TS) >> 7), pl.multiple_of(((row + PAD) >> 3) * 8, 8)

    for side, table, tiles in ((0, own, own_tiles), (1, other, other_tiles)):

        @pl.loop(0, (slots[side, 0] + UNROLL - 1) // UNROLL)
        def _(m, side=side, table=table, tiles=tiles):
            for u in range(UNROLL):
                left, right, first, base = place(slots[side, 1 + m * UNROLL + u], side, table, tiles)
                acc[first, pl.ds(base, PITCH), :] += left
                acc[first + 1, pl.ds(base, PITCH), :] += right

    for k in range(16):
        a, b, c, d = k >> 3, (k >> 2) & 1, (k >> 1) & 1, k & 1
        rest = 2 * c + d if with_meta else 2 * d + c
        left, right = outs[a], outs[2 + b]
        left[4 * b + rest, 0:PATCH, :] = acc[4 * k + 1, PAD : PAD + PATCH, :]
        right[4 * a + rest, :, :] = acc[4 * k + 2, PAD : PAD + PATCH, :]
        if with_meta:
            for slot in range(CAP):
                left[4 * b + rest, PATCH + 8 * slot : PATCH + 8 * slot + 8, :] = meta[k * CAP + slot]


def warp(with_meta, *args):
    smem, vmem = pl.BlockSpec(memory_space=pltpu.SMEM), pl.BlockSpec(memory_space=pltpu.VMEM)
    left = jax.ShapeDtypeStruct((8, PATCH + META if with_meta else PATCH, TS), F32)
    right = jax.ShapeDtypeStruct((8, PATCH, TS), F32)
    outs, specs = [left, left, right, right], [vmem] * 4
    scratch = [pltpu.VMEM((64, 384, TS), F32)]
    if with_meta:
        outs += [jax.ShapeDtypeStruct((2, 128), jnp.int32), jax.ShapeDtypeStruct((2 * TILES, TS), F32)]
        specs += [smem, vmem]
        scratch += [pltpu.VMEM((16 * CAP, 8, TS), F32)] + [pltpu.VMEM((TILES * PITCH + 8, TS), F32)] * 2
    scalars = 2 if with_meta else 3
    return pl.pallas_call(
        functools.partial(warp_kernel, with_meta),
        out_shape=outs,
        in_specs=[smem] * scalars + [vmem] * (len(args) - scalars),
        out_specs=specs,
        scratch_shapes=scratch,
        compiler_params=pltpu.CompilerParams(vmem_limit_bytes=40 << 20),
        cost_estimate=pl.CostEstimate(flops=WARP_COST, bytes_accessed=8 << 20, transcendentals=0),
        name="warp_meta" if with_meta else "warp",
    )(*args)


def cover_kernel(var, got, coadd_var, safe_ref):
    place_of = lax.broadcasted_iota(jnp.int32, (PATCH, TS), 0).astype(F32)

    def cover(offset, shift):
        u = place_of - offset
        lower = jnp.where((u >= 0.0) & (u <= TS - 1.0), 1.0 - shift, 0.0)
        return lower + jnp.where((u >= 1.0) & (u <= float(TS)), shift, 0.0)

    downs, acrosses = [], []
    for slot in range(CAP):
        at = PATCH + 8 * slot
        fields = var[at : at + 8, :] + got[at : at + 8, :]
        weight, row, col, frac_row, frac_col = (fields[f : f + 1, :] for f in range(5))
        down, down_low = split(cover(row, frac_row) * weight)
        across, across_low = split(cover(col, frac_col))
        downs += [down, down_low, down]
        acrosses += [across, across, across_low]
    den = lax.dot_general(
        jnp.concatenate(downs, 1), jnp.concatenate(acrosses, 1), (((1,), (1,)), ((), ())), preferred_element_type=F32
    )
    safe = jnp.maximum(den, 1.0)
    safe_ref[...] = safe
    for half in range(2):
        lo = half * (PATCH + META)
        rows, lanes = slice(lo, lo + PATCH), slice(half * TS, (half + 1) * TS)
        part = safe[:, lanes]
        coadd_var[:, lanes] = (var[rows, :] + got[rows, :]) / (part * part)


def divide_kernel(num, got, safe, coadd):
    for half in range(2):
        rows, lanes = slice(half * PATCH, (half + 1) * PATCH), slice(half * TS, (half + 1) * TS)
        coadd[:, lanes] = (num[rows, :] + got[rows, :]) / safe[:, lanes]


def finish(kernel, name, outs, *args):
    vmem = pl.BlockSpec(memory_space=pltpu.VMEM)
    return pl.pallas_call(
        kernel,
        out_shape=[jax.ShapeDtypeStruct((PATCH, PATCH), F32)] * outs,
        in_specs=[vmem] * len(args),
        out_specs=[vmem] * outs,
        compiler_params=pltpu.CompilerParams(vmem_limit_bytes=8 << 20),
        cost_estimate=pl.CostEstimate(flops=1_000_000_000, bytes_accessed=1 << 20, transcendentals=0),
        name=name,
    )(*args)


EDGES = (((0, 1), (1, 0), (2, 3), (3, 2)), ((1, 2), (2, 1), (3, 0), (0, 3)))


def over_patch(axis, edge):
    pairs = []
    for a, b in EDGES[edge]:
        for other in range(4):
            for core in range(2):
                src, dst = ((a, other), (b, other)) if axis == core else ((other, a), (other, b))
                pairs.append((src[0] * 8 + src[1] * 2 + core, dst[0] * 8 + dst[1] * 2 + core))
    return pairs


def over_visit(edge):
    return [
        (a * 32 + 2 * chip + core, b * 32 + 2 * chip + core)
        for core in range(2)
        for a, b in EDGES[edge ^ core]
        for chip in range(16)
    ]


def halve(left_keep, left_send, right_keep, right_send, last, ahead=()):
    def after(step, *got):
        return lax.optimization_barrier((*got, *ahead[step]))[: len(got)] if step < len(ahead) else got

    left, right = after(
        0, lax.ppermute(left_send, "patch", over_patch(0, 0)), lax.ppermute(right_send, "patch", over_patch(0, 1))
    )
    left_keep, left_send = left_keep[:4] + left[:4], left_keep[4:] + left[4:]
    right_keep, right_send = right_keep[:4] + right[:4], right_keep[4:] + right[4:]
    left_over = [(left_send, right_send)]
    left, right = after(
        1, lax.ppermute(left_send, "patch", over_patch(0, 1)), lax.ppermute(right_send, "patch", over_patch(0, 0))
    )
    keep, send = (
        jnp.concatenate([left_keep[part] + left[part], right_keep[part] + right[part]], 1)
        for part in (slice(0, 2), slice(2, 4))
    )
    left_over.append((send,))
    (got,) = after(2, lax.ppermute(send, "patch", over_patch(1, last)))
    keep, send = keep[:1] + got[:1], keep[1:] + got[1:]
    left_over.append((send,))
    (got,) = after(3, lax.ppermute(send, "patch", over_patch(1, 1 - last)))
    left_over.append((keep[0] + got[0],))
    return left_over[-1][0], left_over


def double(x, first):
    x = x + lax.ppermute(x, ("visit", "patch"), over_visit(first))
    return x, lax.ppermute(x, ("visit", "patch"), over_visit(1 - first))


def shards(image, variance, intersections, boxes, shifts, basis_ids, coefs, taps):
    swap = [(i, i ^ 1) for i in range(32)]
    other_variance = lax.ppermute(variance, "patch", swap)
    table = pack(intersections, boxes, shifts)
    other_table = lax.ppermute(table, "patch", swap)
    matched = match(basis_ids, coefs, taps, image)
    matched, other_table = lax.optimization_barrier((matched, other_table))
    other_matched = lax.ppermute(matched, "patch", swap)
    *var, slots, weights = warp(True, table, other_table, variance, other_variance)
    num = warp(False, slots, table, other_table, weights, matched, other_matched)
    var, ahead = halve(*var, 0)
    num, _ = halve(*num, 1, ahead)
    var, num = double(var, 0), double(num, 1)
    coadd_var, safe = finish(cover_kernel, "cover", 2, *var)
    (coadd,) = finish(divide_kernel, "divide", 1, *num, safe)
    return coadd, coadd_var


def solution(mesh):
    split_spec = ("visit", "patch")
    in_specs = (
        P(split_spec, None, None),
        P(split_spec, None, None),
        P(split_spec, None),
        P(split_spec, None, None),
        P(split_spec, None, None),
        P(split_spec, None),
        P(split_spec, None),
        P(),
    )
    out_specs = (P("patch", None), P("patch", None))
    return jax.shard_map(shards, mesh=mesh, in_specs=in_specs, out_specs=out_specs, check_vma=False)
```

```python
import functools

import jax
import jax.numpy as jnp
from jax import lax
from jax.experimental import pallas as pl
from jax.experimental.pallas import tpu as pltpu
from jax.sharding import PartitionSpec as P

TS = 128
PATCH = 256
NB = 3
NBASIS = 8
HALF = 20
TILES = 32
ROUTES = 2 * TILES
CAP = 3
META = 24
MAIN = 160
PART = (PATCH - MAIN) // 4
PITCH = TS + 8
PAD = 64
F32 = jnp.float32
BF16 = jnp.bfloat16

EMPTY = 1 << 24
UNROLL = 8
MATCH_UNROLL = 16
CHUNKS = 2
MATCH_COST = 100_000_000_000
WARP_COST = 10_000_000_000


def split(x):
    high = x.astype(BF16)
    return high, (x - high.astype(F32)).astype(BF16)


def here():
    patch = lax.axis_index("patch")
    z, y = patch >> 3, (patch >> 1) & 3
    return z, y, patch & 1, lax.axis_index("visit") * 16 + z * 4 + y


def quarter(first, second, core):
    visit = lax.axis_index("visit")
    edges = jnp.where(core == 0, first + 2 * second, 2 * first + second)
    return (visit ^ (visit >> 1)) ^ edges


def place_code(z, y, core):
    first, second = jnp.where(core == 0, z, y), jnp.where(core == 0, y, z)
    first, second = first ^ (first >> 1), second ^ (second >> 1)
    return ((first & 1) << 3) | ((first >> 1) << 2) | ((second & 1) << 1) | (second >> 1)


def pack_kernel(intersections, boxes, shifts, out):
    z, y, _, _ = here()
    out[...] = jnp.zeros_like(out)
    earlier_item = lax.broadcasted_iota(jnp.int32, (TILES, TILES), 0)
    item = lax.broadcasted_iota(jnp.int32, (TILES, TILES), 1)
    dest = [intersections[route : route + 1, :] for route in range(2)]

    def earlier(rows):
        columns = [jnp.sum(jnp.where(earlier_item == item, row, 0), axis=1, keepdims=True) for row in rows]
        counts = []
        for route, row in enumerate(rows):
            same = jnp.where((columns[route] == row) & (earlier_item < item), 1, 0)
            if route == 1:
                same = same + jnp.where(columns[0] == row, 1, 0)
            counts.append(jnp.sum(same, axis=0, keepdims=True))
        return counts

    slots, places = earlier(dest), earlier([d & 1 for d in dest])
    for route in range(2):
        d = dest[route]
        code = place_code(d >> 3, (d >> 1) & 3, d & 1) ^ place_code(z, y, d & 1)
        out[route : route + 1, 0:TILES] = (code + (slots[route] << 4) + ((d & 1) << 8)).astype(F32)
        out[10 + route : 11 + route, 0:TILES] = places[route].astype(F32)
        out[2 + 2 * route : 4 + 2 * route, 0:TILES] = boxes[route].astype(F32)
        out[6 + 2 * route : 8 + 2 * route, 0:TILES] = shifts[route]
    second = jnp.sum(intersections[...] & 1).astype(F32)
    lane = lax.broadcasted_iota(jnp.int32, (1, TS), 1)
    out[12:13, :] = jnp.where(lane == 0, ROUTES - second, second)


def pack(intersections, boxes, shifts):
    vmem = pl.BlockSpec(memory_space=pltpu.VMEM)
    return pl.pallas_call(
        pack_kernel,
        out_shape=jax.ShapeDtypeStruct((16, TS), F32),
        in_specs=[vmem] * 3,
        out_specs=vmem,
        name="pack",
    )(intersections.T, boxes.transpose(1, 2, 0), shifts.transpose(1, 2, 0))


def match_kernel(
    ids_hbm, coefs_hbm, taps_hbm, image_hbm, out, basis_ids, coefs, taps, line, row_mats, col_mats, image, sems, small_sems
):
    size = TILES // CHUNKS
    copies = [
        pltpu.make_async_copy(image_hbm.at[pl.ds(c * size, size)], image.at[pl.ds(c * size, size)], sems.at[c])
        for c in range(CHUNKS)
    ]
    small = [
        pltpu.make_async_copy(source, target, small_sems.at[i])
        for i, (source, target) in enumerate(((taps_hbm, taps), (ids_hbm, basis_ids), (coefs_hbm, coefs)))
    ]
    for copy in small + copies:
        copy.start()
    i = lax.broadcasted_iota(jnp.int32, (TS, TS), 0)
    k = lax.broadcasted_iota(jnp.int32, (TS, TS), 1)
    near = jnp.abs(i - k) <= HALF
    none = jnp.zeros((TS, TS), BF16)
    line[...] = jnp.zeros_like(line)
    for copy in small:
        copy.wait()
    for b in range(NBASIS):
        line[2 * b : 2 * b + 2, 0 : 2 * HALF + 1] = taps[b]
    line[...] = pltpu.roll(line[...], TS - HALF, 1)

    def square(high, low):
        return jnp.concatenate([jnp.concatenate([high, low], 1), jnp.concatenate([high, none], 1)], 0)

    for b in range(NBASIS):
        for side in range(2):
            band = jnp.broadcast_to(line[2 * b + side : 2 * b + side + 1, :], (TS, TS))
            band = jnp.where(near, pltpu.roll(band, 0, 1, stride=1, stride_axis=0), 0.0)
            if side == 0:
                row_mats[b] = jnp.concatenate(split(band.T), 1)
            else:
                col_mats[b] = square(*split(band))

    out[TILES * PITCH :, :] = jnp.zeros((8, TS), F32)
    for c in range(CHUNKS):
        copies[c].wait()

        @pl.loop(c * size, (c + 1) * size, step=MATCH_UNROLL)
        def _(first):
            for t in [first + u for u in range(MATCH_UNROLL)]:
                pixels = square(*split(image[t]))
                bases = [basis_ids[j, t] for j in range(NB)]
                bands = jnp.concatenate([row_mats[basis] for basis in bases], 0)
                p = jnp.dot(bands, pixels, preferred_element_type=F32)
                p = p[:, :TS] + p[:, TS:]
                parts = [jnp.concatenate(split(p[TS * j : TS * (j + 1)] * coefs[j, t]), 1) for j in range(NB)]
                bands = jnp.concatenate([col_mats[basis] for basis in bases], 0)
                total = jnp.dot(jnp.concatenate(parts, 1), bands, preferred_element_type=F32)
                at = pl.multiple_of(t * PITCH, 8)
                out[pl.ds(at, 8), :] = jnp.zeros((8, TS), F32)
                out[pl.ds(at + 8, TS), :] = total[:, :TS] + total[:, TS:]


def match(basis_ids, coefs, taps, image):
    vmem, hbm = pl.BlockSpec(memory_space=pltpu.VMEM), pl.BlockSpec(memory_space=pltpu.HBM)
    return pl.pallas_call(
        match_kernel,
        out_shape=jax.ShapeDtypeStruct((TILES * PITCH + 8, TS), F32),
        in_specs=[hbm] * 4,
        out_specs=vmem,
        scratch_shapes=[
            pltpu.SMEM((NB, TILES), jnp.int32),
            pltpu.SMEM((NB, TILES), F32),
            pltpu.VMEM((NBASIS, 2, 2 * HALF + 1), F32),
            pltpu.VMEM((2 * NBASIS, TS), F32),
            pltpu.VMEM((NBASIS, TS, 2 * TS), BF16),
            pltpu.VMEM((NBASIS, 2 * TS, 2 * TS), BF16),
            pltpu.VMEM((TILES, TS, TS), F32),
            pltpu.SemaphoreType.DMA((CHUNKS,)),
            pltpu.SemaphoreType.DMA((3,)),
        ],
        compiler_params=pltpu.CompilerParams(vmem_limit_bytes=40 << 20),
        cost_estimate=pl.CostEstimate(flops=MATCH_COST, bytes_accessed=6 << 20, transcendentals=0),
        name="match",
    )(*(pltpu.with_memory_space_constraint(x, pltpu.HBM) for x in (basis_ids.T, coefs.T, taps, image)))


def warp_kernel(with_meta, *refs):
    if with_meta:
        own, other, own_raw, other_raw = refs[:4]
        outs, slots, weights = refs[4:10], refs[10], refs[11]
        acc, meta, own_tiles, other_tiles = refs[12:]
    else:
        slots, own, other, weights, own_tiles, other_tiles = refs[:6]
        outs, acc = refs[6:10], refs[10]
    lane = lax.broadcasted_iota(jnp.int32, (8, TS), 1)
    for k in range(16):
        for side in (1, 2):
            acc[4 * k + side, PAD : PAD + PATCH, :] = jnp.zeros((PATCH, TS), F32)

    if with_meta:
        _, _, core, chip = here()
        meta[...] = jnp.zeros_like(meta)

        @pl.loop(0, TILES, step=8)
        def _(first):
            for side, table, raw, tiles in ((0, own, own_raw, own_tiles), (1, other, other_raw, other_tiles)):
                for route in range(2):
                    for t in [first + u for u in range(8)]:
                        what = table[route, t].astype(jnp.int32)
                        at = jnp.where((what >> 8) == core, table[10 + route, t].astype(jnp.int32) + 1, 127)
                        slots[side, at] = (what << 8) + (2 * t + route)
                sums = []
                for t in [first + u for u in range(8)]:
                    tile = raw[t]
                    at = pl.multiple_of(t * PITCH, 8)
                    tiles[pl.ds(at, 8), :] = jnp.zeros((8, TS), F32)
                    tiles[pl.ds(at + 8, TS), :] = tile
                    sums.append(jnp.sum(tile, axis=0, keepdims=True))
                sums = jnp.sum(jnp.concatenate(sums, 0), axis=1, keepdims=True)
                at = pl.multiple_of(side * TILES + first, 8)
                weights[pl.ds(at, 8), :] = jnp.broadcast_to(float(TS * TS) / sums, (8, TS))

        for side, table in ((0, own), (1, other)):
            n = table[12, core].astype(jnp.int32)
            slots[side, 0] = n
            for u in range(UNROLL):
                slots[side, 1 + n + u] = EMPTY
        for tiles in (own_tiles, other_tiles):
            tiles[TILES * PITCH :, :] = jnp.zeros((8, TS), F32)

    def place(entry, side, table, tiles):
        item, k, slot = entry & 255, (entry >> 8) & 15, (entry >> 12) & 3
        t, route = item >> 1, item & 1
        row, col = table[2 + 2 * route, t].astype(jnp.int32), table[3 + 2 * route, t].astype(jnp.int32)
        frac_row, frac_col = table[6 + 2 * route, t], table[7 + 2 * route, t]
        real = jnp.where(entry >= EMPTY, 0.0, 1.0)
        weight = jnp.broadcast_to(weights[pl.ds(side * TILES + t, 1), :], (8, TS))
        scale = weight * real
        if with_meta:
            field = lax.broadcasted_iota(jnp.int32, (8, TS), 0)
            value = jnp.where(field == 1, row.astype(F32), weight)
            value = jnp.where(field == 2, col.astype(F32), value)
            value = jnp.where(field == 3, frac_row, value)
            value = jnp.where(field == 4, frac_col, value)
            value = jnp.where((field < 5) & (lane == 2 * chip + side), value * real, 0.0)
            meta[k * CAP + slot] += value
            scale = scale * weight
        near, far = scale * (1.0 - frac_col), scale * frac_col
        turn, down = (col + TS) & (TS - 1), (row + PAD) & 7
        here = jnp.where(lane >= turn, near, 0.0)
        here_next = jnp.where(lane >= turn + 1, far, 0.0)
        over, over_next = near - here, far - here_next
        start = t * PITCH + 8 - down
        upper, lower = tiles[pl.ds(start, PITCH), :], tiles[pl.ds(start - 1, PITCH), :]
        rows = upper * (1.0 - frac_row) + lower * frac_row
        r0 = pltpu.roll(rows, turn, 1).reshape(PITCH // 8, 8, TS)
        r1 = pltpu.roll(rows, (turn + 1) & (TS - 1), 1).reshape(PITCH // 8, 8, TS)
        left = (r0 * here + r1 * here_next).reshape(PITCH, TS)
        right = (r0 * over + r1 * over_next).reshape(PITCH, TS)
        return left, right, 4 * k + ((col + TS) >> 7), pl.multiple_of(((row + PAD) >> 3) * 8, 8)

    for side, table, tiles in ((0, own, own_tiles), (1, other, other_tiles)):

        @pl.loop(0, (slots[side, 0] + UNROLL - 1) // UNROLL)
        def _(m, side=side, table=table, tiles=tiles):
            for u in range(UNROLL):
                left, right, first, base = place(slots[side, 1 + m * UNROLL + u], side, table, tiles)
                acc[first, pl.ds(base, PITCH), :] += left
                acc[first + 1, pl.ds(base, PITCH), :] += right

    for k in range(16):
        a, b, c, d = k >> 3, (k >> 2) & 1, (k >> 1) & 1, k & 1
        rest = 2 * c + d if with_meta else 2 * d + c
        rows = MAIN if with_meta else PATCH
        left, right = outs[a], outs[2 + b]
        left[4 * b + rest, 0:rows, :] = acc[4 * k + 1, PAD : PAD + rows, :]
        right[4 * a + rest, :, :] = acc[4 * k + 2, PAD : PAD + rows, :]
        if with_meta:
            for slot in range(CAP):
                left[4 * b + rest, MAIN + 8 * slot : MAIN + 8 * slot + 8, :] = meta[k * CAP + slot]

    if with_meta:
        for first in range(2):
            for second in range(2):
                start = pl.multiple_of(PAD + MAIN + PART * quarter(first, second, core), 8)
                for k in range(16):
                    for half in range(2):
                        part = acc[4 * k + 1 + half, pl.ds(start, PART), :]
                        outs[4 + first][second, k, PART * half : PART * (half + 1), :] = part


def warp(with_meta, *args):
    smem, vmem = pl.BlockSpec(memory_space=pltpu.SMEM), pl.BlockSpec(memory_space=pltpu.VMEM)
    left = jax.ShapeDtypeStruct((8, MAIN + META if with_meta else PATCH, TS), F32)
    right = jax.ShapeDtypeStruct((8, MAIN if with_meta else PATCH, TS), F32)
    outs, specs = [left, left, right, right], [vmem] * 4
    if with_meta:
        outs += [jax.ShapeDtypeStruct((2, 16, 2 * PART, TS), F32)] * 2
        specs += [vmem] * 2
    scratch = [pltpu.VMEM((64, 384, TS), F32)]
    if with_meta:
        outs += [jax.ShapeDtypeStruct((2, 128), jnp.int32), jax.ShapeDtypeStruct((2 * TILES, TS), F32)]
        specs += [smem, vmem]
        scratch += [pltpu.VMEM((16 * CAP, 8, TS), F32)] + [pltpu.VMEM((TILES * PITCH + 8, TS), F32)] * 2
    scalars = 2 if with_meta else 3
    return pl.pallas_call(
        functools.partial(warp_kernel, with_meta),
        out_shape=outs,
        in_specs=[smem] * scalars + [vmem] * (len(args) - scalars),
        out_specs=specs,
        scratch_shapes=scratch,
        compiler_params=pltpu.CompilerParams(vmem_limit_bytes=40 << 20),
        cost_estimate=pl.CostEstimate(flops=WARP_COST, bytes_accessed=8 << 20, transcendentals=0),
        name="warp_meta" if with_meta else "warp",
    )(*args)


def cover_kernel(var, got, coadd_var, safe_ref):
    place_of = lax.broadcasted_iota(jnp.int32, (PATCH, TS), 0).astype(F32)

    def cover(offset, shift):
        u = place_of - offset
        lower = jnp.where((u >= 0.0) & (u <= TS - 1.0), 1.0 - shift, 0.0)
        return lower + jnp.where((u >= 1.0) & (u <= float(TS)), shift, 0.0)

    downs, acrosses = [], []
    for slot in range(CAP):
        at = MAIN + 8 * slot
        fields = var[at : at + 8, :] + got[at : at + 8, :]
        weight, row, col, frac_row, frac_col = (fields[f : f + 1, :] for f in range(5))
        down, down_low = split(cover(row, frac_row) * weight)
        across, across_low = split(cover(col, frac_col))
        downs += [down, down_low, down]
        acrosses += [across, across, across_low]
    den = lax.dot_general(
        jnp.concatenate(downs, 1), jnp.concatenate(acrosses, 1), (((1,), (1,)), ((), ())), preferred_element_type=F32
    )
    safe = jnp.maximum(den, 1.0)
    safe_ref[...] = safe
    for half in range(2):
        lo, lanes = half * (MAIN + META), slice(half * TS, (half + 1) * TS)
        part = safe[0:MAIN, lanes]
        coadd_var[0:MAIN, lanes] = (var[lo : lo + MAIN, :] + got[lo : lo + MAIN, :]) / (part * part)
    core = here()[2]
    for second, source in ((0, var), (1, got)):
        for first in range(2):
            rows = pl.ds(pl.multiple_of(MAIN + PART * quarter(first, second, core), 8), PART)
            for half in range(2):
                lo, lanes = 2 * MAIN + META + PART * (2 * first + half), slice(half * TS, (half + 1) * TS)
                part = safe_ref[rows, lanes]
                coadd_var[rows, lanes] = source[lo : lo + PART, :] / (part * part)


def divide_kernel(num, got, safe, coadd):
    for half in range(2):
        rows, lanes = slice(half * PATCH, (half + 1) * PATCH), slice(half * TS, (half + 1) * TS)
        coadd[:, lanes] = (num[rows, :] + got[rows, :]) / safe[:, lanes]


def finish(kernel, name, outs, *args):
    vmem = pl.BlockSpec(memory_space=pltpu.VMEM)
    return pl.pallas_call(
        kernel,
        out_shape=[jax.ShapeDtypeStruct((PATCH, PATCH), F32)] * outs,
        in_specs=[vmem] * len(args),
        out_specs=[vmem] * outs,
        compiler_params=pltpu.CompilerParams(vmem_limit_bytes=8 << 20),
        cost_estimate=pl.CostEstimate(flops=1_000_000_000, bytes_accessed=1 << 20, transcendentals=0),
        name=name,
    )(*args)


EDGES = (((0, 1), (1, 0), (2, 3), (3, 2)), ((1, 2), (2, 1), (3, 0), (0, 3)))


def over_patch(axis, edge):
    pairs = []
    for a, b in EDGES[edge]:
        for other in range(4):
            for core in range(2):
                src, dst = ((a, other), (b, other)) if axis == core else ((other, a), (other, b))
                pairs.append((src[0] * 8 + src[1] * 2 + core, dst[0] * 8 + dst[1] * 2 + core))
    return pairs


def over_visit(edge):
    return [
        (a * 32 + 2 * chip + core, b * 32 + 2 * chip + core)
        for core in range(2)
        for a, b in EDGES[edge ^ core]
        for chip in range(16)
    ]


def halve(left_keep, left_send, right_keep, right_send, last, ahead=()):
    def after(step, *got):
        return lax.optimization_barrier((*got, *ahead[step]))[: len(got)] if step < len(ahead) else got

    left, right = after(
        0, lax.ppermute(left_send, "patch", over_patch(0, 0)), lax.ppermute(right_send, "patch", over_patch(0, 1))
    )
    left_keep, left_send = left_keep[:4] + left[:4], left_keep[4:] + left[4:]
    right_keep, right_send = right_keep[:4] + right[:4], right_keep[4:] + right[4:]
    left, right = after(
        1, lax.ppermute(left_send, "patch", over_patch(0, 1)), lax.ppermute(right_send, "patch", over_patch(0, 0))
    )
    keep, send = (
        jnp.concatenate([left_keep[part] + left[part], right_keep[part] + right[part]], 1)
        for part in (slice(0, 2), slice(2, 4))
    )
    (got,) = after(2, lax.ppermute(send, "patch", over_patch(1, last)))
    keep, send = keep[:1] + got[:1], keep[1:] + got[1:]
    (got,) = after(3, lax.ppermute(send, "patch", over_patch(1, 1 - last)))
    return keep[0] + got[0]


def double(x, first):
    x = x + lax.ppermute(x, ("visit", "patch"), over_visit(first))
    return x, lax.ppermute(x, ("visit", "patch"), over_visit(1 - first))


def halve_var(left_keep, left_send, right_keep, right_send, part_keep, part_send):
    def cross(x, axis, edge):
        return lax.ppermute(x, "patch", over_patch(axis, edge))

    def visit(x, edge):
        return lax.ppermute(x, ("visit", "patch"), over_visit(edge))

    def fold(keep, got):
        n = keep.shape[0] // 2
        return keep[:n] + got[:n], keep[n:] + got[n:]

    left, right, part = cross(left_send, 0, 0), cross(right_send, 0, 1), visit(part_send, 0)
    left_keep, left_send = fold(left_keep, left)
    right_keep, right_send = fold(right_keep, right)
    part_keep, part_send = part_keep[0] + part[0], part_keep[1] + part[1]
    left_over = [(left_send, right_send, part_send)]
    left, right, part = cross(left_send, 0, 1), cross(right_send, 0, 0), visit(part_send, 1)
    part_keep, part_send = fold(part_keep, part)
    left_over.append((part_send,))
    part_keep, part_send = fold(part_keep, cross(part_send, 0, 0))
    part = cross(part_send, 0, 1)
    keep, send = (
        jnp.concatenate([left_keep[p] + left[p], right_keep[p] + right[p], part_keep[p] + part[p]], 1)
        for p in (slice(0, 2), slice(2, 4))
    )
    left_over.append((send,))
    keep, send = fold(keep, cross(send, 1, 0))
    x = keep[0] + cross(send, 1, 1)[0]
    got, main = visit(x, 0), 2 * MAIN + META
    x = jnp.concatenate([x[:main] + got[:main], x[main:], got[main:]], 0)
    return (x, visit(x, 1)), left_over


def shards(image, variance, intersections, boxes, shifts, basis_ids, coefs, taps):
    swap = [(i, i ^ 1) for i in range(32)]
    other_variance = lax.ppermute(variance, "patch", swap)
    table = pack(intersections, boxes, shifts)
    other_table = lax.ppermute(table, "patch", swap)
    matched = match(basis_ids, coefs, taps, image)
    matched, other_table = lax.optimization_barrier((matched, other_table))
    other_matched = lax.ppermute(matched, "patch", swap)
    *var, slots, weights = warp(True, table, other_table, variance, other_variance)
    num = warp(False, slots, table, other_table, weights, matched, other_matched)
    var, ahead = halve_var(*var)
    num = double(halve(*num, 1, ahead), 1)
    coadd_var, safe = finish(cover_kernel, "cover", 2, *var)
    (coadd,) = finish(divide_kernel, "divide", 1, *num, safe)
    return coadd, coadd_var


def solution(mesh):
    split_spec = ("visit", "patch")
    in_specs = (
        P(split_spec, None, None),
        P(split_spec, None, None),
        P(split_spec, None),
        P(split_spec, None, None),
        P(split_spec, None, None),
        P(split_spec, None),
        P(split_spec, None),
        P(),
    )
    out_specs = (P("patch", None), P("patch", None))
    return jax.shard_map(shards, mesh=mesh, in_specs=in_specs, out_specs=out_specs, check_vma=False)
```

```python
import functools

import jax
import jax.numpy as jnp
from jax import lax
from jax.experimental import pallas as pl
from jax.experimental.pallas import tpu as pltpu
from jax.sharding import PartitionSpec as P

TS = 128
PATCH = 256
NB = 3
NBASIS = 8
HALF = 20
TILES = 32
ROUTES = 2 * TILES
CAP = 3
META = 24
MAIN = 160
PART = (PATCH - MAIN) // 4
PITCH = TS + 8
PAD = 64
F32 = jnp.float32
BF16 = jnp.bfloat16

EMPTY = 1 << 24
UNROLL = 8
MATCH_UNROLL = 16
CHUNKS = 2
MATCH_COST = 100_000_000_000
WARP_COST = 10_000_000_000


def split(x):
    high = x.astype(BF16)
    return high, (x - high.astype(F32)).astype(BF16)


def here():
    patch = lax.axis_index("patch")
    z, y = patch >> 3, (patch >> 1) & 3
    return z, y, patch & 1, lax.axis_index("visit") * 16 + z * 4 + y


def quarter(first, second, core):
    visit = lax.axis_index("visit")
    edges = jnp.where(core == 0, first + 2 * second, 2 * first + second)
    return (visit ^ (visit >> 1)) ^ edges


def place_code(z, y, core):
    first, second = jnp.where(core == 0, z, y), jnp.where(core == 0, y, z)
    first, second = first ^ (first >> 1), second ^ (second >> 1)
    return ((first & 1) << 3) | ((first >> 1) << 2) | ((second & 1) << 1) | (second >> 1)


def pack_kernel(intersections, boxes, shifts, out):
    z, y, _, _ = here()
    out[...] = jnp.zeros_like(out)
    earlier_item = lax.broadcasted_iota(jnp.int32, (TILES, TILES), 0)
    item = lax.broadcasted_iota(jnp.int32, (TILES, TILES), 1)
    dest = [intersections[route : route + 1, :] for route in range(2)]

    def earlier(rows):
        columns = [jnp.sum(jnp.where(earlier_item == item, row, 0), axis=1, keepdims=True) for row in rows]
        counts = []
        for route, row in enumerate(rows):
            same = jnp.where((columns[route] == row) & (earlier_item < item), 1, 0)
            if route == 1:
                same = same + jnp.where(columns[0] == row, 1, 0)
            counts.append(jnp.sum(same, axis=0, keepdims=True))
        return counts

    slots, places = earlier(dest), earlier([d & 1 for d in dest])
    for route in range(2):
        d = dest[route]
        code = place_code(d >> 3, (d >> 1) & 3, d & 1) ^ place_code(z, y, d & 1)
        out[route : route + 1, 0:TILES] = (code + (slots[route] << 4) + ((d & 1) << 8)).astype(F32)
        out[10 + route : 11 + route, 0:TILES] = places[route].astype(F32)
        out[2 + 2 * route : 4 + 2 * route, 0:TILES] = boxes[route].astype(F32)
        out[6 + 2 * route : 8 + 2 * route, 0:TILES] = shifts[route]
    second = jnp.sum(intersections[...] & 1).astype(F32)
    lane = lax.broadcasted_iota(jnp.int32, (1, TS), 1)
    out[12:13, :] = jnp.where(lane == 0, ROUTES - second, second)


def pack(intersections, boxes, shifts):
    vmem = pl.BlockSpec(memory_space=pltpu.VMEM)
    return pl.pallas_call(
        pack_kernel,
        out_shape=jax.ShapeDtypeStruct((16, TS), F32),
        in_specs=[vmem] * 3,
        out_specs=vmem,
        name="pack",
    )(intersections.T, boxes.transpose(1, 2, 0), shifts.transpose(1, 2, 0))


def match_kernel(
    ids_hbm, coefs_hbm, taps_hbm, image_hbm, out, basis_ids, coefs, taps, line, row_mats, col_mats, image, sems, small_sems
):
    size = TILES // CHUNKS
    copies = [
        pltpu.make_async_copy(image_hbm.at[pl.ds(c * size, size)], image.at[pl.ds(c * size, size)], sems.at[c])
        for c in range(CHUNKS)
    ]
    small = [
        pltpu.make_async_copy(source, target, small_sems.at[i])
        for i, (source, target) in enumerate(((taps_hbm, taps), (ids_hbm, basis_ids), (coefs_hbm, coefs)))
    ]
    for copy in small + copies:
        copy.start()
    i = lax.broadcasted_iota(jnp.int32, (TS, TS), 0)
    k = lax.broadcasted_iota(jnp.int32, (TS, TS), 1)
    near = jnp.abs(i - k) <= HALF
    none = jnp.zeros((TS, TS), BF16)
    line[...] = jnp.zeros_like(line)
    for copy in small:
        copy.wait()
    for b in range(NBASIS):
        line[2 * b : 2 * b + 2, 0 : 2 * HALF + 1] = taps[b]
    line[...] = pltpu.roll(line[...], TS - HALF, 1)

    def square(high, low):
        return jnp.concatenate([jnp.concatenate([high, low], 1), jnp.concatenate([high, none], 1)], 0)

    for b in range(NBASIS):
        for side in range(2):
            band = jnp.broadcast_to(line[2 * b + side : 2 * b + side + 1, :], (TS, TS))
            band = jnp.where(near, pltpu.roll(band, 0, 1, stride=1, stride_axis=0), 0.0)
            if side == 0:
                row_mats[b] = jnp.concatenate(split(band.T), 1)
            else:
                col_mats[b] = square(*split(band))

    out[TILES * PITCH :, :] = jnp.zeros((8, TS), F32)
    for c in range(CHUNKS):
        copies[c].wait()

        @pl.loop(c * size, (c + 1) * size, step=MATCH_UNROLL)
        def _(first):
            for t in [first + u for u in range(MATCH_UNROLL)]:
                pixels = square(*split(image[t]))
                bases = [basis_ids[j, t] for j in range(NB)]
                bands = jnp.concatenate([row_mats[basis] for basis in bases], 0)
                p = jnp.dot(bands, pixels, preferred_element_type=F32)
                p = p[:, :TS] + p[:, TS:]
                parts = [jnp.concatenate(split(p[TS * j : TS * (j + 1)] * coefs[j, t]), 1) for j in range(NB)]
                bands = jnp.concatenate([col_mats[basis] for basis in bases], 0)
                total = jnp.dot(jnp.concatenate(parts, 1), bands, preferred_element_type=F32)
                at = pl.multiple_of(t * PITCH, 8)
                out[pl.ds(at, 8), :] = jnp.zeros((8, TS), F32)
                out[pl.ds(at + 8, TS), :] = total[:, :TS] + total[:, TS:]


def match(basis_ids, coefs, taps, image):
    vmem, hbm = pl.BlockSpec(memory_space=pltpu.VMEM), pl.BlockSpec(memory_space=pltpu.HBM)
    return pl.pallas_call(
        match_kernel,
        out_shape=jax.ShapeDtypeStruct((TILES * PITCH + 8, TS), F32),
        in_specs=[hbm] * 4,
        out_specs=vmem,
        scratch_shapes=[
            pltpu.SMEM((NB, TILES), jnp.int32),
            pltpu.SMEM((NB, TILES), F32),
            pltpu.VMEM((NBASIS, 2, 2 * HALF + 1), F32),
            pltpu.VMEM((2 * NBASIS, TS), F32),
            pltpu.VMEM((NBASIS, TS, 2 * TS), BF16),
            pltpu.VMEM((NBASIS, 2 * TS, 2 * TS), BF16),
            pltpu.VMEM((TILES, TS, TS), F32),
            pltpu.SemaphoreType.DMA((CHUNKS,)),
            pltpu.SemaphoreType.DMA((3,)),
        ],
        compiler_params=pltpu.CompilerParams(vmem_limit_bytes=40 << 20),
        cost_estimate=pl.CostEstimate(flops=MATCH_COST, bytes_accessed=6 << 20, transcendentals=0),
        name="match",
    )(*(pltpu.with_memory_space_constraint(x, pltpu.HBM) for x in (basis_ids.T, coefs.T, taps, image)))


def warp_kernel(with_meta, *refs):
    if with_meta:
        own, other, own_raw, other_raw = refs[:4]
        outs, slots, weights = refs[4:10], refs[10], refs[11]
        acc, meta, own_tiles, other_tiles = refs[12:]
    else:
        slots, own, other, weights, own_tiles, other_tiles = refs[:6]
        outs, acc = refs[6:10], refs[10]
    lane = lax.broadcasted_iota(jnp.int32, (8, TS), 1)
    for k in range(16):
        for side in (1, 2):
            acc[4 * k + side, PAD : PAD + PATCH, :] = jnp.zeros((PATCH, TS), F32)

    if with_meta:
        _, _, core, chip = here()
        meta[...] = jnp.zeros_like(meta)

        @pl.loop(0, TILES, step=8)
        def _(first):
            for side, table, raw, tiles in ((0, own, own_raw, own_tiles), (1, other, other_raw, other_tiles)):
                for route in range(2):
                    for t in [first + u for u in range(8)]:
                        what = table[route, t].astype(jnp.int32)
                        at = jnp.where((what >> 8) == core, table[10 + route, t].astype(jnp.int32) + 1, 127)
                        slots[side, at] = (what << 8) + (2 * t + route)
                sums = []
                for t in [first + u for u in range(8)]:
                    tile = raw[t]
                    at = pl.multiple_of(t * PITCH, 8)
                    tiles[pl.ds(at, 8), :] = jnp.zeros((8, TS), F32)
                    tiles[pl.ds(at + 8, TS), :] = tile
                    sums.append(jnp.sum(tile, axis=0, keepdims=True))
                sums = jnp.sum(jnp.concatenate(sums, 0), axis=1, keepdims=True)
                at = pl.multiple_of(side * TILES + first, 8)
                weights[pl.ds(at, 8), :] = jnp.broadcast_to(float(TS * TS) / sums, (8, TS))

        for side, table in ((0, own), (1, other)):
            n = table[12, core].astype(jnp.int32)
            slots[side, 0] = n
            for u in range(UNROLL):
                slots[side, 1 + n + u] = EMPTY
        for tiles in (own_tiles, other_tiles):
            tiles[TILES * PITCH :, :] = jnp.zeros((8, TS), F32)

    def place(entry, side, table, tiles):
        item, k, slot = entry & 255, (entry >> 8) & 15, (entry >> 12) & 3
        t, route = item >> 1, item & 1
        row, col = table[2 + 2 * route, t].astype(jnp.int32), table[3 + 2 * route, t].astype(jnp.int32)
        frac_row, frac_col = table[6 + 2 * route, t], table[7 + 2 * route, t]
        real = jnp.where(entry >= EMPTY, 0.0, 1.0)
        weight = jnp.broadcast_to(weights[pl.ds(side * TILES + t, 1), :], (8, TS))
        scale = weight * real
        if with_meta:
            field = lax.broadcasted_iota(jnp.int32, (8, TS), 0)
            value = jnp.where(field == 1, row.astype(F32), weight)
            value = jnp.where(field == 2, col.astype(F32), value)
            value = jnp.where(field == 3, frac_row, value)
            value = jnp.where(field == 4, frac_col, value)
            value = jnp.where((field < 5) & (lane == 2 * chip + side), value * real, 0.0)
            meta[k * CAP + slot] += value
            scale = scale * weight
        near, far = scale * (1.0 - frac_col), scale * frac_col
        turn, down = (col + TS) & (TS - 1), (row + PAD) & 7
        here = jnp.where(lane >= turn, near, 0.0)
        here_next = jnp.where(lane >= turn + 1, far, 0.0)
        over, over_next = near - here, far - here_next
        start = t * PITCH + 8 - down
        upper, lower = tiles[pl.ds(start, PITCH), :], tiles[pl.ds(start - 1, PITCH), :]
        rows = upper * (1.0 - frac_row) + lower * frac_row
        r0 = pltpu.roll(rows, turn, 1).reshape(PITCH // 8, 8, TS)
        r1 = pltpu.roll(rows, (turn + 1) & (TS - 1), 1).reshape(PITCH // 8, 8, TS)
        left = (r0 * here + r1 * here_next).reshape(PITCH, TS)
        right = (r0 * over + r1 * over_next).reshape(PITCH, TS)
        return left, right, 4 * k + ((col + TS) >> 7), pl.multiple_of(((row + PAD) >> 3) * 8, 8)

    for side, table, tiles in ((0, own, own_tiles), (1, other, other_tiles)):

        @pl.loop(0, (slots[side, 0] + UNROLL - 1) // UNROLL)
        def _(m, side=side, table=table, tiles=tiles):
            for u in range(UNROLL):
                left, right, first, base = place(slots[side, 1 + m * UNROLL + u], side, table, tiles)
                acc[first, pl.ds(base, PITCH), :] += left
                acc[first + 1, pl.ds(base, PITCH), :] += right

    for k in range(16):
        a, b, c, d = k >> 3, (k >> 2) & 1, (k >> 1) & 1, k & 1
        rest = 2 * c + d if with_meta else 2 * d + c
        rows = MAIN if with_meta else PATCH
        left, right = outs[a], outs[2 + b]
        left[4 * b + rest, 0:rows, :] = acc[4 * k + 1, PAD : PAD + rows, :]
        right[4 * a + rest, :, :] = acc[4 * k + 2, PAD : PAD + rows, :]
        if with_meta:
            for slot in range(CAP):
                left[4 * b + rest, MAIN + 8 * slot : MAIN + 8 * slot + 8, :] = meta[k * CAP + slot]

    if with_meta:
        for first in range(2):
            for second in range(2):
                start = pl.multiple_of(PAD + MAIN + PART * quarter(first, second, core), 8)
                for k in range(16):
                    for half in range(2):
                        part = acc[4 * k + 1 + half, pl.ds(start, PART), :]
                        outs[4 + first][second, k, PART * half : PART * (half + 1), :] = part


def warp(with_meta, *args):
    smem, vmem = pl.BlockSpec(memory_space=pltpu.SMEM), pl.BlockSpec(memory_space=pltpu.VMEM)
    left = jax.ShapeDtypeStruct((8, MAIN + META if with_meta else PATCH, TS), F32)
    right = jax.ShapeDtypeStruct((8, MAIN if with_meta else PATCH, TS), F32)
    outs, specs = [left, left, right, right], [vmem] * 4
    if with_meta:
        outs += [jax.ShapeDtypeStruct((2, 16, 2 * PART, TS), F32)] * 2
        specs += [vmem] * 2
    scratch = [pltpu.VMEM((64, 384, TS), F32)]
    if with_meta:
        outs += [jax.ShapeDtypeStruct((2, 128), jnp.int32), jax.ShapeDtypeStruct((2 * TILES, TS), F32)]
        specs += [smem, vmem]
        scratch += [pltpu.VMEM((16 * CAP, 8, TS), F32)] + [pltpu.VMEM((TILES * PITCH + 8, TS), F32)] * 2
    scalars = 2 if with_meta else 3
    return pl.pallas_call(
        functools.partial(warp_kernel, with_meta),
        out_shape=outs,
        in_specs=[smem] * scalars + [vmem] * (len(args) - scalars),
        out_specs=specs,
        scratch_shapes=scratch,
        compiler_params=pltpu.CompilerParams(vmem_limit_bytes=40 << 20),
        cost_estimate=pl.CostEstimate(flops=WARP_COST, bytes_accessed=8 << 20, transcendentals=0),
        name="warp_meta" if with_meta else "warp",
    )(*args)


def cover_kernel(var, got, coadd_var, safe_ref):
    place_of = lax.broadcasted_iota(jnp.int32, (PATCH, TS), 0).astype(F32)

    def cover(offset, shift):
        u = place_of - offset
        lower = jnp.where((u >= 0.0) & (u <= TS - 1.0), 1.0 - shift, 0.0)
        return lower + jnp.where((u >= 1.0) & (u <= float(TS)), shift, 0.0)

    downs, acrosses = [], []
    for slot in range(CAP):
        at = MAIN + 8 * slot
        fields = var[at : at + 8, :] + got[at : at + 8, :]
        weight, row, col, frac_row, frac_col = (fields[f : f + 1, :] for f in range(5))
        down, down_low = split(cover(row, frac_row) * weight)
        across, across_low = split(cover(col, frac_col))
        downs += [down, down_low, down]
        acrosses += [across, across, across_low]
    den = lax.dot_general(
        jnp.concatenate(downs, 1), jnp.concatenate(acrosses, 1), (((1,), (1,)), ((), ())), preferred_element_type=F32
    )
    safe = jnp.maximum(den, 1.0)
    safe_ref[...] = safe
    for half in range(2):
        lo, lanes = half * (MAIN + META), slice(half * TS, (half + 1) * TS)
        part = safe[0:MAIN, lanes]
        coadd_var[0:MAIN, lanes] = (var[lo : lo + MAIN, :] + got[lo : lo + MAIN, :]) / (part * part)
    core = here()[2]
    for second, source in ((0, var), (1, got)):
        for first in range(2):
            rows = pl.ds(pl.multiple_of(MAIN + PART * quarter(first, second, core), 8), PART)
            for half in range(2):
                lo, lanes = 2 * MAIN + META + PART * (2 * first + half), slice(half * TS, (half + 1) * TS)
                part = safe_ref[rows, lanes]
                coadd_var[rows, lanes] = source[lo : lo + PART, :] / (part * part)


def divide_kernel(num, got, safe, coadd):
    for half in range(2):
        rows, lanes = slice(half * PATCH, (half + 1) * PATCH), slice(half * TS, (half + 1) * TS)
        coadd[:, lanes] = (num[rows, :] + got[rows, :]) / safe[:, lanes]


def finish(kernel, name, outs, *args):
    vmem = pl.BlockSpec(memory_space=pltpu.VMEM)
    return pl.pallas_call(
        kernel,
        out_shape=[jax.ShapeDtypeStruct((PATCH, PATCH), F32)] * outs,
        in_specs=[vmem] * len(args),
        out_specs=[vmem] * outs,
        compiler_params=pltpu.CompilerParams(vmem_limit_bytes=8 << 20),
        cost_estimate=pl.CostEstimate(flops=1_000_000_000, bytes_accessed=1 << 20, transcendentals=0),
        name=name,
    )(*args)


EDGES = (((0, 1), (1, 0), (2, 3), (3, 2)), ((1, 2), (2, 1), (3, 0), (0, 3)))


def over_patch(axis, edge):
    pairs = []
    for a, b in EDGES[edge]:
        for other in range(4):
            for core in range(2):
                src, dst = ((a, other), (b, other)) if axis == core else ((other, a), (other, b))
                pairs.append((src[0] * 8 + src[1] * 2 + core, dst[0] * 8 + dst[1] * 2 + core))
    return pairs


def over_visit(edge):
    return [
        (a * 32 + 2 * chip + core, b * 32 + 2 * chip + core)
        for core in range(2)
        for a, b in EDGES[edge ^ core]
        for chip in range(16)
    ]


def combine(var, num):
    def cross(x, axis, edge):
        return lax.ppermute(x, "patch", over_patch(axis, edge))

    def visit(x, edge):
        return lax.ppermute(x, ("visit", "patch"), over_visit(edge))

    def fold(keep, got):
        n = keep.shape[0] // 2
        return keep[:n] + got[:n], keep[n:] + got[n:]

    def after(got, *earlier):
        return lax.optimization_barrier((*got, *earlier))[: len(got)]

    (vl, vl_send, vr, vr_send, vp, vp_send), (nl, nl_send, nr, nr_send) = var, num
    vl_got, vr_got, vp_got = cross(vl_send, 0, 0), cross(vr_send, 0, 1), visit(vp_send, 0)
    nl_got, nr_got = cross(nl_send, 0, 0), cross(nr_send, 0, 1)

    (vl, vl_send), (vr, vr_send) = fold(vl, vl_got), fold(vr, vr_got)
    vp, vp_send = vp[0] + vp_got[0], vp[1] + vp_got[1]
    vl_got, vr_got, vp_got = cross(vl_send, 0, 1), cross(vr_send, 0, 0), visit(vp_send, 1)
    nl_got, nr_got = after((nl_got, nr_got), vl_send, vr_send, vp_send)
    vp, vp_send = fold(vp, vp_got)
    vp, vp_send = fold(vp, cross(vp_send, 0, 0))
    vp = vp + cross(vp_send, 0, 1)

    (nl, nl_send), (nr, nr_send) = fold(nl, nl_got), fold(nr, nr_got)
    nl_got, nr_got = cross(nl_send, 0, 1), cross(nr_send, 0, 0)

    vl_got, vr_got = after((vl_got, vr_got), nl_send, nr_send, vp_send)
    v, v_send = (
        jnp.concatenate([vl[p] + vl_got[p], vr[p] + vr_got[p], vp[p]], 1) for p in (slice(0, 2), slice(2, 4))
    )
    v_got = cross(v_send, 1, 0)

    nl_got, nr_got = after((nl_got, nr_got), v_send)
    n, n_send = (jnp.concatenate([nl[p] + nl_got[p], nr[p] + nr_got[p]], 1) for p in (slice(0, 2), slice(2, 4)))
    n_got = cross(n_send, 1, 1)

    v, v_send = fold(v, v_got)
    v = v[0] + cross(v_send, 1, 1)[0]
    (n_got,) = after((n_got,), v_send)
    n, n_send = fold(n, n_got)
    n = n[0] + cross(n_send, 1, 0)[0]

    v_got, main = visit(v, 0), 2 * MAIN + META
    v = jnp.concatenate([v[:main] + v_got[:main], v[main:], v_got[main:]], 0)
    n = n + visit(n, 0)
    return (v, visit(v, 1)), (n, visit(n, 1))


def shards(image, variance, intersections, boxes, shifts, basis_ids, coefs, taps):
    swap = [(i, i ^ 1) for i in range(32)]
    other_variance = lax.ppermute(variance, "patch", swap)
    table = pack(intersections, boxes, shifts)
    other_table = lax.ppermute(table, "patch", swap)
    matched = match(basis_ids, coefs, taps, image)
    matched, other_table = lax.optimization_barrier((matched, other_table))
    other_matched = lax.ppermute(matched, "patch", swap)
    *var, slots, weights = warp(True, table, other_table, variance, other_variance)
    num = warp(False, slots, table, other_table, weights, matched, other_matched)
    var, num = combine(var, num)
    coadd_var, safe = finish(cover_kernel, "cover", 2, *var)
    (coadd,) = finish(divide_kernel, "divide", 1, *num, safe)
    return coadd, coadd_var


def solution(mesh):
    split_spec = ("visit", "patch")
    in_specs = (
        P(split_spec, None, None),
        P(split_spec, None, None),
        P(split_spec, None),
        P(split_spec, None, None),
        P(split_spec, None, None),
        P(split_spec, None),
        P(split_spec, None),
        P(),
    )
    out_specs = (P("patch", None), P("patch", None))
    return jax.shard_map(shards, mesh=mesh, in_specs=in_specs, out_specs=out_specs, check_vma=False)
```

```python
import functools

import jax
import jax.numpy as jnp
from jax import lax
from jax.experimental import pallas as pl
from jax.experimental.pallas import tpu as pltpu
from jax.sharding import PartitionSpec as P

TS = 128
PATCH = 256
NB = 3
NBASIS = 8
HALF = 20
TILES = 32
ROUTES = 2 * TILES
CAP = 3
META = 24
MAIN = 160
PART = (PATCH - MAIN) // 4
PITCH = TS + 8
PAD = 64
F32 = jnp.float32
BF16 = jnp.bfloat16

EMPTY = 1 << 24
UNROLL = 8
MATCH_UNROLL = 16
CHUNKS = 2
MATCH_COST = 100_000_000_000
WARP_COST = 10_000_000_000


def split(x):
    high = x.astype(BF16)
    return high, (x - high.astype(F32)).astype(BF16)


def here():
    patch = lax.axis_index("patch")
    z, y = patch >> 3, (patch >> 1) & 3
    return z, y, patch & 1, lax.axis_index("visit") * 16 + z * 4 + y


def quarter(first, second, core):
    visit = lax.axis_index("visit")
    edges = jnp.where(core == 0, first + 2 * second, 2 * first + second)
    return (visit ^ (visit >> 1)) ^ edges


def place_code(z, y, core):
    first, second = jnp.where(core == 0, z, y), jnp.where(core == 0, y, z)
    first, second = first ^ (first >> 1), second ^ (second >> 1)
    return ((first & 1) << 3) | ((first >> 1) << 2) | ((second & 1) << 1) | (second >> 1)


def pack_kernel(intersections, boxes, shifts, out):
    z, y, _, _ = here()
    out[...] = jnp.zeros_like(out)
    earlier_item = lax.broadcasted_iota(jnp.int32, (TILES, TILES), 0)
    item = lax.broadcasted_iota(jnp.int32, (TILES, TILES), 1)
    dest = [intersections[route : route + 1, :] for route in range(2)]

    def earlier(rows):
        columns = [jnp.sum(jnp.where(earlier_item == item, row, 0), axis=1, keepdims=True) for row in rows]
        counts = []
        for route, row in enumerate(rows):
            same = jnp.where((columns[route] == row) & (earlier_item < item), 1, 0)
            if route == 1:
                same = same + jnp.where(columns[0] == row, 1, 0)
            counts.append(jnp.sum(same, axis=0, keepdims=True))
        return counts

    slots, places = earlier(dest), earlier([d & 1 for d in dest])
    for route in range(2):
        d = dest[route]
        code = place_code(d >> 3, (d >> 1) & 3, d & 1) ^ place_code(z, y, d & 1)
        out[route : route + 1, 0:TILES] = (code + (slots[route] << 4) + ((d & 1) << 8)).astype(F32)
        out[10 + route : 11 + route, 0:TILES] = places[route].astype(F32)
        out[2 + 2 * route : 4 + 2 * route, 0:TILES] = boxes[route].astype(F32)
        out[6 + 2 * route : 8 + 2 * route, 0:TILES] = shifts[route]
    second = jnp.sum(intersections[...] & 1).astype(F32)
    lane = lax.broadcasted_iota(jnp.int32, (1, TS), 1)
    out[12:13, :] = jnp.where(lane == 0, ROUTES - second, second)


def pack(intersections, boxes, shifts):
    vmem = pl.BlockSpec(memory_space=pltpu.VMEM)
    return pl.pallas_call(
        pack_kernel,
        out_shape=jax.ShapeDtypeStruct((16, TS), F32),
        in_specs=[vmem] * 3,
        out_specs=vmem,
        name="pack",
    )(intersections.T, boxes.transpose(1, 2, 0), shifts.transpose(1, 2, 0))


def match_kernel(
    ids_hbm, coefs_hbm, taps_hbm, image_hbm, out, basis_ids, coefs, taps, line, row_mats, col_mats, image, sems, small_sems
):
    size = TILES // CHUNKS
    copies = [
        pltpu.make_async_copy(image_hbm.at[pl.ds(c * size, size)], image.at[pl.ds(c * size, size)], sems.at[c])
        for c in range(CHUNKS)
    ]
    small = [
        pltpu.make_async_copy(source, target, small_sems.at[i])
        for i, (source, target) in enumerate(((taps_hbm, taps), (ids_hbm, basis_ids), (coefs_hbm, coefs)))
    ]
    for copy in small + copies:
        copy.start()
    i = lax.broadcasted_iota(jnp.int32, (TS, TS), 0)
    k = lax.broadcasted_iota(jnp.int32, (TS, TS), 1)
    near = jnp.abs(i - k) <= HALF
    none = jnp.zeros((TS, TS), BF16)
    line[...] = jnp.zeros_like(line)
    for copy in small:
        copy.wait()
    for b in range(NBASIS):
        line[2 * b : 2 * b + 2, 0 : 2 * HALF + 1] = taps[b]
    line[...] = pltpu.roll(line[...], TS - HALF, 1)

    def square(high, low):
        return jnp.concatenate([jnp.concatenate([high, low], 1), jnp.concatenate([high, none], 1)], 0)

    for b in range(NBASIS):
        for side in range(2):
            band = jnp.broadcast_to(line[2 * b + side : 2 * b + side + 1, :], (TS, TS))
            band = jnp.where(near, pltpu.roll(band, 0, 1, stride=1, stride_axis=0), 0.0)
            if side == 0:
                row_mats[b] = jnp.concatenate(split(band.T), 1)
            else:
                col_mats[b] = square(*split(band))

    out[TILES * PITCH :, :] = jnp.zeros((8, TS), F32)
    for c in range(CHUNKS):
        copies[c].wait()

        @pl.loop(c * size, (c + 1) * size, step=MATCH_UNROLL)
        def _(first):
            for t in [first + u for u in range(MATCH_UNROLL)]:
                pixels = square(*split(image[t]))
                bases = [basis_ids[j, t] for j in range(NB)]
                bands = jnp.concatenate([row_mats[basis] for basis in bases], 0)
                p = jnp.dot(bands, pixels, preferred_element_type=F32)
                p = p[:, :TS] + p[:, TS:]
                parts = [jnp.concatenate(split(p[TS * j : TS * (j + 1)] * coefs[j, t]), 1) for j in range(NB)]
                bands = jnp.concatenate([col_mats[basis] for basis in bases], 0)
                total = jnp.dot(jnp.concatenate(parts, 1), bands, preferred_element_type=F32)
                at = pl.multiple_of(t * PITCH, 8)
                out[pl.ds(at, 8), :] = jnp.zeros((8, TS), F32)
                out[pl.ds(at + 8, TS), :] = total[:, :TS] + total[:, TS:]


def match(basis_ids, coefs, taps, image):
    vmem, hbm = pl.BlockSpec(memory_space=pltpu.VMEM), pl.BlockSpec(memory_space=pltpu.HBM)
    return pl.pallas_call(
        match_kernel,
        out_shape=jax.ShapeDtypeStruct((TILES * PITCH + 8, TS), F32),
        in_specs=[hbm] * 4,
        out_specs=vmem,
        scratch_shapes=[
            pltpu.SMEM((NB, TILES), jnp.int32),
            pltpu.SMEM((NB, TILES), F32),
            pltpu.VMEM((NBASIS, 2, 2 * HALF + 1), F32),
            pltpu.VMEM((2 * NBASIS, TS), F32),
            pltpu.VMEM((NBASIS, TS, 2 * TS), BF16),
            pltpu.VMEM((NBASIS, 2 * TS, 2 * TS), BF16),
            pltpu.VMEM((TILES, TS, TS), F32),
            pltpu.SemaphoreType.DMA((CHUNKS,)),
            pltpu.SemaphoreType.DMA((3,)),
        ],
        compiler_params=pltpu.CompilerParams(vmem_limit_bytes=40 << 20),
        cost_estimate=pl.CostEstimate(flops=MATCH_COST, bytes_accessed=6 << 20, transcendentals=0),
        name="match",
    )(*(pltpu.with_memory_space_constraint(x, pltpu.HBM) for x in (basis_ids.T, coefs.T, taps, image)))


def warp_kernel(with_meta, *refs):
    if with_meta:
        own, other, own_raw, other_raw = refs[:4]
        outs, slots, weights = refs[4:10], refs[10], refs[11]
        acc, meta, own_tiles, other_tiles = refs[12:]
    else:
        slots, own, other, weights, own_tiles, other_tiles = refs[:6]
        outs, acc = refs[6:10], refs[10]
    lane = lax.broadcasted_iota(jnp.int32, (8, TS), 1)
    for k in range(16):
        for side in (1, 2):
            acc[4 * k + side, PAD : PAD + PATCH, :] = jnp.zeros((PATCH, TS), F32)

    if with_meta:
        _, _, core, chip = here()
        meta[...] = jnp.zeros_like(meta)

        @pl.loop(0, TILES, step=8)
        def _(first):
            for side, table, raw, tiles in ((0, own, own_raw, own_tiles), (1, other, other_raw, other_tiles)):
                for route in range(2):
                    for t in [first + u for u in range(8)]:
                        what = table[route, t].astype(jnp.int32)
                        at = jnp.where((what >> 8) == core, table[10 + route, t].astype(jnp.int32) + 1, 127)
                        slots[side, at] = (what << 8) + (2 * t + route)
                sums = []
                for t in [first + u for u in range(8)]:
                    tile = raw[t]
                    at = pl.multiple_of(t * PITCH, 8)
                    tiles[pl.ds(at, 8), :] = jnp.zeros((8, TS), F32)
                    tiles[pl.ds(at + 8, TS), :] = tile
                    sums.append(jnp.sum(tile, axis=0, keepdims=True))
                sums = jnp.sum(jnp.concatenate(sums, 0), axis=1, keepdims=True)
                at = pl.multiple_of(side * TILES + first, 8)
                weights[pl.ds(at, 8), :] = jnp.broadcast_to(float(TS * TS) / sums, (8, TS))

        for side, table in ((0, own), (1, other)):
            n = table[12, core].astype(jnp.int32)
            slots[side, 0] = n
            for u in range(UNROLL):
                slots[side, 1 + n + u] = EMPTY
        for tiles in (own_tiles, other_tiles):
            tiles[TILES * PITCH :, :] = jnp.zeros((8, TS), F32)

    def place(entry, side, table, tiles):
        item, k, slot = entry & 255, (entry >> 8) & 15, (entry >> 12) & 3
        t, route = item >> 1, item & 1
        row, col = table[2 + 2 * route, t].astype(jnp.int32), table[3 + 2 * route, t].astype(jnp.int32)
        frac_row, frac_col = table[6 + 2 * route, t], table[7 + 2 * route, t]
        real = jnp.where(entry >= EMPTY, 0.0, 1.0)
        weight = jnp.broadcast_to(weights[pl.ds(side * TILES + t, 1), :], (8, TS))
        scale = weight * real
        if with_meta:
            field = lax.broadcasted_iota(jnp.int32, (8, TS), 0)
            value = jnp.where(field == 1, row.astype(F32), weight)
            value = jnp.where(field == 2, col.astype(F32), value)
            value = jnp.where(field == 3, frac_row, value)
            value = jnp.where(field == 4, frac_col, value)
            value = jnp.where((field < 5) & (lane == 2 * chip + side), value * real, 0.0)
            meta[k * CAP + slot] += value
            scale = scale * weight
        near, far = scale * (1.0 - frac_col), scale * frac_col
        turn, down = (col + TS) & (TS - 1), (row + PAD) & 7
        here = jnp.where(lane >= turn, near, 0.0)
        here_next = jnp.where(lane >= turn + 1, far, 0.0)
        over, over_next = near - here, far - here_next
        start = t * PITCH + 8 - down
        upper, lower = tiles[pl.ds(start, PITCH), :], tiles[pl.ds(start - 1, PITCH), :]
        rows = upper * (1.0 - frac_row) + lower * frac_row
        r0 = pltpu.roll(rows, turn, 1).reshape(PITCH // 8, 8, TS)
        r1 = pltpu.roll(rows, (turn + 1) & (TS - 1), 1).reshape(PITCH // 8, 8, TS)
        left = (r0 * here + r1 * here_next).reshape(PITCH, TS)
        right = (r0 * over + r1 * over_next).reshape(PITCH, TS)
        return left, right, 4 * k + ((col + TS) >> 7), pl.multiple_of(((row + PAD) >> 3) * 8, 8)

    for side, table, tiles in ((0, own, own_tiles), (1, other, other_tiles)):

        @pl.loop(0, (slots[side, 0] + UNROLL - 1) // UNROLL)
        def _(m, side=side, table=table, tiles=tiles):
            for u in range(UNROLL):
                left, right, first, base = place(slots[side, 1 + m * UNROLL + u], side, table, tiles)
                acc[first, pl.ds(base, PITCH), :] += left
                acc[first + 1, pl.ds(base, PITCH), :] += right

    for k in range(16):
        a, b, c, d = k >> 3, (k >> 2) & 1, (k >> 1) & 1, k & 1
        rest = 2 * c + d if with_meta else 2 * d + c
        rows = MAIN if with_meta else PATCH
        left, right = outs[a], outs[2 + b]
        left[4 * b + rest, 0:rows, :] = acc[4 * k + 1, PAD : PAD + rows, :]
        right[4 * a + rest, :, :] = acc[4 * k + 2, PAD : PAD + rows, :]
        if with_meta:
            for slot in range(CAP):
                left[4 * b + rest, MAIN + 8 * slot : MAIN + 8 * slot + 8, :] = meta[k * CAP + slot]

    if with_meta:
        for first in range(2):
            for second in range(2):
                start = pl.multiple_of(PAD + MAIN + PART * quarter(first, second, core), 8)
                for k in range(16):
                    for half in range(2):
                        part = acc[4 * k + 1 + half, pl.ds(start, PART), :]
                        outs[4 + first][second, k, PART * half : PART * (half + 1), :] = part


def warp(with_meta, *args):
    smem, vmem = pl.BlockSpec(memory_space=pltpu.SMEM), pl.BlockSpec(memory_space=pltpu.VMEM)
    left = jax.ShapeDtypeStruct((8, MAIN + META if with_meta else PATCH, TS), F32)
    right = jax.ShapeDtypeStruct((8, MAIN if with_meta else PATCH, TS), F32)
    outs, specs = [left, left, right, right], [vmem] * 4
    if with_meta:
        outs += [jax.ShapeDtypeStruct((2, 16, 2 * PART, TS), F32)] * 2
        specs += [vmem] * 2
    scratch = [pltpu.VMEM((64, 384, TS), F32)]
    if with_meta:
        outs += [jax.ShapeDtypeStruct((2, 128), jnp.int32), jax.ShapeDtypeStruct((2 * TILES, TS), F32)]
        specs += [smem, vmem]
        scratch += [pltpu.VMEM((16 * CAP, 8, TS), F32)] + [pltpu.VMEM((TILES * PITCH + 8, TS), F32)] * 2
    scalars = 2 if with_meta else 3
    return pl.pallas_call(
        functools.partial(warp_kernel, with_meta),
        out_shape=outs,
        in_specs=[smem] * scalars + [vmem] * (len(args) - scalars),
        out_specs=specs,
        scratch_shapes=scratch,
        compiler_params=pltpu.CompilerParams(vmem_limit_bytes=40 << 20),
        cost_estimate=pl.CostEstimate(flops=WARP_COST, bytes_accessed=8 << 20, transcendentals=0),
        name="warp_meta" if with_meta else "warp",
    )(*args)


def cover_kernel(var, got, coadd_var, safe_ref):
    place_of = lax.broadcasted_iota(jnp.int32, (PATCH, TS), 0).astype(F32)

    def cover(offset, shift):
        u = place_of - offset
        lower = jnp.where((u >= 0.0) & (u <= TS - 1.0), 1.0 - shift, 0.0)
        return lower + jnp.where((u >= 1.0) & (u <= float(TS)), shift, 0.0)

    downs, acrosses = [], []
    for slot in range(CAP):
        at = MAIN + 8 * slot
        fields = var[at : at + 8, :] + got[at : at + 8, :]
        weight, row, col, frac_row, frac_col = (fields[f : f + 1, :] for f in range(5))
        down, down_low = split(cover(row, frac_row) * weight)
        across, across_low = split(cover(col, frac_col))
        downs += [down, down_low, down]
        acrosses += [across, across, across_low]
    den = lax.dot_general(
        jnp.concatenate(downs, 1), jnp.concatenate(acrosses, 1), (((1,), (1,)), ((), ())), preferred_element_type=F32
    )
    safe = jnp.maximum(den, 1.0)
    safe_ref[...] = safe
    for half in range(2):
        lo, lanes = half * (MAIN + META), slice(half * TS, (half + 1) * TS)
        part = safe[0:MAIN, lanes]
        coadd_var[0:MAIN, lanes] = (var[lo : lo + MAIN, :] + got[lo : lo + MAIN, :]) / (part * part)
    core = here()[2]
    for first, source in ((0, var), (1, got)):
        for second in range(2):
            rows = pl.ds(pl.multiple_of(MAIN + PART * quarter(first, second, core), 8), PART)
            for half in range(2):
                lo, lanes = 2 * MAIN + META + PART * (2 * second + half), slice(half * TS, (half + 1) * TS)
                part = safe_ref[rows, lanes]
                coadd_var[rows, lanes] = source[lo : lo + PART, :] / (part * part)


def divide_kernel(num, got, safe, coadd):
    for half in range(2):
        rows, lanes = slice(half * PATCH, (half + 1) * PATCH), slice(half * TS, (half + 1) * TS)
        coadd[:, lanes] = (num[rows, :] + got[rows, :]) / safe[:, lanes]


def finish(kernel, name, outs, *args):
    vmem = pl.BlockSpec(memory_space=pltpu.VMEM)
    return pl.pallas_call(
        kernel,
        out_shape=[jax.ShapeDtypeStruct((PATCH, PATCH), F32)] * outs,
        in_specs=[vmem] * len(args),
        out_specs=[vmem] * outs,
        compiler_params=pltpu.CompilerParams(vmem_limit_bytes=8 << 20),
        cost_estimate=pl.CostEstimate(flops=1_000_000_000, bytes_accessed=1 << 20, transcendentals=0),
        name=name,
    )(*args)


EDGES = (((0, 1), (1, 0), (2, 3), (3, 2)), ((1, 2), (2, 1), (3, 0), (0, 3)))


def over_patch(axis, edge):
    pairs = []
    for a, b in EDGES[edge]:
        for other in range(4):
            for core in range(2):
                src, dst = ((a, other), (b, other)) if axis == core else ((other, a), (other, b))
                pairs.append((src[0] * 8 + src[1] * 2 + core, dst[0] * 8 + dst[1] * 2 + core))
    return pairs


def over_visit(edge):
    return [
        (a * 32 + 2 * chip + core, b * 32 + 2 * chip + core)
        for core in range(2)
        for a, b in EDGES[edge ^ core]
        for chip in range(16)
    ]


def combine(var, num):
    def cross(x, axis, edge):
        return lax.ppermute(x, "patch", over_patch(axis, edge))

    def visit(x, edge):
        return lax.ppermute(x, ("visit", "patch"), over_visit(edge))

    def fold(keep, got):
        n = keep.shape[0] // 2
        return keep[:n] + got[:n], keep[n:] + got[n:]

    def after(got, *earlier):
        return lax.optimization_barrier((*got, *earlier))[: len(got)]

    (vl, vl_send, vr, vr_send, vp, vp_send), (nl, nl_send, nr, nr_send) = var, num
    vl_got, vr_got, vp_got = cross(vl_send, 0, 0), cross(vr_send, 0, 1), visit(vp_send, 0)
    nl_got, nr_got = cross(nl_send, 0, 0), cross(nr_send, 0, 1)

    (vl, vl_send), (vr, vr_send) = fold(vl, vl_got), fold(vr, vr_got)
    vp, vp_send = vp[0] + vp_got[0], vp[1] + vp_got[1]
    vl_got, vr_got, vp_got = cross(vl_send, 0, 1), cross(vr_send, 0, 0), visit(vp_send, 1)
    nl_got, nr_got = after((nl_got, nr_got), vl_send, vr_send, vp_send)
    vp, vp_send = fold(vp, vp_got)
    vp, vp_send = fold(vp, cross(vp_send, 0, 0))
    vp = vp + cross(vp_send, 0, 1)

    (nl, nl_send), (nr, nr_send) = fold(nl, nl_got), fold(nr, nr_got)
    nl_got, nr_got = cross(nl_send, 0, 1), cross(nr_send, 0, 0)

    vl_got, vr_got = after((vl_got, vr_got), nl_send, nr_send, vp_send)
    v, v_send = (
        jnp.concatenate([vl[p] + vl_got[p], vr[p] + vr_got[p], vp[p]], 1) for p in (slice(0, 2), slice(2, 4))
    )
    v_got = cross(v_send, 1, 0)

    nl_got, nr_got = after((nl_got, nr_got), vp_send)
    n, n_send = (jnp.concatenate([nl[p] + nl_got[p], nr[p] + nr_got[p]], 1) for p in (slice(0, 2), slice(2, 4)))
    n_got = cross(n_send, 1, 1)

    (n_got,) = after((n_got,), v_send)
    n, n_send = fold(n, n_got)
    (v_got,) = after((v_got,), n_send)
    v, v_send = fold(v, v_got)
    n = n[0] + cross(n_send, 1, 0)[0]
    v = v[0] + cross(v_send, 1, 1)[0]

    n = n + visit(n, 0)
    v_got, main = visit(v, 1), 2 * MAIN + META
    v = jnp.concatenate([v[:main] + v_got[:main], v[main:], v_got[main:]], 0)
    return (v, visit(v, 0)), (n, visit(n, 1))


def shards(image, variance, intersections, boxes, shifts, basis_ids, coefs, taps):
    swap = [(i, i ^ 1) for i in range(32)]
    other_variance = lax.ppermute(variance, "patch", swap)
    table = pack(intersections, boxes, shifts)
    other_table = lax.ppermute(table, "patch", swap)
    matched = match(basis_ids, coefs, taps, image)
    matched, other_table = lax.optimization_barrier((matched, other_table))
    other_matched = lax.ppermute(matched, "patch", swap)
    *var, slots, weights = warp(True, table, other_table, variance, other_variance)
    num = warp(False, slots, table, other_table, weights, matched, other_matched)
    var, num = combine(var, num)
    coadd_var, safe = finish(cover_kernel, "cover", 2, *var)
    (coadd,) = finish(divide_kernel, "divide", 1, *num, safe)
    return coadd, coadd_var


def solution(mesh):
    split_spec = ("visit", "patch")
    in_specs = (
        P(split_spec, None, None),
        P(split_spec, None, None),
        P(split_spec, None),
        P(split_spec, None, None),
        P(split_spec, None, None),
        P(split_spec, None),
        P(split_spec, None),
        P(),
    )
    out_specs = (P("patch", None), P("patch", None))
    return jax.shard_map(shards, mesh=mesh, in_specs=in_specs, out_specs=out_specs, check_vma=False)
```

```python
import functools

import jax
import jax.numpy as jnp
from jax import lax
from jax.experimental import pallas as pl
from jax.experimental.pallas import tpu as pltpu
from jax.sharding import PartitionSpec as P

TS = 128
PATCH = 256
NB = 3
NBASIS = 8
HALF = 20
TILES = 32
ROUTES = 2 * TILES
CAP = 3
META = 24
MAIN = 160
PART = (PATCH - MAIN) // 4
PITCH = TS + 8
PAD = 64
F32 = jnp.float32
BF16 = jnp.bfloat16

EMPTY = 1 << 24
UNROLL = 8
MATCH_UNROLL = 16
CHUNKS = 2
MATCH_COST = 100_000_000_000
WARP_COST = 10_000_000_000


def split(x):
    high = x.astype(BF16)
    return high, (x - high.astype(F32)).astype(BF16)


def here():
    patch = lax.axis_index("patch")
    z, y = patch >> 3, (patch >> 1) & 3
    return z, y, patch & 1, lax.axis_index("visit") * 16 + z * 4 + y


def quarter(first, second, core):
    visit = lax.axis_index("visit")
    edges = jnp.where(core == 0, first + 2 * second, 2 * first + second)
    return (visit ^ (visit >> 1)) ^ edges


def place_code(z, y, core):
    first, second = jnp.where(core == 0, z, y), jnp.where(core == 0, y, z)
    first, second = first ^ (first >> 1), second ^ (second >> 1)
    return ((first & 1) << 3) | ((first >> 1) << 2) | ((second & 1) << 1) | (second >> 1)


def pack_kernel(intersections, boxes, shifts, out):
    z, y, _, _ = here()
    out[...] = jnp.zeros_like(out)
    earlier_item = lax.broadcasted_iota(jnp.int32, (TILES, TILES), 0)
    item = lax.broadcasted_iota(jnp.int32, (TILES, TILES), 1)
    dest = [intersections[route : route + 1, :] for route in range(2)]

    def earlier(rows):
        columns = [jnp.sum(jnp.where(earlier_item == item, row, 0), axis=1, keepdims=True) for row in rows]
        counts = []
        for route, row in enumerate(rows):
            same = jnp.where((columns[route] == row) & (earlier_item < item), 1, 0)
            if route == 1:
                same = same + jnp.where(columns[0] == row, 1, 0)
            counts.append(jnp.sum(same, axis=0, keepdims=True))
        return counts

    slots, places = earlier(dest), earlier([d & 1 for d in dest])
    for route in range(2):
        d = dest[route]
        code = place_code(d >> 3, (d >> 1) & 3, d & 1) ^ place_code(z, y, d & 1)
        out[route : route + 1, 0:TILES] = (code + (slots[route] << 4) + ((d & 1) << 8)).astype(F32)
        out[10 + route : 11 + route, 0:TILES] = places[route].astype(F32)
        out[2 + 2 * route : 4 + 2 * route, 0:TILES] = boxes[route].astype(F32)
        out[6 + 2 * route : 8 + 2 * route, 0:TILES] = shifts[route]
    second = jnp.sum(intersections[...] & 1).astype(F32)
    lane = lax.broadcasted_iota(jnp.int32, (1, TS), 1)
    out[12:13, :] = jnp.where(lane == 0, ROUTES - second, second)


def pack(intersections, boxes, shifts):
    vmem = pl.BlockSpec(memory_space=pltpu.VMEM)
    return pl.pallas_call(
        pack_kernel,
        out_shape=jax.ShapeDtypeStruct((16, TS), F32),
        in_specs=[vmem] * 3,
        out_specs=vmem,
        name="pack",
    )(intersections.T, boxes.transpose(1, 2, 0), shifts.transpose(1, 2, 0))


def match_kernel(
    ids_hbm, coefs_hbm, taps_hbm, image_hbm, out, basis_ids, coefs, taps, line, row_mats, col_mats, image, sems, small_sems
):
    size = TILES // CHUNKS
    copies = [
        pltpu.make_async_copy(image_hbm.at[pl.ds(c * size, size)], image.at[pl.ds(c * size, size)], sems.at[c])
        for c in range(CHUNKS)
    ]
    small = [
        pltpu.make_async_copy(source, target, small_sems.at[i])
        for i, (source, target) in enumerate(((taps_hbm, taps), (ids_hbm, basis_ids), (coefs_hbm, coefs)))
    ]
    for copy in small + copies:
        copy.start()
    i = lax.broadcasted_iota(jnp.int32, (TS, TS), 0)
    k = lax.broadcasted_iota(jnp.int32, (TS, TS), 1)
    near = jnp.abs(i - k) <= HALF
    none = jnp.zeros((TS, TS), BF16)
    line[...] = jnp.zeros_like(line)
    for copy in small:
        copy.wait()
    for b in range(NBASIS):
        line[2 * b : 2 * b + 2, 0 : 2 * HALF + 1] = taps[b]
    line[...] = pltpu.roll(line[...], TS - HALF, 1)

    def square(high, low):
        return jnp.concatenate([jnp.concatenate([high, low], 1), jnp.concatenate([high, none], 1)], 0)

    for b in range(NBASIS):
        for side in range(2):
            band = jnp.broadcast_to(line[2 * b + side : 2 * b + side + 1, :], (TS, TS))
            band = jnp.where(near, pltpu.roll(band, 0, 1, stride=1, stride_axis=0), 0.0)
            if side == 0:
                row_mats[b] = jnp.concatenate(split(band.T), 1)
            else:
                col_mats[b] = square(*split(band))

    out[TILES * PITCH :, :] = jnp.zeros((8, TS), F32)
    for c in range(CHUNKS):
        copies[c].wait()

        @pl.loop(c * size, (c + 1) * size, step=MATCH_UNROLL)
        def _(first):
            for t in [first + u for u in range(MATCH_UNROLL)]:
                pixels = square(*split(image[t]))
                bases = [basis_ids[j, t] for j in range(NB)]
                bands = jnp.concatenate([row_mats[basis] for basis in bases], 0)
                p = jnp.dot(bands, pixels, preferred_element_type=F32)
                p = p[:, :TS] + p[:, TS:]
                parts = [jnp.concatenate(split(p[TS * j : TS * (j + 1)] * coefs[j, t]), 1) for j in range(NB)]
                bands = jnp.concatenate([col_mats[basis] for basis in bases], 0)
                total = jnp.dot(jnp.concatenate(parts, 1), bands, preferred_element_type=F32)
                at = pl.multiple_of(t * PITCH, 8)
                out[pl.ds(at, 8), :] = jnp.zeros((8, TS), F32)
                out[pl.ds(at + 8, TS), :] = total[:, :TS] + total[:, TS:]


def match(basis_ids, coefs, taps, image):
    vmem, hbm = pl.BlockSpec(memory_space=pltpu.VMEM), pl.BlockSpec(memory_space=pltpu.HBM)
    return pl.pallas_call(
        match_kernel,
        out_shape=jax.ShapeDtypeStruct((TILES * PITCH + 8, TS), F32),
        in_specs=[hbm] * 4,
        out_specs=vmem,
        scratch_shapes=[
            pltpu.SMEM((NB, TILES), jnp.int32),
            pltpu.SMEM((NB, TILES), F32),
            pltpu.VMEM((NBASIS, 2, 2 * HALF + 1), F32),
            pltpu.VMEM((2 * NBASIS, TS), F32),
            pltpu.VMEM((NBASIS, TS, 2 * TS), BF16),
            pltpu.VMEM((NBASIS, 2 * TS, 2 * TS), BF16),
            pltpu.VMEM((TILES, TS, TS), F32),
            pltpu.SemaphoreType.DMA((CHUNKS,)),
            pltpu.SemaphoreType.DMA((3,)),
        ],
        compiler_params=pltpu.CompilerParams(vmem_limit_bytes=40 << 20),
        cost_estimate=pl.CostEstimate(flops=MATCH_COST, bytes_accessed=6 << 20, transcendentals=0),
        name="match",
    )(*(pltpu.with_memory_space_constraint(x, pltpu.HBM) for x in (basis_ids.T, coefs.T, taps, image)))


def warp_kernel(with_meta, *refs):
    if with_meta:
        own, other, own_raw, other_raw = refs[:4]
        outs, slots, weights = refs[4:10], refs[10], refs[11]
        acc, meta, own_tiles, other_tiles = refs[12:]
    else:
        slots, own, other, weights, own_tiles, other_tiles = refs[:6]
        outs, acc = refs[6:10], refs[10]
    lane = lax.broadcasted_iota(jnp.int32, (8, TS), 1)
    for k in range(16):
        for side in (1, 2):
            acc[4 * k + side, PAD : PAD + PATCH, :] = jnp.zeros((PATCH, TS), F32)

    if with_meta:
        _, _, core, chip = here()
        meta[...] = jnp.zeros_like(meta)

        @pl.loop(0, TILES, step=8)
        def _(first):
            for side, table, raw, tiles in ((0, own, own_raw, own_tiles), (1, other, other_raw, other_tiles)):
                for route in range(2):
                    for t in [first + u for u in range(8)]:
                        what = table[route, t].astype(jnp.int32)
                        at = jnp.where((what >> 8) == core, table[10 + route, t].astype(jnp.int32) + 1, 127)
                        slots[side, at] = (what << 8) + (2 * t + route)
                sums = []
                for t in [first + u for u in range(8)]:
                    tile = raw[t]
                    at = pl.multiple_of(t * PITCH, 8)
                    tiles[pl.ds(at, 8), :] = jnp.zeros((8, TS), F32)
                    tiles[pl.ds(at + 8, TS), :] = tile
                    sums.append(jnp.sum(tile, axis=0, keepdims=True))
                sums = jnp.sum(jnp.concatenate(sums, 0), axis=1, keepdims=True)
                at = pl.multiple_of(side * TILES + first, 8)
                weights[pl.ds(at, 8), :] = jnp.broadcast_to(float(TS * TS) / sums, (8, TS))

        for side, table in ((0, own), (1, other)):
            n = table[12, core].astype(jnp.int32)
            slots[side, 0] = n
            for u in range(UNROLL):
                slots[side, 1 + n + u] = EMPTY
        for tiles in (own_tiles, other_tiles):
            tiles[TILES * PITCH :, :] = jnp.zeros((8, TS), F32)

    def place(entry, side, table, tiles):
        item, k, slot = entry & 255, (entry >> 8) & 15, (entry >> 12) & 3
        t, route = item >> 1, item & 1
        row, col = table[2 + 2 * route, t].astype(jnp.int32), table[3 + 2 * route, t].astype(jnp.int32)
        frac_row, frac_col = table[6 + 2 * route, t], table[7 + 2 * route, t]
        real = jnp.where(entry >= EMPTY, 0.0, 1.0)
        weight = jnp.broadcast_to(weights[pl.ds(side * TILES + t, 1), :], (8, TS))
        scale = weight * real
        if with_meta:
            field = lax.broadcasted_iota(jnp.int32, (8, TS), 0)
            value = jnp.where(field == 1, row.astype(F32), weight)
            value = jnp.where(field == 2, col.astype(F32), value)
            value = jnp.where(field == 3, frac_row, value)
            value = jnp.where(field == 4, frac_col, value)
            value = jnp.where((field < 5) & (lane == 2 * chip + side), value * real, 0.0)
            meta[k * CAP + slot] += value
            scale = scale * weight
        near, far = scale * (1.0 - frac_col), scale * frac_col
        turn, down = (col + TS) & (TS - 1), (row + PAD) & 7
        here = jnp.where(lane >= turn, near, 0.0)
        here_next = jnp.where(lane >= turn + 1, far, 0.0)
        over, over_next = near - here, far - here_next
        start = t * PITCH + 8 - down
        upper, lower = tiles[pl.ds(start, PITCH), :], tiles[pl.ds(start - 1, PITCH), :]
        rows = upper * (1.0 - frac_row) + lower * frac_row
        r0 = pltpu.roll(rows, turn, 1).reshape(PITCH // 8, 8, TS)
        r1 = pltpu.roll(rows, (turn + 1) & (TS - 1), 1).reshape(PITCH // 8, 8, TS)
        left = (r0 * here + r1 * here_next).reshape(PITCH, TS)
        right = (r0 * over + r1 * over_next).reshape(PITCH, TS)
        return left, right, 4 * k + ((col + TS) >> 7), pl.multiple_of(((row + PAD) >> 3) * 8, 8)

    for side, table, tiles in ((0, own, own_tiles), (1, other, other_tiles)):

        @pl.loop(0, (slots[side, 0] + UNROLL - 1) // UNROLL)
        def _(m, side=side, table=table, tiles=tiles):
            for u in range(UNROLL):
                left, right, first, base = place(slots[side, 1 + m * UNROLL + u], side, table, tiles)
                acc[first, pl.ds(base, PITCH), :] += left
                acc[first + 1, pl.ds(base, PITCH), :] += right

    for k in range(16):
        a, b, c, d = k >> 3, (k >> 2) & 1, (k >> 1) & 1, k & 1
        rest = 2 * c + d if with_meta else 2 * d + c
        rows = MAIN if with_meta else PATCH
        left, right = outs[a], outs[2 + b]
        left[4 * b + rest, 0:rows, :] = acc[4 * k + 1, PAD : PAD + rows, :]
        right[4 * a + rest, :, :] = acc[4 * k + 2, PAD : PAD + rows, :]
        if with_meta:
            for slot in range(CAP):
                left[4 * b + rest, MAIN + 8 * slot : MAIN + 8 * slot + 8, :] = meta[k * CAP + slot]

    if with_meta:
        for first in range(2):
            for second in range(2):
                start = pl.multiple_of(PAD + MAIN + PART * quarter(first, second, core), 8)
                for k in range(16):
                    for half in range(2):
                        part = acc[4 * k + 1 + half, pl.ds(start, PART), :]
                        outs[4 + first][second, k, PART * half : PART * (half + 1), :] = part


def warp(with_meta, *args):
    smem, vmem = pl.BlockSpec(memory_space=pltpu.SMEM), pl.BlockSpec(memory_space=pltpu.VMEM)
    left = jax.ShapeDtypeStruct((8, MAIN + META if with_meta else PATCH, TS), F32)
    right = jax.ShapeDtypeStruct((8, MAIN if with_meta else PATCH, TS), F32)
    outs, specs = [left, left, right, right], [vmem] * 4
    if with_meta:
        outs += [jax.ShapeDtypeStruct((2, 16, 2 * PART, TS), F32)] * 2
        specs += [vmem] * 2
    scratch = [pltpu.VMEM((64, 384, TS), F32)]
    if with_meta:
        outs += [jax.ShapeDtypeStruct((2, 128), jnp.int32), jax.ShapeDtypeStruct((2 * TILES, TS), F32)]
        specs += [smem, vmem]
        scratch += [pltpu.VMEM((16 * CAP, 8, TS), F32)] + [pltpu.VMEM((TILES * PITCH + 8, TS), F32)] * 2
    scalars = 2 if with_meta else 3
    return pl.pallas_call(
        functools.partial(warp_kernel, with_meta),
        out_shape=outs,
        in_specs=[smem] * scalars + [vmem] * (len(args) - scalars),
        out_specs=specs,
        scratch_shapes=scratch,
        compiler_params=pltpu.CompilerParams(vmem_limit_bytes=40 << 20),
        cost_estimate=pl.CostEstimate(flops=WARP_COST, bytes_accessed=8 << 20, transcendentals=0),
        name="warp_meta" if with_meta else "warp",
    )(*args)


def cover_kernel(var, got, coadd_var, safe_ref):
    place_of = lax.broadcasted_iota(jnp.int32, (PATCH, TS), 0).astype(F32)

    def cover(offset, shift):
        u = place_of - offset
        lower = jnp.where((u >= 0.0) & (u <= TS - 1.0), 1.0 - shift, 0.0)
        return lower + jnp.where((u >= 1.0) & (u <= float(TS)), shift, 0.0)

    downs, acrosses = [], []
    for slot in range(CAP):
        at = MAIN + 8 * slot
        fields = var[at : at + 8, :] + got[at : at + 8, :]
        weight, row, col, frac_row, frac_col = (fields[f : f + 1, :] for f in range(5))
        down, down_low = split(cover(row, frac_row) * weight)
        across, across_low = split(cover(col, frac_col))
        downs += [down, down_low, down]
        acrosses += [across, across, across_low]
    den = lax.dot_general(
        jnp.concatenate(downs, 1), jnp.concatenate(acrosses, 1), (((1,), (1,)), ((), ())), preferred_element_type=F32
    )
    safe = jnp.maximum(den, 1.0)
    safe_ref[...] = safe
    for half in range(2):
        lo, lanes = half * (MAIN + META), slice(half * TS, (half + 1) * TS)
        part = safe[0:MAIN, lanes]
        coadd_var[0:MAIN, lanes] = (var[lo : lo + MAIN, :] + got[lo : lo + MAIN, :]) / (part * part)
    core = here()[2]
    for first, source in ((0, var), (1, got)):
        for second in range(2):
            rows = pl.ds(pl.multiple_of(MAIN + PART * quarter(first, second, core), 8), PART)
            for half in range(2):
                lo, lanes = 2 * MAIN + META + PART * (2 * second + half), slice(half * TS, (half + 1) * TS)
                part = safe_ref[rows, lanes]
                coadd_var[rows, lanes] = source[lo : lo + PART, :] / (part * part)


def divide_kernel(num, got, safe, coadd):
    for half in range(2):
        rows, lanes = slice(half * PATCH, (half + 1) * PATCH), slice(half * TS, (half + 1) * TS)
        coadd[:, lanes] = (num[rows, :] + got[rows, :]) / safe[:, lanes]


def finish(kernel, name, outs, *args):
    vmem = pl.BlockSpec(memory_space=pltpu.VMEM)
    return pl.pallas_call(
        kernel,
        out_shape=[jax.ShapeDtypeStruct((PATCH, PATCH), F32)] * outs,
        in_specs=[vmem] * len(args),
        out_specs=[vmem] * outs,
        compiler_params=pltpu.CompilerParams(vmem_limit_bytes=8 << 20),
        cost_estimate=pl.CostEstimate(flops=1_000_000_000, bytes_accessed=1 << 20, transcendentals=0),
        name=name,
    )(*args)


EDGES = (((0, 1), (1, 0), (2, 3), (3, 2)), ((1, 2), (2, 1), (3, 0), (0, 3)))


def over_patch(axis, edge):
    pairs = []
    for a, b in EDGES[edge]:
        for other in range(4):
            for core in range(2):
                src, dst = ((a, other), (b, other)) if axis == core else ((other, a), (other, b))
                pairs.append((src[0] * 8 + src[1] * 2 + core, dst[0] * 8 + dst[1] * 2 + core))
    return pairs


def over_visit(edge):
    return [
        (a * 32 + 2 * chip + core, b * 32 + 2 * chip + core)
        for core in range(2)
        for a, b in EDGES[edge ^ core]
        for chip in range(16)
    ]


def combine(var, num):
    def cross(x, axis, edge):
        return lax.ppermute(x, "patch", over_patch(axis, edge))

    def visit(x, edge):
        return lax.ppermute(x, ("visit", "patch"), over_visit(edge))

    def fold(keep, got):
        n = keep.shape[0] // 2
        return keep[:n] + got[:n], keep[n:] + got[n:]

    def after(got, *earlier):
        return lax.optimization_barrier((*got, *earlier))[: len(got)]

    (vl, vl_send, vr, vr_send, vp, vp_send), (nl, nl_send, nr, nr_send) = var, num
    vl_got, vr_got, vp_got = cross(vl_send, 0, 0), cross(vr_send, 0, 1), visit(vp_send, 0)
    nl_got, nr_got = cross(nl_send, 0, 0), cross(nr_send, 0, 1)

    (vl, vl_send), (vr, vr_send) = fold(vl, vl_got), fold(vr, vr_got)
    vp, vp_send = vp[0] + vp_got[0], vp[1] + vp_got[1]
    vl_got, vr_got, vp_got = cross(vl_send, 0, 1), cross(vr_send, 0, 0), visit(vp_send, 1)
    nl_got, nr_got = after((nl_got, nr_got), vl_send, vr_send, vp_send)
    vp, vp_send = fold(vp, vp_got)
    vp, vp_send = fold(vp, cross(vp_send, 0, 0))
    vp = vp + cross(vp_send, 0, 1)

    (nl, nl_send), (nr, nr_send) = fold(nl, nl_got), fold(nr, nr_got)
    nl_got, nr_got = cross(nl_send, 0, 1), cross(nr_send, 0, 0)

    vl_got, vr_got = after((vl_got, vr_got), nl_send, nr_send, vp_send)
    v, v_send = (
        jnp.concatenate([vl[p] + vl_got[p], vr[p] + vr_got[p], vp[p]], 1) for p in (slice(0, 2), slice(2, 4))
    )
    v_got = cross(v_send, 1, 0)

    nl_got, nr_got = after((nl_got, nr_got), vp_send)
    n, n_send = (jnp.concatenate([nl[p] + nl_got[p], nr[p] + nr_got[p]], 1) for p in (slice(0, 2), slice(2, 4)))
    n_got = cross(n_send, 1, 1)

    (n_got,) = after((n_got,), v_send)
    n, n_send = fold(n, n_got)
    (v_got,) = after((v_got,), n_send)
    v, v_send = fold(v, v_got)
    n = n[0] + cross(n_send, 1, 0)[0]
    (v_got,) = after((cross(v_send, 1, 1),), n)
    v = v[0] + v_got[0]

    n = n + visit(n, 0)
    v_got, main = visit(v, 1), 2 * MAIN + META
    v = jnp.concatenate([v[:main] + v_got[:main], v[main:], v_got[main:]], 0)
    return (v, visit(v, 0)), (n, visit(n, 1))


def shards(image, variance, intersections, boxes, shifts, basis_ids, coefs, taps):
    swap = [(i, i ^ 1) for i in range(32)]
    other_variance = lax.ppermute(variance, "patch", swap)
    table = pack(intersections, boxes, shifts)
    other_table = lax.ppermute(table, "patch", swap)
    matched = match(basis_ids, coefs, taps, image)
    matched, other_table = lax.optimization_barrier((matched, other_table))
    other_matched = lax.ppermute(matched, "patch", swap)
    *var, slots, weights = warp(True, table, other_table, variance, other_variance)
    num = warp(False, slots, table, other_table, weights, matched, other_matched)
    var, num = combine(var, num)
    coadd_var, safe = finish(cover_kernel, "cover", 2, *var)
    (coadd,) = finish(divide_kernel, "divide", 1, *num, safe)
    return coadd, coadd_var


def solution(mesh):
    split_spec = ("visit", "patch")
    in_specs = (
        P(split_spec, None, None),
        P(split_spec, None, None),
        P(split_spec, None),
        P(split_spec, None, None),
        P(split_spec, None, None),
        P(split_spec, None),
        P(split_spec, None),
        P(),
    )
    out_specs = (P("patch", None), P("patch", None))
    return jax.shard_map(shards, mesh=mesh, in_specs=in_specs, out_specs=out_specs, check_vma=False)
```

```python
import functools

import jax
import jax.numpy as jnp
from jax import lax
from jax.experimental import pallas as pl
from jax.experimental.pallas import tpu as pltpu
from jax.sharding import PartitionSpec as P

TS = 128
PATCH = 256
NB = 3
NBASIS = 8
HALF = 20
TILES = 32
ROUTES = 2 * TILES
CAP = 3
META = 24
MAIN = 160
PART = (PATCH - MAIN) // 4
PITCH = TS + 8
PAD = 64
F32 = jnp.float32
BF16 = jnp.bfloat16

EMPTY = 1 << 24
UNROLL = 12
MATCH_UNROLL = 16
CHUNKS = 2
MATCH_COST = 100_000_000_000
WARP_COST = 10_000_000_000


def split(x):
    high = x.astype(BF16)
    return high, (x - high.astype(F32)).astype(BF16)


def here():
    patch = lax.axis_index("patch")
    z, y = patch >> 3, (patch >> 1) & 3
    return z, y, patch & 1, lax.axis_index("visit") * 16 + z * 4 + y


def quarter(first, second, core):
    visit = lax.axis_index("visit")
    edges = jnp.where(core == 0, first + 2 * second, 2 * first + second)
    return (visit ^ (visit >> 1)) ^ edges


def place_code(z, y, core):
    first, second = jnp.where(core == 0, z, y), jnp.where(core == 0, y, z)
    first, second = first ^ (first >> 1), second ^ (second >> 1)
    return ((first & 1) << 3) | ((first >> 1) << 2) | ((second & 1) << 1) | (second >> 1)


def pack_kernel(intersections, boxes, shifts, out):
    z, y, _, _ = here()
    out[...] = jnp.zeros_like(out)
    earlier_item = lax.broadcasted_iota(jnp.int32, (TILES, TILES), 0)
    item = lax.broadcasted_iota(jnp.int32, (TILES, TILES), 1)
    dest = [intersections[route : route + 1, :] for route in range(2)]

    def earlier(rows):
        columns = [jnp.sum(jnp.where(earlier_item == item, row, 0), axis=1, keepdims=True) for row in rows]
        counts = []
        for route, row in enumerate(rows):
            same = jnp.where((columns[route] == row) & (earlier_item < item), 1, 0)
            if route == 1:
                same = same + jnp.where(columns[0] == row, 1, 0)
            counts.append(jnp.sum(same, axis=0, keepdims=True))
        return counts

    slots, places = earlier(dest), earlier([d & 1 for d in dest])
    for route in range(2):
        d = dest[route]
        code = place_code(d >> 3, (d >> 1) & 3, d & 1) ^ place_code(z, y, d & 1)
        out[route : route + 1, 0:TILES] = (code + (slots[route] << 4) + ((d & 1) << 8)).astype(F32)
        out[10 + route : 11 + route, 0:TILES] = places[route].astype(F32)
        out[2 + 2 * route : 4 + 2 * route, 0:TILES] = boxes[route].astype(F32)
        out[6 + 2 * route : 8 + 2 * route, 0:TILES] = shifts[route]
    second = jnp.sum(intersections[...] & 1).astype(F32)
    lane = lax.broadcasted_iota(jnp.int32, (1, TS), 1)
    out[12:13, :] = jnp.where(lane == 0, ROUTES - second, second)


def pack(intersections, boxes, shifts):
    vmem = pl.BlockSpec(memory_space=pltpu.VMEM)
    return pl.pallas_call(
        pack_kernel,
        out_shape=jax.ShapeDtypeStruct((16, TS), F32),
        in_specs=[vmem] * 3,
        out_specs=vmem,
        name="pack",
    )(intersections.T, boxes.transpose(1, 2, 0), shifts.transpose(1, 2, 0))


def match_kernel(
    ids_hbm, coefs_hbm, taps_hbm, image_hbm, out, basis_ids, coefs, taps, line, row_mats, col_mats, image, sems, small_sems
):
    size = TILES // CHUNKS
    copies = [
        pltpu.make_async_copy(image_hbm.at[pl.ds(c * size, size)], image.at[pl.ds(c * size, size)], sems.at[c])
        for c in range(CHUNKS)
    ]
    small = [
        pltpu.make_async_copy(source, target, small_sems.at[i])
        for i, (source, target) in enumerate(((taps_hbm, taps), (ids_hbm, basis_ids), (coefs_hbm, coefs)))
    ]
    for copy in small + copies:
        copy.start()
    i = lax.broadcasted_iota(jnp.int32, (TS, TS), 0)
    k = lax.broadcasted_iota(jnp.int32, (TS, TS), 1)
    near = jnp.abs(i - k) <= HALF
    none = jnp.zeros((TS, TS), BF16)
    line[...] = jnp.zeros_like(line)
    for copy in small:
        copy.wait()
    for b in range(NBASIS):
        line[2 * b : 2 * b + 2, 0 : 2 * HALF + 1] = taps[b]
    line[...] = pltpu.roll(line[...], TS - HALF, 1)

    def square(high, low):
        return jnp.concatenate([jnp.concatenate([high, low], 1), jnp.concatenate([high, none], 1)], 0)

    for b in range(NBASIS):
        for side in range(2):
            band = jnp.broadcast_to(line[2 * b + side : 2 * b + side + 1, :], (TS, TS))
            band = jnp.where(near, pltpu.roll(band, 0, 1, stride=1, stride_axis=0), 0.0)
            if side == 0:
                row_mats[b] = jnp.concatenate(split(band.T), 1)
            else:
                col_mats[b] = square(*split(band))

    out[TILES * PITCH :, :] = jnp.zeros((8, TS), F32)
    for c in range(CHUNKS):
        copies[c].wait()

        @pl.loop(c * size, (c + 1) * size, step=MATCH_UNROLL)
        def _(first):
            for t in [first + u for u in range(MATCH_UNROLL)]:
                pixels = square(*split(image[t]))
                bases = [basis_ids[j, t] for j in range(NB)]
                bands = jnp.concatenate([row_mats[basis] for basis in bases], 0)
                p = jnp.dot(bands, pixels, preferred_element_type=F32)
                p = p[:, :TS] + p[:, TS:]
                parts = [jnp.concatenate(split(p[TS * j : TS * (j + 1)] * coefs[j, t]), 1) for j in range(NB)]
                bands = jnp.concatenate([col_mats[basis] for basis in bases], 0)
                total = jnp.dot(jnp.concatenate(parts, 1), bands, preferred_element_type=F32)
                at = pl.multiple_of(t * PITCH, 8)
                out[pl.ds(at, 8), :] = jnp.zeros((8, TS), F32)
                out[pl.ds(at + 8, TS), :] = total[:, :TS] + total[:, TS:]


def match(basis_ids, coefs, taps, image):
    vmem, hbm = pl.BlockSpec(memory_space=pltpu.VMEM), pl.BlockSpec(memory_space=pltpu.HBM)
    return pl.pallas_call(
        match_kernel,
        out_shape=jax.ShapeDtypeStruct((TILES * PITCH + 8, TS), F32),
        in_specs=[hbm] * 4,
        out_specs=vmem,
        scratch_shapes=[
            pltpu.SMEM((NB, TILES), jnp.int32),
            pltpu.SMEM((NB, TILES), F32),
            pltpu.VMEM((NBASIS, 2, 2 * HALF + 1), F32),
            pltpu.VMEM((2 * NBASIS, TS), F32),
            pltpu.VMEM((NBASIS, TS, 2 * TS), BF16),
            pltpu.VMEM((NBASIS, 2 * TS, 2 * TS), BF16),
            pltpu.VMEM((TILES, TS, TS), F32),
            pltpu.SemaphoreType.DMA((CHUNKS,)),
            pltpu.SemaphoreType.DMA((3,)),
        ],
        compiler_params=pltpu.CompilerParams(vmem_limit_bytes=40 << 20),
        cost_estimate=pl.CostEstimate(flops=MATCH_COST, bytes_accessed=6 << 20, transcendentals=0),
        name="match",
    )(*(pltpu.with_memory_space_constraint(x, pltpu.HBM) for x in (basis_ids.T, coefs.T, taps, image)))


def warp_kernel(with_meta, *refs):
    if with_meta:
        own, other, own_raw, other_raw = refs[:4]
        outs, slots, weights = refs[4:10], refs[10], refs[11]
        acc, meta, own_tiles, other_tiles = refs[12:]
    else:
        slots, own, other, weights, own_tiles, other_tiles = refs[:6]
        outs, acc = refs[6:10], refs[10]
    lane = lax.broadcasted_iota(jnp.int32, (8, TS), 1)
    for k in range(16):
        for side in (1, 2):
            acc[4 * k + side, PAD : PAD + PATCH, :] = jnp.zeros((PATCH, TS), F32)

    if with_meta:
        _, _, core, chip = here()
        meta[...] = jnp.zeros_like(meta)

        @pl.loop(0, TILES, step=8)
        def _(first):
            for side, table, raw, tiles in ((0, own, own_raw, own_tiles), (1, other, other_raw, other_tiles)):
                for route in range(2):
                    for t in [first + u for u in range(8)]:
                        what = table[route, t].astype(jnp.int32)
                        at = jnp.where((what >> 8) == core, table[10 + route, t].astype(jnp.int32) + 1, 127)
                        slots[side, at] = (what << 8) + (2 * t + route)
                sums = []
                for t in [first + u for u in range(8)]:
                    tile = raw[t]
                    at = pl.multiple_of(t * PITCH, 8)
                    tiles[pl.ds(at, 8), :] = jnp.zeros((8, TS), F32)
                    tiles[pl.ds(at + 8, TS), :] = tile
                    sums.append(jnp.sum(tile, axis=0, keepdims=True))
                sums = jnp.sum(jnp.concatenate(sums, 0), axis=1, keepdims=True)
                at = pl.multiple_of(side * TILES + first, 8)
                weights[pl.ds(at, 8), :] = jnp.broadcast_to(float(TS * TS) / sums, (8, TS))

        for side, table in ((0, own), (1, other)):
            n = table[12, core].astype(jnp.int32)
            slots[side, 0] = n
            for u in range(UNROLL):
                slots[side, 1 + n + u] = EMPTY
        for tiles in (own_tiles, other_tiles):
            tiles[TILES * PITCH :, :] = jnp.zeros((8, TS), F32)

    def place(entry, side, table, tiles):
        item, k, slot = entry & 255, (entry >> 8) & 15, (entry >> 12) & 3
        t, route = item >> 1, item & 1
        row, col = table[2 + 2 * route, t].astype(jnp.int32), table[3 + 2 * route, t].astype(jnp.int32)
        frac_row, frac_col = table[6 + 2 * route, t], table[7 + 2 * route, t]
        real = jnp.where(entry >= EMPTY, 0.0, 1.0)
        weight = jnp.broadcast_to(weights[pl.ds(side * TILES + t, 1), :], (8, TS))
        scale = weight * real
        if with_meta:
            field = lax.broadcasted_iota(jnp.int32, (8, TS), 0)
            value = jnp.where(field == 1, row.astype(F32), weight)
            value = jnp.where(field == 2, col.astype(F32), value)
            value = jnp.where(field == 3, frac_row, value)
            value = jnp.where(field == 4, frac_col, value)
            value = jnp.where((field < 5) & (lane == 2 * chip + side), value * real, 0.0)
            meta[k * CAP + slot] += value
            scale = scale * weight
        near, far = scale * (1.0 - frac_col), scale * frac_col
        turn, down = (col + TS) & (TS - 1), (row + PAD) & 7
        here = jnp.where(lane >= turn, near, 0.0)
        here_next = jnp.where(lane >= turn + 1, far, 0.0)
        over, over_next = near - here, far - here_next
        start = t * PITCH + 8 - down
        upper, lower = tiles[pl.ds(start, PITCH), :], tiles[pl.ds(start - 1, PITCH), :]
        rows = upper * (1.0 - frac_row) + lower * frac_row
        r0 = pltpu.roll(rows, turn, 1).reshape(PITCH // 8, 8, TS)
        r1 = pltpu.roll(rows, (turn + 1) & (TS - 1), 1).reshape(PITCH // 8, 8, TS)
        left = (r0 * here + r1 * here_next).reshape(PITCH, TS)
        right = (r0 * over + r1 * over_next).reshape(PITCH, TS)
        return left, right, 4 * k + ((col + TS) >> 7), pl.multiple_of(((row + PAD) >> 3) * 8, 8)

    for side, table, tiles in ((0, own, own_tiles), (1, other, other_tiles)):

        @pl.loop(0, (slots[side, 0] + UNROLL - 1) // UNROLL)
        def _(m, side=side, table=table, tiles=tiles):
            for u in range(UNROLL):
                left, right, first, base = place(slots[side, 1 + m * UNROLL + u], side, table, tiles)
                acc[first, pl.ds(base, PITCH), :] += left
                acc[first + 1, pl.ds(base, PITCH), :] += right

    for k in range(16):
        a, b, c, d = k >> 3, (k >> 2) & 1, (k >> 1) & 1, k & 1
        rest = 2 * c + d if with_meta else 2 * d + c
        rows = MAIN if with_meta else PATCH
        left, right = outs[a], outs[2 + b]
        left[4 * b + rest, 0:rows, :] = acc[4 * k + 1, PAD : PAD + rows, :]
        right[4 * a + rest, :, :] = acc[4 * k + 2, PAD : PAD + rows, :]
        if with_meta:
            for slot in range(CAP):
                left[4 * b + rest, MAIN + 8 * slot : MAIN + 8 * slot + 8, :] = meta[k * CAP + slot]

    if with_meta:
        for first in range(2):
            for second in range(2):
                start = pl.multiple_of(PAD + MAIN + PART * quarter(first, second, core), 8)
                for k in range(16):
                    for half in range(2):
                        part = acc[4 * k + 1 + half, pl.ds(start, PART), :]
                        outs[4 + first][second, k, PART * half : PART * (half + 1), :] = part


def warp(with_meta, *args):
    smem, vmem = pl.BlockSpec(memory_space=pltpu.SMEM), pl.BlockSpec(memory_space=pltpu.VMEM)
    left = jax.ShapeDtypeStruct((8, MAIN + META if with_meta else PATCH, TS), F32)
    right = jax.ShapeDtypeStruct((8, MAIN if with_meta else PATCH, TS), F32)
    outs, specs = [left, left, right, right], [vmem] * 4
    if with_meta:
        outs += [jax.ShapeDtypeStruct((2, 16, 2 * PART, TS), F32)] * 2
        specs += [vmem] * 2
    scratch = [pltpu.VMEM((64, 384, TS), F32)]
    if with_meta:
        outs += [jax.ShapeDtypeStruct((2, 128), jnp.int32), jax.ShapeDtypeStruct((2 * TILES, TS), F32)]
        specs += [smem, vmem]
        scratch += [pltpu.VMEM((16 * CAP, 8, TS), F32)] + [pltpu.VMEM((TILES * PITCH + 8, TS), F32)] * 2
    scalars = 2 if with_meta else 3
    return pl.pallas_call(
        functools.partial(warp_kernel, with_meta),
        out_shape=outs,
        in_specs=[smem] * scalars + [vmem] * (len(args) - scalars),
        out_specs=specs,
        scratch_shapes=scratch,
        compiler_params=pltpu.CompilerParams(vmem_limit_bytes=40 << 20),
        cost_estimate=pl.CostEstimate(flops=WARP_COST, bytes_accessed=8 << 20, transcendentals=0),
        name="warp_meta" if with_meta else "warp",
    )(*args)


def cover_kernel(var, got, coadd_var, safe_ref):
    place_of = lax.broadcasted_iota(jnp.int32, (PATCH, TS), 0).astype(F32)

    def cover(offset, shift):
        u = place_of - offset
        lower = jnp.where((u >= 0.0) & (u <= TS - 1.0), 1.0 - shift, 0.0)
        return lower + jnp.where((u >= 1.0) & (u <= float(TS)), shift, 0.0)

    downs, acrosses = [], []
    for slot in range(CAP):
        at = MAIN + 8 * slot
        fields = var[at : at + 8, :] + got[at : at + 8, :]
        weight, row, col, frac_row, frac_col = (fields[f : f + 1, :] for f in range(5))
        down, down_low = split(cover(row, frac_row) * weight)
        across, across_low = split(cover(col, frac_col))
        downs += [down, down_low, down]
        acrosses += [across, across, across_low]
    den = lax.dot_general(
        jnp.concatenate(downs, 1), jnp.concatenate(acrosses, 1), (((1,), (1,)), ((), ())), preferred_element_type=F32
    )
    safe = jnp.maximum(den, 1.0)
    safe_ref[...] = safe
    for half in range(2):
        lo, lanes = half * (MAIN + META), slice(half * TS, (half + 1) * TS)
        part = safe[0:MAIN, lanes]
        coadd_var[0:MAIN, lanes] = (var[lo : lo + MAIN, :] + got[lo : lo + MAIN, :]) / (part * part)
    core = here()[2]
    for first, source in ((0, var), (1, got)):
        for second in range(2):
            rows = pl.ds(pl.multiple_of(MAIN + PART * quarter(first, second, core), 8), PART)
            for half in range(2):
                lo, lanes = 2 * MAIN + META + PART * (2 * second + half), slice(half * TS, (half + 1) * TS)
                part = safe_ref[rows, lanes]
                coadd_var[rows, lanes] = source[lo : lo + PART, :] / (part * part)


def divide_kernel(num, got, safe, coadd):
    for half in range(2):
        rows, lanes = slice(half * PATCH, (half + 1) * PATCH), slice(half * TS, (half + 1) * TS)
        coadd[:, lanes] = (num[rows, :] + got[rows, :]) / safe[:, lanes]


def finish(kernel, name, outs, *args):
    vmem = pl.BlockSpec(memory_space=pltpu.VMEM)
    return pl.pallas_call(
        kernel,
        out_shape=[jax.ShapeDtypeStruct((PATCH, PATCH), F32)] * outs,
        in_specs=[vmem] * len(args),
        out_specs=[vmem] * outs,
        compiler_params=pltpu.CompilerParams(vmem_limit_bytes=8 << 20),
        cost_estimate=pl.CostEstimate(flops=1_000_000_000, bytes_accessed=1 << 20, transcendentals=0),
        name=name,
    )(*args)


EDGES = (((0, 1), (1, 0), (2, 3), (3, 2)), ((1, 2), (2, 1), (3, 0), (0, 3)))


def over_patch(axis, edge):
    pairs = []
    for a, b in EDGES[edge]:
        for other in range(4):
            for core in range(2):
                src, dst = ((a, other), (b, other)) if axis == core else ((other, a), (other, b))
                pairs.append((src[0] * 8 + src[1] * 2 + core, dst[0] * 8 + dst[1] * 2 + core))
    return pairs


def over_visit(edge):
    return [
        (a * 32 + 2 * chip + core, b * 32 + 2 * chip + core)
        for core in range(2)
        for a, b in EDGES[edge ^ core]
        for chip in range(16)
    ]


def combine(var, num):
    def cross(x, axis, edge):
        return lax.ppermute(x, "patch", over_patch(axis, edge))

    def visit(x, edge):
        return lax.ppermute(x, ("visit", "patch"), over_visit(edge))

    def fold(keep, got):
        n = keep.shape[0] // 2
        return keep[:n] + got[:n], keep[n:] + got[n:]

    def after(got, *earlier):
        return lax.optimization_barrier((*got, *earlier))[: len(got)]

    (vl, vl_send, vr, vr_send, vp, vp_send), (nl, nl_send, nr, nr_send) = var, num
    vl_got, vr_got, vp_got = cross(vl_send, 0, 0), cross(vr_send, 0, 1), visit(vp_send, 0)
    nl_got, nr_got = cross(nl_send, 0, 0), cross(nr_send, 0, 1)

    (vl, vl_send), (vr, vr_send) = fold(vl, vl_got), fold(vr, vr_got)
    vp, vp_send = vp[0] + vp_got[0], vp[1] + vp_got[1]
    vl_got, vr_got, vp_got = cross(vl_send, 0, 1), cross(vr_send, 0, 0), visit(vp_send, 1)
    nl_got, nr_got = after((nl_got, nr_got), vl_send, vr_send, vp_send)
    vp, vp_send = fold(vp, vp_got)
    vp, vp_send = fold(vp, cross(vp_send, 0, 0))
    vp = vp + cross(vp_send, 0, 1)

    (nl, nl_send), (nr, nr_send) = fold(nl, nl_got), fold(nr, nr_got)
    nl_got, nr_got = cross(nl_send, 0, 1), cross(nr_send, 0, 0)

    vl_got, vr_got = after((vl_got, vr_got), nl_send, nr_send, vp_send)
    v, v_send = (
        jnp.concatenate([vl[p] + vl_got[p], vr[p] + vr_got[p], vp[p]], 1) for p in (slice(0, 2), slice(2, 4))
    )
    v_got = cross(v_send, 1, 0)

    nl_got, nr_got = after((nl_got, nr_got), vp_send)
    n, n_send = (jnp.concatenate([nl[p] + nl_got[p], nr[p] + nr_got[p]], 1) for p in (slice(0, 2), slice(2, 4)))
    n_got = cross(n_send, 1, 1)

    (n_got,) = after((n_got,), v_send)
    n, n_send = fold(n, n_got)
    (v_got,) = after((v_got,), n_send)
    v, v_send = fold(v, v_got)
    n = n[0] + cross(n_send, 1, 0)[0]
    (v_got,) = after((cross(v_send, 1, 1),), n)
    v = v[0] + v_got[0]

    n = n + visit(n, 0)
    v_got, main = visit(v, 1), 2 * MAIN + META
    v = jnp.concatenate([v[:main] + v_got[:main], v[main:], v_got[main:]], 0)
    return (v, visit(v, 0)), (n, visit(n, 1))


def shards(image, variance, intersections, boxes, shifts, basis_ids, coefs, taps):
    swap = [(i, i ^ 1) for i in range(32)]
    other_variance = lax.ppermute(variance, "patch", swap)
    table = pack(intersections, boxes, shifts)
    other_table = lax.ppermute(table, "patch", swap)
    matched = match(basis_ids, coefs, taps, image)
    matched, other_table = lax.optimization_barrier((matched, other_table))
    other_matched = lax.ppermute(matched, "patch", swap)
    *var, slots, weights = warp(True, table, other_table, variance, other_variance)
    num = warp(False, slots, table, other_table, weights, matched, other_matched)
    var, num = combine(var, num)
    coadd_var, safe = finish(cover_kernel, "cover", 2, *var)
    (coadd,) = finish(divide_kernel, "divide", 1, *num, safe)
    return coadd, coadd_var


def solution(mesh):
    split_spec = ("visit", "patch")
    in_specs = (
        P(split_spec, None, None),
        P(split_spec, None, None),
        P(split_spec, None),
        P(split_spec, None, None),
        P(split_spec, None, None),
        P(split_spec, None),
        P(split_spec, None),
        P(),
    )
    out_specs = (P("patch", None), P("patch", None))
    return jax.shard_map(shards, mesh=mesh, in_specs=in_specs, out_specs=out_specs, check_vma=False)
```

```python
import functools

import jax
import jax.numpy as jnp
from jax import lax
from jax.experimental import pallas as pl
from jax.experimental.pallas import tpu as pltpu
from jax.sharding import PartitionSpec as P

TS = 128
PATCH = 256
NB = 3
NBASIS = 8
HALF = 20
TILES = 32
ROUTES = 2 * TILES
CAP = 3
META = 24
MAIN = 160
PART = (PATCH - MAIN) // 4
PITCH = TS + 8
PAD = 64
F32 = jnp.float32
BF16 = jnp.bfloat16

EMPTY = 1 << 24
UNROLL = 12
MATCH_UNROLL = 32
CHUNKS = 1
MATCH_COST = 100_000_000_000
WARP_COST = 10_000_000_000


def split(x):
    high = x.astype(BF16)
    return high, (x - high.astype(F32)).astype(BF16)


def here():
    patch = lax.axis_index("patch")
    z, y = patch >> 3, (patch >> 1) & 3
    return z, y, patch & 1, lax.axis_index("visit") * 16 + z * 4 + y


def quarter(first, second, core):
    visit = lax.axis_index("visit")
    edges = jnp.where(core == 0, first + 2 * second, 2 * first + second)
    return (visit ^ (visit >> 1)) ^ edges


def place_code(z, y, core):
    first, second = jnp.where(core == 0, z, y), jnp.where(core == 0, y, z)
    first, second = first ^ (first >> 1), second ^ (second >> 1)
    return ((first & 1) << 3) | ((first >> 1) << 2) | ((second & 1) << 1) | (second >> 1)


def pack_kernel(intersections, boxes, shifts, out):
    z, y, _, _ = here()
    out[...] = jnp.zeros_like(out)
    earlier_item = lax.broadcasted_iota(jnp.int32, (TILES, TILES), 0)
    item = lax.broadcasted_iota(jnp.int32, (TILES, TILES), 1)
    dest = [intersections[route : route + 1, :] for route in range(2)]

    def earlier(rows):
        columns = [jnp.sum(jnp.where(earlier_item == item, row, 0), axis=1, keepdims=True) for row in rows]
        counts = []
        for route, row in enumerate(rows):
            same = jnp.where((columns[route] == row) & (earlier_item < item), 1, 0)
            if route == 1:
                same = same + jnp.where(columns[0] == row, 1, 0)
            counts.append(jnp.sum(same, axis=0, keepdims=True))
        return counts

    slots, places = earlier(dest), earlier([d & 1 for d in dest])
    for route in range(2):
        d = dest[route]
        code = place_code(d >> 3, (d >> 1) & 3, d & 1) ^ place_code(z, y, d & 1)
        out[route : route + 1, 0:TILES] = (code + (slots[route] << 4) + ((d & 1) << 8)).astype(F32)
        out[10 + route : 11 + route, 0:TILES] = places[route].astype(F32)
        out[2 + 2 * route : 4 + 2 * route, 0:TILES] = boxes[route].astype(F32)
        out[6 + 2 * route : 8 + 2 * route, 0:TILES] = shifts[route]
    second = jnp.sum(intersections[...] & 1).astype(F32)
    lane = lax.broadcasted_iota(jnp.int32, (1, TS), 1)
    out[12:13, :] = jnp.where(lane == 0, ROUTES - second, second)


def pack(intersections, boxes, shifts):
    vmem = pl.BlockSpec(memory_space=pltpu.VMEM)
    return pl.pallas_call(
        pack_kernel,
        out_shape=jax.ShapeDtypeStruct((16, TS), F32),
        in_specs=[vmem] * 3,
        out_specs=vmem,
        name="pack",
    )(intersections.T, boxes.transpose(1, 2, 0), shifts.transpose(1, 2, 0))


def match_kernel(
    ids_hbm, coefs_hbm, taps_hbm, image_hbm, out, basis_ids, coefs, taps, line, row_mats, col_mats, image, sems, small_sems
):
    size = TILES // CHUNKS
    copies = [
        pltpu.make_async_copy(image_hbm.at[pl.ds(c * size, size)], image.at[pl.ds(c * size, size)], sems.at[c])
        for c in range(CHUNKS)
    ]
    small = [
        pltpu.make_async_copy(source, target, small_sems.at[i])
        for i, (source, target) in enumerate(((taps_hbm, taps), (ids_hbm, basis_ids), (coefs_hbm, coefs)))
    ]
    for copy in small + copies:
        copy.start()
    i = lax.broadcasted_iota(jnp.int32, (TS, TS), 0)
    k = lax.broadcasted_iota(jnp.int32, (TS, TS), 1)
    near = jnp.abs(i - k) <= HALF
    none = jnp.zeros((TS, TS), BF16)
    line[...] = jnp.zeros_like(line)
    for copy in small:
        copy.wait()
    for b in range(NBASIS):
        line[2 * b : 2 * b + 2, 0 : 2 * HALF + 1] = taps[b]
    line[...] = pltpu.roll(line[...], TS - HALF, 1)

    def square(high, low):
        return jnp.concatenate([jnp.concatenate([high, low], 1), jnp.concatenate([high, none], 1)], 0)

    for b in range(NBASIS):
        for side in range(2):
            band = jnp.broadcast_to(line[2 * b + side : 2 * b + side + 1, :], (TS, TS))
            band = jnp.where(near, pltpu.roll(band, 0, 1, stride=1, stride_axis=0), 0.0)
            if side == 0:
                row_mats[b] = jnp.concatenate(split(band.T), 1)
            else:
                col_mats[b] = square(*split(band))

    out[TILES * PITCH :, :] = jnp.zeros((8, TS), F32)
    for c in range(CHUNKS):
        copies[c].wait()

        @pl.loop(c * size, (c + 1) * size, step=MATCH_UNROLL)
        def _(first):
            for t in [first + u for u in range(MATCH_UNROLL)]:
                pixels = square(*split(image[t]))
                bases = [basis_ids[j, t] for j in range(NB)]
                bands = jnp.concatenate([row_mats[basis] for basis in bases], 0)
                p = jnp.dot(bands, pixels, preferred_element_type=F32)
                p = p[:, :TS] + p[:, TS:]
                parts = [jnp.concatenate(split(p[TS * j : TS * (j + 1)] * coefs[j, t]), 1) for j in range(NB)]
                bands = jnp.concatenate([col_mats[basis] for basis in bases], 0)
                total = jnp.dot(jnp.concatenate(parts, 1), bands, preferred_element_type=F32)
                at = pl.multiple_of(t * PITCH, 8)
                out[pl.ds(at, 8), :] = jnp.zeros((8, TS), F32)
                out[pl.ds(at + 8, TS), :] = total[:, :TS] + total[:, TS:]


def match(basis_ids, coefs, taps, image):
    vmem, hbm = pl.BlockSpec(memory_space=pltpu.VMEM), pl.BlockSpec(memory_space=pltpu.HBM)
    return pl.pallas_call(
        match_kernel,
        out_shape=jax.ShapeDtypeStruct((TILES * PITCH + 8, TS), F32),
        in_specs=[hbm] * 4,
        out_specs=vmem,
        scratch_shapes=[
            pltpu.SMEM((NB, TILES), jnp.int32),
            pltpu.SMEM((NB, TILES), F32),
            pltpu.VMEM((NBASIS, 2, 2 * HALF + 1), F32),
            pltpu.VMEM((2 * NBASIS, TS), F32),
            pltpu.VMEM((NBASIS, TS, 2 * TS), BF16),
            pltpu.VMEM((NBASIS, 2 * TS, 2 * TS), BF16),
            pltpu.VMEM((TILES, TS, TS), F32),
            pltpu.SemaphoreType.DMA((CHUNKS,)),
            pltpu.SemaphoreType.DMA((3,)),
        ],
        compiler_params=pltpu.CompilerParams(vmem_limit_bytes=40 << 20),
        cost_estimate=pl.CostEstimate(flops=MATCH_COST, bytes_accessed=6 << 20, transcendentals=0),
        name="match",
    )(*(pltpu.with_memory_space_constraint(x, pltpu.HBM) for x in (basis_ids.T, coefs.T, taps, image)))


def warp_kernel(with_meta, *refs):
    if with_meta:
        own, other, own_raw, other_raw = refs[:4]
        outs, slots, weights = refs[4:10], refs[10], refs[11]
        acc, meta, own_tiles, other_tiles = refs[12:]
    else:
        slots, own, other, weights, own_tiles, other_tiles = refs[:6]
        outs, acc = refs[6:10], refs[10]
    lane = lax.broadcasted_iota(jnp.int32, (8, TS), 1)
    for k in range(16):
        for side in (1, 2):
            acc[4 * k + side, PAD : PAD + PATCH, :] = jnp.zeros((PATCH, TS), F32)

    if with_meta:
        _, _, core, chip = here()
        meta[...] = jnp.zeros_like(meta)

        @pl.loop(0, TILES, step=8)
        def _(first):
            for side, table, raw, tiles in ((0, own, own_raw, own_tiles), (1, other, other_raw, other_tiles)):
                for route in range(2):
                    for t in [first + u for u in range(8)]:
                        what = table[route, t].astype(jnp.int32)
                        at = jnp.where((what >> 8) == core, table[10 + route, t].astype(jnp.int32) + 1, 127)
                        slots[side, at] = (what << 8) + (2 * t + route)
                sums = []
                for t in [first + u for u in range(8)]:
                    tile = raw[t]
                    at = pl.multiple_of(t * PITCH, 8)
                    tiles[pl.ds(at, 8), :] = jnp.zeros((8, TS), F32)
                    tiles[pl.ds(at + 8, TS), :] = tile
                    sums.append(jnp.sum(tile, axis=0, keepdims=True))
                sums = jnp.sum(jnp.concatenate(sums, 0), axis=1, keepdims=True)
                at = pl.multiple_of(side * TILES + first, 8)
                weights[pl.ds(at, 8), :] = jnp.broadcast_to(float(TS * TS) / sums, (8, TS))

        for side, table in ((0, own), (1, other)):
            n = table[12, core].astype(jnp.int32)
            slots[side, 0] = n
            for u in range(UNROLL):
                slots[side, 1 + n + u] = EMPTY
        for tiles in (own_tiles, other_tiles):
            tiles[TILES * PITCH :, :] = jnp.zeros((8, TS), F32)

    def place(entry, side, table, tiles):
        item, k, slot = entry & 255, (entry >> 8) & 15, (entry >> 12) & 3
        t, route = item >> 1, item & 1
        row, col = table[2 + 2 * route, t].astype(jnp.int32), table[3 + 2 * route, t].astype(jnp.int32)
        frac_row, frac_col = table[6 + 2 * route, t], table[7 + 2 * route, t]
        real = jnp.where(entry >= EMPTY, 0.0, 1.0)
        weight = jnp.broadcast_to(weights[pl.ds(side * TILES + t, 1), :], (8, TS))
        scale = weight * real
        if with_meta:
            field = lax.broadcasted_iota(jnp.int32, (8, TS), 0)
            value = jnp.where(field == 1, row.astype(F32), weight)
            value = jnp.where(field == 2, col.astype(F32), value)
            value = jnp.where(field == 3, frac_row, value)
            value = jnp.where(field == 4, frac_col, value)
            value = jnp.where((field < 5) & (lane == 2 * chip + side), value * real, 0.0)
            meta[k * CAP + slot] += value
            scale = scale * weight
        near, far = scale * (1.0 - frac_col), scale * frac_col
        turn, down = (col + TS) & (TS - 1), (row + PAD) & 7
        here = jnp.where(lane >= turn, near, 0.0)
        here_next = jnp.where(lane >= turn + 1, far, 0.0)
        over, over_next = near - here, far - here_next
        start = t * PITCH + 8 - down
        upper, lower = tiles[pl.ds(start, PITCH), :], tiles[pl.ds(start - 1, PITCH), :]
        rows = upper * (1.0 - frac_row) + lower * frac_row
        r0 = pltpu.roll(rows, turn, 1).reshape(PITCH // 8, 8, TS)
        r1 = pltpu.roll(rows, (turn + 1) & (TS - 1), 1).reshape(PITCH // 8, 8, TS)
        left = (r0 * here + r1 * here_next).reshape(PITCH, TS)
        right = (r0 * over + r1 * over_next).reshape(PITCH, TS)
        return left, right, 4 * k + ((col + TS) >> 7), pl.multiple_of(((row + PAD) >> 3) * 8, 8)

    for side, table, tiles in ((0, own, own_tiles), (1, other, other_tiles)):

        @pl.loop(0, (slots[side, 0] + UNROLL - 1) // UNROLL)
        def _(m, side=side, table=table, tiles=tiles):
            for u in range(UNROLL):
                left, right, first, base = place(slots[side, 1 + m * UNROLL + u], side, table, tiles)
                acc[first, pl.ds(base, PITCH), :] += left
                acc[first + 1, pl.ds(base, PITCH), :] += right

    for k in range(16):
        a, b, c, d = k >> 3, (k >> 2) & 1, (k >> 1) & 1, k & 1
        rest = 2 * c + d if with_meta else 2 * d + c
        rows = MAIN if with_meta else PATCH
        left, right = outs[a], outs[2 + b]
        left[4 * b + rest, 0:rows, :] = acc[4 * k + 1, PAD : PAD + rows, :]
        right[4 * a + rest, :, :] = acc[4 * k + 2, PAD : PAD + rows, :]
        if with_meta:
            for slot in range(CAP):
                left[4 * b + rest, MAIN + 8 * slot : MAIN + 8 * slot + 8, :] = meta[k * CAP + slot]

    if with_meta:
        for first in range(2):
            for second in range(2):
                start = pl.multiple_of(PAD + MAIN + PART * quarter(first, second, core), 8)
                for k in range(16):
                    for half in range(2):
                        part = acc[4 * k + 1 + half, pl.ds(start, PART), :]
                        outs[4 + first][second, k, PART * half : PART * (half + 1), :] = part


def warp(with_meta, *args):
    smem, vmem = pl.BlockSpec(memory_space=pltpu.SMEM), pl.BlockSpec(memory_space=pltpu.VMEM)
    left = jax.ShapeDtypeStruct((8, MAIN + META if with_meta else PATCH, TS), F32)
    right = jax.ShapeDtypeStruct((8, MAIN if with_meta else PATCH, TS), F32)
    outs, specs = [left, left, right, right], [vmem] * 4
    if with_meta:
        outs += [jax.ShapeDtypeStruct((2, 16, 2 * PART, TS), F32)] * 2
        specs += [vmem] * 2
    scratch = [pltpu.VMEM((64, 384, TS), F32)]
    if with_meta:
        outs += [jax.ShapeDtypeStruct((2, 128), jnp.int32), jax.ShapeDtypeStruct((2 * TILES, TS), F32)]
        specs += [smem, vmem]
        scratch += [pltpu.VMEM((16 * CAP, 8, TS), F32)] + [pltpu.VMEM((TILES * PITCH + 8, TS), F32)] * 2
    scalars = 2 if with_meta else 3
    return pl.pallas_call(
        functools.partial(warp_kernel, with_meta),
        out_shape=outs,
        in_specs=[smem] * scalars + [vmem] * (len(args) - scalars),
        out_specs=specs,
        scratch_shapes=scratch,
        compiler_params=pltpu.CompilerParams(vmem_limit_bytes=40 << 20),
        cost_estimate=pl.CostEstimate(flops=WARP_COST, bytes_accessed=8 << 20, transcendentals=0),
        name="warp_meta" if with_meta else "warp",
    )(*args)


def cover_kernel(var, got, coadd_var, safe_ref):
    place_of = lax.broadcasted_iota(jnp.int32, (PATCH, TS), 0).astype(F32)

    def cover(offset, shift):
        u = place_of - offset
        lower = jnp.where((u >= 0.0) & (u <= TS - 1.0), 1.0 - shift, 0.0)
        return lower + jnp.where((u >= 1.0) & (u <= float(TS)), shift, 0.0)

    downs, acrosses = [], []
    for slot in range(CAP):
        at = MAIN + 8 * slot
        fields = var[at : at + 8, :] + got[at : at + 8, :]
        weight, row, col, frac_row, frac_col = (fields[f : f + 1, :] for f in range(5))
        down, down_low = split(cover(row, frac_row) * weight)
        across, across_low = split(cover(col, frac_col))
        downs += [down, down_low, down]
        acrosses += [across, across, across_low]
    den = lax.dot_general(
        jnp.concatenate(downs, 1), jnp.concatenate(acrosses, 1), (((1,), (1,)), ((), ())), preferred_element_type=F32
    )
    safe = jnp.maximum(den, 1.0)
    safe_ref[...] = safe
    for half in range(2):
        lo, lanes = half * (MAIN + META), slice(half * TS, (half + 1) * TS)
        part = safe[0:MAIN, lanes]
        coadd_var[0:MAIN, lanes] = (var[lo : lo + MAIN, :] + got[lo : lo + MAIN, :]) / (part * part)
    core = here()[2]
    for first, source in ((0, var), (1, got)):
        for second in range(2):
            rows = pl.ds(pl.multiple_of(MAIN + PART * quarter(first, second, core), 8), PART)
            for half in range(2):
                lo, lanes = 2 * MAIN + META + PART * (2 * second + half), slice(half * TS, (half + 1) * TS)
                part = safe_ref[rows, lanes]
                coadd_var[rows, lanes] = source[lo : lo + PART, :] / (part * part)


def divide_kernel(num, got, safe, coadd):
    for half in range(2):
        rows, lanes = slice(half * PATCH, (half + 1) * PATCH), slice(half * TS, (half + 1) * TS)
        coadd[:, lanes] = (num[rows, :] + got[rows, :]) / safe[:, lanes]


def finish(kernel, name, outs, *args):
    vmem = pl.BlockSpec(memory_space=pltpu.VMEM)
    return pl.pallas_call(
        kernel,
        out_shape=[jax.ShapeDtypeStruct((PATCH, PATCH), F32)] * outs,
        in_specs=[vmem] * len(args),
        out_specs=[vmem] * outs,
        compiler_params=pltpu.CompilerParams(vmem_limit_bytes=8 << 20),
        cost_estimate=pl.CostEstimate(flops=1_000_000_000, bytes_accessed=1 << 20, transcendentals=0),
        name=name,
    )(*args)


EDGES = (((0, 1), (1, 0), (2, 3), (3, 2)), ((1, 2), (2, 1), (3, 0), (0, 3)))


def over_patch(axis, edge):
    pairs = []
    for a, b in EDGES[edge]:
        for other in range(4):
            for core in range(2):
                src, dst = ((a, other), (b, other)) if axis == core else ((other, a), (other, b))
                pairs.append((src[0] * 8 + src[1] * 2 + core, dst[0] * 8 + dst[1] * 2 + core))
    return pairs


def over_visit(edge):
    return [
        (a * 32 + 2 * chip + core, b * 32 + 2 * chip + core)
        for core in range(2)
        for a, b in EDGES[edge ^ core]
        for chip in range(16)
    ]


def combine(var, num):
    def cross(x, axis, edge):
        return lax.ppermute(x, "patch", over_patch(axis, edge))

    def visit(x, edge):
        return lax.ppermute(x, ("visit", "patch"), over_visit(edge))

    def fold(keep, got):
        n = keep.shape[0] // 2
        return keep[:n] + got[:n], keep[n:] + got[n:]

    def after(got, *earlier):
        return lax.optimization_barrier((*got, *earlier))[: len(got)]

    (vl, vl_send, vr, vr_send, vp, vp_send), (nl, nl_send, nr, nr_send) = var, num
    vl_got, vr_got, vp_got = cross(vl_send, 0, 0), cross(vr_send, 0, 1), visit(vp_send, 0)
    nl_got, nr_got = cross(nl_send, 0, 0), cross(nr_send, 0, 1)

    (vl, vl_send), (vr, vr_send) = fold(vl, vl_got), fold(vr, vr_got)
    vp, vp_send = vp[0] + vp_got[0], vp[1] + vp_got[1]
    vl_got, vr_got, vp_got = cross(vl_send, 0, 1), cross(vr_send, 0, 0), visit(vp_send, 1)
    nl_got, nr_got = after((nl_got, nr_got), vl_send, vr_send, vp_send)
    vp, vp_send = fold(vp, vp_got)
    vp, vp_send = fold(vp, cross(vp_send, 0, 0))
    vp = vp + cross(vp_send, 0, 1)

    (nl, nl_send), (nr, nr_send) = fold(nl, nl_got), fold(nr, nr_got)
    nl_got, nr_got = cross(nl_send, 0, 1), cross(nr_send, 0, 0)

    vl_got, vr_got = after((vl_got, vr_got), nl_send, nr_send, vp_send)
    v, v_send = (
        jnp.concatenate([vl[p] + vl_got[p], vr[p] + vr_got[p], vp[p]], 1) for p in (slice(0, 2), slice(2, 4))
    )
    v_got = cross(v_send, 1, 0)

    nl_got, nr_got = after((nl_got, nr_got), vp_send)
    n, n_send = (jnp.concatenate([nl[p] + nl_got[p], nr[p] + nr_got[p]], 1) for p in (slice(0, 2), slice(2, 4)))
    n_got = cross(n_send, 1, 1)

    (n_got,) = after((n_got,), v_send)
    n, n_send = fold(n, n_got)
    (v_got,) = after((v_got,), n_send)
    v, v_send = fold(v, v_got)
    n = n[0] + cross(n_send, 1, 0)[0]
    (v_got,) = after((cross(v_send, 1, 1),), n)
    v = v[0] + v_got[0]

    n = n + visit(n, 0)
    v_got, main = visit(v, 1), 2 * MAIN + META
    v = jnp.concatenate([v[:main] + v_got[:main], v[main:], v_got[main:]], 0)
    return (v, visit(v, 0)), (n, visit(n, 1))


def shards(image, variance, intersections, boxes, shifts, basis_ids, coefs, taps):
    swap = [(i, i ^ 1) for i in range(32)]
    other_variance = lax.ppermute(variance, "patch", swap)
    table = pack(intersections, boxes, shifts)
    other_table = lax.ppermute(table, "patch", swap)
    matched = match(basis_ids, coefs, taps, image)
    matched, other_table = lax.optimization_barrier((matched, other_table))
    other_matched = lax.ppermute(matched, "patch", swap)
    *var, slots, weights = warp(True, table, other_table, variance, other_variance)
    num = warp(False, slots, table, other_table, weights, matched, other_matched)
    var, num = combine(var, num)
    coadd_var, safe = finish(cover_kernel, "cover", 2, *var)
    (coadd,) = finish(divide_kernel, "divide", 1, *num, safe)
    return coadd, coadd_var


def solution(mesh):
    split_spec = ("visit", "patch")
    in_specs = (
        P(split_spec, None, None),
        P(split_spec, None, None),
        P(split_spec, None),
        P(split_spec, None, None),
        P(split_spec, None, None),
        P(split_spec, None),
        P(split_spec, None),
        P(),
    )
    out_specs = (P("patch", None), P("patch", None))
    return jax.shard_map(shards, mesh=mesh, in_specs=in_specs, out_specs=out_specs, check_vma=False)
```
